32 devices in a mesh: gx: 8 (over z, core), gy: 4 (over y, x).
Axes of the slice: x: 2, y: 2, z: 4, core: 2. Of those that a mesh axis runs over, the one named last changes fastest.
Arguments:
- right_side: float32 [8, 256, 1024], P(None, 'gx', 'gy'), may hold values from -6 to 6
- conductivity: float32 [8, 256, 1024], P(None, 'gx', 'gy'), may hold values from 0.1 to 1
Outputs:
- solution_field: float32 [8, 256, 1024], P(None, 'gx', 'gy')
- residual: float32 [8, 256, 1024], P(None, 'gx', 'gy')
The draws below stay inside these ranges and needn't reach their ends.
All inputs are finite; a program needn't handle non-finite values.
Results may differ from the reference program's by a relative error of at most 0.0003.
Values sent between devices are 32-bit elements; how exact they have to be, the bound alone decides.
A program may use at most 64 MiB of HBM per device.

```python
import math
import jax
import jax.numpy as jnp

LZ = 8
ITERS = 2
NX = 256
NY = 1024


def block_levels(stream_key, dims, shards, low, high):
    factor_of, own = 1.0, jax.random.fold_in(stream_key, 6)
    for position, blocks in shards:
        heights = jnp.exp(jax.random.uniform(jax.random.fold_in(own, position), (blocks,), jnp.float32, low / len(shards), high / len(shards)))
        factor_of = factor_of * jnp.repeat(heights, dims[position] // blocks).reshape([-1 if axis == position else 1 for axis in range(len(dims))])
    return factor_of


def gaussian(rng, shape, width, reach, pieces=(), held_as=jnp.bfloat16):
    entries = width * jax.random.normal(rng, shape, jnp.float32)
    if pieces:
        entries = entries * block_levels(rng, shape, pieces, -0.22, 0.18)
    return jnp.clip(entries, -reach, reach).astype(held_as)


def setup_inputs(seed: int = 0) -> dict:
    key_of = jax.random.split(jax.random.key(seed), 3)
    return {
        "right_side": gaussian(key_of[0], (LZ, NX, NY), 1.0, 6.0, ((1, 8), (2, 4)), jnp.float32),
        "conductivity": jnp.clip(jnp.exp(math.log(1.0) - 2.3025851 * jax.random.uniform(key_of[1], (LZ, NX, NY), jnp.float32) ** block_levels(key_of[1], (LZ, NX, NY), ((1, 8), (2, 4)), -0.2, 0.2)), 0.1, 1.0),
    }


low_bound = 0.4
high_bound = 12.0
cheb_theta = 0.5 * (high_bound + low_bound)
cheb_delta = 0.5 * (high_bound - low_bound)
cheb_sigma = cheb_theta / cheb_delta
rho_first = 1.0 / cheb_sigma
rho_second = 1.0 / (2.0 * cheb_sigma - rho_first)
rho_third = 1.0 / (2.0 * cheb_sigma - rho_second)
neighbours = ((1, 0, 0), (-1, 0, 0), (0, 1, 0), (0, -1, 0), (0, 0, 1), (0, 0, -1))


def shifted(padded, dz, dx, dy):
    return padded[1 + dz:padded.shape[0] - 1 + dz, 1 + dx:padded.shape[1] - 1 + dx, 1 + dy:padded.shape[2] - 1 + dy]


def stencil(field_pad, cond_pad):
    field_full = jnp.pad(field_pad, ((1, 1), (0, 0), (0, 0)))
    cond_full = jnp.pad(cond_pad, ((1, 1), (0, 0), (0, 0)))
    centre = shifted(field_full, 0, 0, 0)
    cond_centre = shifted(cond_full, 0, 0, 0)
    total = jnp.zeros_like(centre)
    for dz, dx, dy in neighbours:
        total = total + 0.5 * (cond_centre + shifted(cond_full, dz, dx, dy)) * (centre - shifted(field_full, dz, dx, dy))
    return total


def reference(right_side, conductivity):
    cond_pad = jnp.pad(conductivity, ((0, 0), (1, 1), (1, 1)))

    def operate(field):
        return stencil(jnp.pad(field, ((0, 0), (1, 1), (1, 1))), cond_pad)

    def chain(source):
        first = source / cheb_theta
        res_one = source - operate(first)
        step_one = rho_second * rho_first * first + (2.0 * rho_second / cheb_delta) * res_one
        second = first + step_one
        res_two = res_one - operate(step_one)
        step_two = rho_third * rho_second * step_one + (2.0 * rho_third / cheb_delta) * res_two
        precond = second + step_two
        return precond, operate(precond)

    solution_field = jnp.zeros_like(right_side)
    residual = right_side
    precond, applied = chain(residual)
    gamma_old = jnp.float32(1.0)
    alpha_old = jnp.float32(1.0)
    direction = dir_image = dir_precond = dir_double = None
    for iteration in range(ITERS):
        gamma_now = jnp.sum(residual * precond)
        delta_now = jnp.sum(applied * precond)
        pre_applied, image = chain(applied)
        if iteration == 0:
            alpha_now = gamma_now / delta_now
            dir_double, dir_precond, dir_image, direction = image, pre_applied, applied, precond
        else:
            beta_now = gamma_now / gamma_old
            alpha_now = gamma_now / (delta_now - beta_now * gamma_now / alpha_old)
            dir_double = image + beta_now * dir_double
            dir_precond = pre_applied + beta_now * dir_precond
            dir_image = applied + beta_now * dir_image
            direction = precond + beta_now * direction
        solution_field = solution_field + alpha_now * direction
        residual = residual - alpha_now * dir_image
        precond = precond - alpha_now * dir_precond
        applied = applied - alpha_now * dir_double
        gamma_old = gamma_now
        alpha_old = alpha_now
    return solution_field, residual
```

```python
import jax
import jax.numpy as jnp
from jax import lax
from jax.experimental import pallas as pl
from jax.experimental.pallas import tpu as pltpu
from jax.sharding import PartitionSpec as P

low_bound = 0.4
high_bound = 12.0
cheb_theta = 0.5 * (high_bound + low_bound)
cheb_delta = 0.5 * (high_bound - low_bound)
cheb_sigma = cheb_theta / cheb_delta
rho_first = 1.0 / cheb_sigma
rho_second = 1.0 / (2.0 * cheb_sigma - rho_first)
rho_third = 1.0 / (2.0 * cheb_sigma - rho_second)

step_0 = rho_second * rho_first / cheb_theta + 2.0 * rho_second / cheb_delta
step_1 = 2.0 * rho_second / cheb_delta / cheb_theta
mix_0 = 1.0 + rho_third * rho_second
mix_1 = 2.0 * rho_third / cheb_delta
power_0 = 1.0 / cheb_theta + mix_0 * step_0 + mix_1
power_1 = -mix_0 * step_1 - mix_1 / cheb_theta - mix_1 * step_0
power_2 = mix_1 * step_1
shift_1 = power_1 / power_2
shift_0 = power_0 / power_2

HALO = 6
LANES = 128
STRIP = 8
GROUP = 8
ONE_STAGE = 64
MESH = pl.DeviceIdType.MESH
WAYS = ((-1, 0), (1, 0), (0, -1), (0, 1), (-1, -1), (-1, 1), (1, -1), (1, 1))


def stages_of(num_x, num_y):
    if num_x * num_y <= ONE_STAGE:
        return ((num_x, num_y),)
    return ((num_x, 1), (1, num_y))


def kernel(
    num_x, num_y, r_hbm, c_hbm, p_out, w_out, m_out, n_out, r_out, sums_out,
    r_in, c_in, x_in, rc, src, coef, scoef, field, sfield,
    packed, side_in, corner_in, slots,
    in_sem, halo_send, halo_recv, red_send, red_recv,
):
    levels, rows, cols = r_in.shape
    tiles = rows // GROUP
    groups = tiles + 2
    width = LANES // groups
    last = cols - LANES
    me_x = lax.axis_index("gx")
    me_y = lax.axis_index("gy")
    stages = stages_of(num_x, num_y)

    def exists(dx, dy):
        ok = jnp.bool_(True)
        if dx < 0:
            ok = me_x > 0
        if dx > 0:
            ok = me_x < num_x - 1
        if dy < 0:
            ok_y = me_y > 0
            ok = ok_y if dx == 0 else jnp.logical_and(ok, ok_y)
        if dy > 0:
            ok_y = me_y < num_y - 1
            ok = ok_y if dx == 0 else jnp.logical_and(ok, ok_y)
        return ok

    loads = [
        pltpu.make_async_copy(r_hbm, r_in, in_sem.at[0]),
        pltpu.make_async_copy(c_hbm, c_in, in_sem.at[1]),
    ]
    for load in loads:
        load.start()

    def partners(stage):
        count_x, count_y = stage
        mine = (me_x if count_x > 1 else 0) * count_y + (me_y if count_y > 1 else 0)
        total = count_x * count_y
        found = []
        for k in range(1, total):
            other = lax.rem(mine + k, total)
            found.append((
                other // count_y if count_x > 1 else me_x,
                lax.rem(other, count_y) if count_y > 1 else me_y,
            ))
        return mine, found

    barrier = pltpu.get_barrier_semaphore()
    expected = jnp.int32(0)
    for stage in stages:
        for device in partners(stage)[1]:
            pl.semaphore_signal(barrier, inc=1, device_id=device, device_id_type=MESH)
            expected = expected + 1
    if len(stages) > 1:
        for dx, dy in WAYS[4:]:
            ok = exists(dx, dy)

            @pl.when(ok)
            def _():
                pl.semaphore_signal(
                    barrier, inc=1, device_id=(me_x + dx, me_y + dy), device_id_type=MESH
                )

            expected = expected + ok.astype(jnp.int32)
    pl.semaphore_wait(barrier, expected)

    def halo_copies(way):
        dx, dy = WAYS[way]
        if dy == 0:
            side = 1 if dx < 0 else 0
            low = 0 if dx < 0 else rows - HALO
            land = 0 if dx < 0 else GROUP - HALO
            pairs = [
                (ref.at[:, pl.ds(low, HALO)], x_in.at[a, side, :, pl.ds(land, HALO)])
                for a, ref in enumerate((r_hbm, c_hbm))
            ]
        elif dx == 0:
            pairs = [(packed.at[0 if dy < 0 else 1], side_in.at[0 if dy < 0 else 1])]
        else:
            pairs = [(
                packed.at[0 if dy < 0 else 1, 0 if dx < 0 else tiles - 1],
                corner_in.at[way - 4],
            )]
        return [
            pltpu.make_async_remote_copy(
                src_ref=one, dst_ref=two,
                send_sem=halo_send.at[way, a], recv_sem=halo_recv.at[way, a],
                device_id=(me_x + dx, me_y + dy), device_id_type=MESH,
            )
            for a, (one, two) in enumerate(pairs)
        ]

    def start(way):
        @pl.when(exists(*WAYS[way]))
        def _():
            for copy in halo_copies(way):
                copy.start()

    for way in (0, 1):
        start(way)

    lane = lax.broadcasted_iota(jnp.int32, (levels, LANES), 1)

    def between(low, high, like):
        at = lax.broadcasted_iota(jnp.int32, (1,) * (len(like) - 1) + (LANES,), len(like) - 1)
        return (at >= low) & (at < high)

    def rolled(v, by):
        by = by % v.shape[-1]
        return pltpu.roll(v, by, v.ndim - 1) if by else v

    for load in loads:
        load.wait()
    for a, source in enumerate((r_in, c_in)):
        for t in range(tiles):
            rc[a, HALO + t * GROUP : HALO + (t + 1) * GROUP] = jnp.transpose(
                source[:, t * GROUP : (t + 1) * GROUP, :], (1, 0, 2)
            )
    for side in range(2):
        first_lane = 0 if side == 0 else last
        offset = 0 if side == 0 else LANES - STRIP
        for t in range(tiles):
            acc = jnp.zeros((levels, LANES), jnp.float32)
            for a in range(2):
                for g in range(GROUP):
                    place = (a * GROUP + g) * STRIP
                    moved = rolled(
                        rc[a, HALO + t * GROUP + g, :, first_lane : first_lane + LANES],
                        place - offset,
                    )
                    acc = jnp.where((lane >= place) & (lane < place + STRIP), moved, acc)
            packed[side, t] = acc
    for way in (2, 3, 4, 5, 6, 7):
        start(way)

    for way in range(8):
        dx, dy = WAYS[way]

        @pl.when(jnp.logical_not(exists(-dx, -dy)))
        def _():
            if dy == 0:
                x_in[:, 1 if dx < 0 else 0] = jnp.zeros((2, levels, GROUP, cols), jnp.float32)
            elif dx == 0:
                side_in[0 if dy < 0 else 1] = jnp.zeros((tiles, levels, LANES), jnp.float32)
            else:
                corner_in[way - 4] = jnp.zeros((levels, LANES), jnp.float32)

    own_low = (HALO, 0)
    halo_low = (0, 2 * HALO)
    for a in range(2):
        for side in range(2):
            acc = jnp.zeros((GROUP, levels, LANES), jnp.float32)
            for g in range(1, tiles + 1):
                low = width * g + own_low[side]
                block = rc[
                    a, HALO + (g - 1) * GROUP : HALO + g * GROUP, :,
                    (0 if side == 0 else last) : (LANES if side == 0 else cols),
                ]
                moved = rolled(block, low if side == 0 else low + 2 * HALO)
                acc = jnp.where(between(low, low + 2 * HALO, block.shape), moved, acc)
            src[a, side, 1 : 1 + GROUP] = acc

    def wrap(ref, side):
        ref[side, 0] = rolled(ref[side, GROUP], width)
        ref[side, GROUP + 1] = rolled(ref[side, 1], -width)

    level_of = lambda shape: lax.broadcasted_iota(
        jnp.int32, (1,) * (len(shape) - 2) + shape[-2:], len(shape) - 2
    )

    def flux_coefficients(c, c_up, up):
        return jnp.where(jnp.minimum(c, c_up) > 0.0, 0.5 * (c + c_up), 0.0)

    def row_coefficients(ref, low, n, main):
        c = ref[pl.ds(low, n)]
        axis = c.ndim - 1
        level = level_of(c.shape)
        ky = 0.5 * (c + pltpu.roll(c, c.shape[-1] - 1, axis))
        if main:
            at = lax.broadcasted_iota(jnp.int32, (1, 1, cols), 2)
            ky = jnp.where(at < cols - 1, ky, 0.0)
        kz = jnp.where(level < levels - 1, 0.5 * (c + pltpu.roll(c, levels - 1, axis - 1)), 0.0)
        inside = jnp.logical_and(level > 0, level < levels - 1)
        kb = jnp.where(inside, 0.0, 0.5 * c)
        return c, ky, kz, kb

    def own_coefficients(low, n, closed):
        c, ky, kz, kb = row_coefficients(rc.at[1], low, n, True)
        coef[1, pl.ds(low, n)] = ky
        coef[2, pl.ds(low, n)] = kz
        if closed:
            coef[3, pl.ds(low, n)] = kb
            coef[4, pl.ds(low, n)] = kb + shift_1

    def x_faces(low, n):
        c = rc[1, pl.ds(low, n)]
        coef[0, pl.ds(low, n)] = 0.5 * (c + rc[1, pl.ds(low + 1, n)])

    def edge_coefficients(low, n):
        c, ky, kz, kb = row_coefficients(rc.at[1], low, n, True)
        before = rc[1, pl.ds(low - 1, n)]
        after = rc[1, pl.ds(low + 1, n)]
        inside = c > 0.0
        half = 0.5 * c
        kb = kb + jnp.where(before > 0.0, 0.0, half) + jnp.where(after > 0.0, 0.0, half)
        coef[1, pl.ds(low, n)] = jnp.where(inside, ky, 0.0)
        coef[2, pl.ds(low, n)] = jnp.where(inside, kz, 0.0)
        coef[3, pl.ds(low, n)] = kb
        coef[4, pl.ds(low, n)] = kb + shift_1

    def edge_faces(low, n):
        c, c_up = rc[1, pl.ds(low, n)], rc[1, pl.ds(low + 1, n)]
        coef[0, pl.ds(low, n)] = flux_coefficients(c, c_up, True)

    def strip_coefficients(side):
        ref = src.at[1, side]
        c = ref[1 : 1 + GROUP]
        level = level_of(c.shape)
        east, west = pltpu.roll(c, LANES - 1, 2), pltpu.roll(c, 1, 2)
        before, after = ref[0:GROUP], ref[2 : 2 + GROUP]
        half = 0.5 * c
        inside = jnp.logical_and(level > 0, level < levels - 1)
        kb = jnp.where(inside, 0.0, half)
        for other in (east, west, before, after):
            kb = kb + jnp.where(other > 0.0, 0.0, half)
        scoef[0, side, 0 : GROUP + 1] = flux_coefficients(
            ref[0 : GROUP + 1], ref[1 : GROUP + 2], True
        )
        scoef[1, side, 1 : 1 + GROUP] = flux_coefficients(c, east, True)
        scoef[2, side, 1 : 1 + GROUP] = jnp.where(
            level < levels - 1, half + 0.5 * pltpu.roll(c, levels - 1, 1), 0.0
        )
        scoef[3, side, 1 : 1 + GROUP] = kb
        scoef[4, side, 1 : 1 + GROUP] = kb + shift_1

    def apply(v, v_down, v_up, ks, low, n, which):
        axis = v.ndim - 1
        span = v.shape[-1]
        across = ks[0, pl.ds(low, n)] * (v - v_up)
        back = ks[0, pl.ds(low - 1, n)] * (v_down - v)
        fy = ks[1, pl.ds(low, n)] * (v - pltpu.roll(v, span - 1, axis))
        fz = ks[2, pl.ds(low, n)] * (v - pltpu.roll(v, levels - 1, axis - 1))
        return (
            (across - back)
            + (fy - pltpu.roll(fy, 1, axis))
            + ((fz - pltpu.roll(fz, 1, axis - 1)) + ks[which, pl.ds(low, n)] * v)
        )

    U, PP, WW, UU, MM, NN = range(6)

    def sweep(number, ks, r, f, low, n):
        source = r if number == 0 else f.at[number - 1]
        v = source[pl.ds(low, n)]
        image = apply(
            v, source[pl.ds(low - 1, n)], source[pl.ds(low + 1, n)], ks, low, n,
            4 if number in (0, 3) else 3,
        )
        if number == 1:
            image = image + shift_0 * r[pl.ds(low, n)]
        if number == 4:
            image = image + shift_0 * f[WW, pl.ds(low, n)]
        f[number, pl.ds(low, n)] = image
        return image

    def products(state, r, f, low, n, q):
        rr, p, w, m = (x[pl.ds(low, n)] for x in (r, f.at[PP], f.at[WW], f.at[MM]))
        return tuple(
            s + jnp.sum(t, axis=0) for s, t in zip(state, (rr * p, w * p, w * m, q * m))
        )

    main_r = rc.at[0]
    STEP = 4
    for low in range(0, rows, STEP):
        own_coefficients(HALO + low, STEP, True)
    for low in range(0, rows - 1, STEP):
        x_faces(HALO + low, min(STEP, rows - 1 - low))
    acc = (jnp.zeros((levels, cols), jnp.float32),) * 4
    for number in range(6):
        first, end = number + 1, rows - number - 1
        for low in range(first, end, STEP):
            n = min(STEP, end - low)
            q = sweep(number, coef, main_r, field, HALO + low, n)
            if number == 5:
                acc = products(acc, main_r, field, HALO + low, n, q)

    for way in range(8):
        dx, dy = WAYS[way]

        @pl.when(exists(-dx, -dy))
        def _():
            for copy in halo_copies(way):
                copy.wait_recv()

    for a in range(2):
        rc[a, 0:HALO] = jnp.transpose(x_in[a, 0], (1, 0, 2))[GROUP - HALO : GROUP]
        rc[a, HALO + rows : HALO + rows + HALO] = jnp.transpose(x_in[a, 1], (1, 0, 2))[0:HALO]
    for a in range(2):
        for side in range(2):
            edge = (0, LANES) if side == 0 else (last, cols)
            blocks = []
            for g, (row, slot) in ((0, (0, GROUP - HALO)), (groups - 1, (HALO + rows, 0))):
                low = width * g + own_low[side]
                block = rc[a, row : row + HALO, :, edge[0] : edge[1]]
                blocks.append((low, slot, rolled(block, low if side == 0 else low + 2 * HALO)))
            for i in range(GROUP):
                out = src[a, side, 1 + i]
                for low, slot, moved in blocks:
                    if 0 <= i - slot < HALO:
                        out = jnp.where((lane >= low) & (lane < low + 2 * HALO), moved[i - slot], out)
                for g in range(groups):
                    if g == 0:
                        if i < GROUP - HALO:
                            continue
                        tile = corner_in[3 if side == 0 else 2]
                    elif g == groups - 1:
                        if i >= HALO:
                            continue
                        tile = corner_in[1 if side == 0 else 0]
                    else:
                        tile = side_in[1 if side == 0 else 0, g - 1]
                    place = (a * GROUP + i) * STRIP + (STRIP - HALO if side == 0 else 0)
                    low = width * g + halo_low[side]
                    out = jnp.where(
                        (lane >= low) & (lane < low + HALO), rolled(tile, low - place), out
                    )
                src[a, side, 1 + i] = out
            wrap(src.at[a], side)

    edge_faces(0, HALO)
    edge_faces(HALO + rows - 1, HALO)
    edge_coefficients(1, HALO)
    edge_coefficients(HALO + rows - 1, HALO)
    for side in range(2):
        strip_coefficients(side)

    sacc = (jnp.zeros((levels, LANES), jnp.float32),) * 4
    PART = 3
    for number in range(6):
        for side in range(2):
            q = sweep(number, scoef.at[:, side], src.at[0, side], sfield.at[:, side], 1, GROUP)
            if number < 5:
                wrap(sfield.at[number], side)
            else:
                sacc = products(sacc, src.at[0, side], sfield.at[:, side], 1, GROUP, q)
        for base in (number + 1, rows - number - 1 + HALO):
            for low in range(base, base + HALO, PART):
                q = sweep(number, coef, main_r, field, low, PART)
                if number == 5:
                    acc = products(acc, main_r, field, low, PART, q)

    in_strip = jnp.zeros((levels, LANES), jnp.bool_)
    for g in range(1, tiles + 1):
        low = width * g + HALO
        in_strip = jnp.logical_or(in_strip, (lane >= low) & (lane < low + HALO))
    message = jnp.zeros((levels, LANES), jnp.float32)
    share = LANES // 4
    for i in range(4):
        s = jnp.where(in_strip, sacc[i], 0.0)
        for low in range(0, cols, LANES):
            part = acc[i][:, low : low + LANES]
            if low == 0:
                part = jnp.where(lane >= HALO, part, 0.0)
            if low == last:
                part = jnp.where(lane < LANES - HALO, part, 0.0)
            s = s + part
        s = s + rolled(s, 2 * share)
        s = s + rolled(s, share)
        message = jnp.where((lane >= i * share) & (lane < (i + 1) * share), s, message)
    total = jnp.sum(message, axis=0, keepdims=True)

    def finish():
        for number, out in ((PP, p_out), (WW, w_out), (MM, m_out), (NN, n_out)):
            for t in range(tiles):
                block = field[number, HALO + t * GROUP : HALO + (t + 1) * GROUP]
                parts = [block[:, :, low : low + LANES] for low in range(0, cols, LANES)]
                for side in range(2):
                    strip = sfield[number, side, 1 : 1 + GROUP]
                    low = width * (t + 1) + HALO
                    to = 0 if side == 0 else LANES - HALO
                    part = 0 if side == 0 else len(parts) - 1
                    parts[part] = jnp.where(
                        between(to, to + HALO, strip.shape), rolled(strip, to - low), parts[part]
                    )
                for k, part in enumerate(parts):
                    out[:, t * GROUP : (t + 1) * GROUP, k * LANES : (k + 1) * LANES] = jnp.transpose(
                        part, (1, 0, 2)
                    )
        r_out[...] = r_in[...]

    base = 0
    sent = []
    for index, stage in enumerate(stages):
        count = stage[0] * stage[1]
        mine, others = partners(stage)
        mine = base + mine
        slots[pl.ds(mine, 1), :] = total
        copies = [
            pltpu.make_async_remote_copy(
                src_ref=slots.at[pl.ds(mine, 1)], dst_ref=slots.at[pl.ds(mine, 1)],
                send_sem=red_send.at[index], recv_sem=red_recv.at[index],
                device_id=device, device_id_type=MESH,
            )
            for device in others
        ]
        for copy in copies:
            copy.start()
        if index == 0:
            finish()
        if count > 1:
            whole = slots.at[pl.ds(base, count - 1)]
            pltpu.make_async_copy(whole, whole, red_recv.at[index]).wait()
            sent.append((whole, red_send.at[index]))
        total = jnp.sum(slots[base : base + count], axis=0, keepdims=True)
        base += -(-count // 8) * 8
    sums_out[...] = total

    for way in range(8):

        @pl.when(exists(*WAYS[way]))
        def _():
            for copy in halo_copies(way):
                copy.wait_send()

    for whole, sem in sent:
        pltpu.make_async_copy(whole, whole, sem).wait()


def combine(p, w, m, n, r, sums, x_hbm, res_hbm, x_vmem, res_vmem, sem):
    levels = p.shape[0]
    total = sums[...]
    lane = lax.broadcasted_iota(jnp.int32, total.shape, 1)
    share = LANES // 4

    def of(i, scale):
        chosen = (lane >= i * share) & (lane < (i + 1) * share)
        return scale * jnp.sum(jnp.where(chosen, total, 0.0), axis=1, keepdims=True)

    rp, wp, wm, nm = (of(i, power_2 ** (i + 1)) for i in range(4))
    gamma_old = rp
    alpha_old = gamma_old / wp
    gamma = (rp - alpha_old * wp) - alpha_old * (wp - alpha_old * wm)
    delta = (wp - alpha_old * wm) - alpha_old * (wm - alpha_old * nm)
    beta = gamma / gamma_old
    alpha = gamma / (delta - beta * gamma / alpha_old)
    near = power_2 * (alpha_old + alpha * (1.0 + beta))
    far = (power_2 * power_2) * (alpha * alpha_old)
    copies = []
    for z in range(levels):
        x_vmem[z] = near * p[z] - far * m[z]
        res_vmem[z] = (r[z] - near * w[z]) + far * n[z]
        for a, (one, two) in enumerate(((x_vmem, x_hbm), (res_vmem, res_hbm))):
            copies.append(pltpu.make_async_copy(one.at[z], two.at[z], sem.at[a, z]))
            copies[-1].start()
    for copy in copies:
        copy.wait()


def solution(mesh):
    num_x, num_y = mesh.shape["gx"], mesh.shape["gy"]

    def per_device(right_side, conductivity):
        levels, rows, cols = right_side.shape
        high = rows + 2 * HALO
        tiles = rows // GROUP
        stages = stages_of(num_x, num_y)
        deep = sum(-(-(a * b) // 8) * 8 for a, b in stages)

        def body(*refs):
            kernel(num_x, num_y, *refs)

        block = (levels, rows, cols)
        full = (high, levels, cols)
        slim = (2, GROUP + 2, levels, LANES)
        out = jax.ShapeDtypeStruct(block, jnp.float32)
        sums = jax.ShapeDtypeStruct((1, LANES), jnp.float32)
        vmem = lambda shape: pltpu.VMEM(shape, jnp.float32)
        dma = lambda *n: pltpu.SemaphoreType.DMA(n)
        in_vmem = pl.BlockSpec(memory_space=pltpu.VMEM)
        in_hbm = pl.BlockSpec(memory_space=pltpu.HBM)
        parts = pl.pallas_call(
            body,
            out_shape=(out,) * 5 + (sums,),
            in_specs=[in_hbm] * 2,
            out_specs=(in_vmem,) * 6,
            scratch_shapes=[
                vmem(block), vmem(block), vmem((2, 2, levels, GROUP, cols)),
                vmem((2,) + full), vmem((2,) + slim),
                vmem((5,) + full), vmem((5,) + slim), vmem((6,) + full), vmem((6,) + slim),
                vmem((2, tiles, levels, LANES)), vmem((2, tiles, levels, LANES)),
                vmem((4, levels, LANES)), vmem((deep, LANES)),
                dma(2), dma(8, 2), dma(8, 2), dma(len(stages)), dma(len(stages)),
            ],
            compiler_params=pltpu.CompilerParams(
                collective_id=0, has_side_effects=True, vmem_limit_bytes=55000000
            ),
        )(right_side, conductivity)
        return pl.pallas_call(
            combine,
            out_shape=(out, out),
            in_specs=[in_vmem] * 6,
            out_specs=(in_hbm,) * 2,
            scratch_shapes=[vmem(block), vmem(block), dma(2, levels)],
            compiler_params=pltpu.CompilerParams(vmem_limit_bytes=4000000),
        )(*parts)

    return jax.shard_map(
        per_device,
        mesh=mesh,
        in_specs=(P(None, "gx", "gy"), P(None, "gx", "gy")),
        out_specs=(P(None, "gx", "gy"), P(None, "gx", "gy")),
        check_vma=False,
    )
```

```python
import jax
import jax.numpy as jnp
from jax import lax
from jax.experimental import pallas as pl
from jax.experimental.pallas import tpu as pltpu
from jax.sharding import PartitionSpec as P

low_bound = 0.4
high_bound = 12.0
cheb_theta = 0.5 * (high_bound + low_bound)
cheb_delta = 0.5 * (high_bound - low_bound)
cheb_sigma = cheb_theta / cheb_delta
rho_first = 1.0 / cheb_sigma
rho_second = 1.0 / (2.0 * cheb_sigma - rho_first)
rho_third = 1.0 / (2.0 * cheb_sigma - rho_second)

step_0 = rho_second * rho_first / cheb_theta + 2.0 * rho_second / cheb_delta
step_1 = 2.0 * rho_second / cheb_delta / cheb_theta
mix_0 = 1.0 + rho_third * rho_second
mix_1 = 2.0 * rho_third / cheb_delta
power_0 = 1.0 / cheb_theta + mix_0 * step_0 + mix_1
power_1 = -mix_0 * step_1 - mix_1 / cheb_theta - mix_1 * step_0
power_2 = mix_1 * step_1
shift_1 = power_1 / power_2
shift_0 = power_0 / power_2

HALO = 6
AHEAD = 2
LANES = 128
STRIP = 8
GROUP = 8
ONE_STAGE = 64
MESH = pl.DeviceIdType.MESH
LOGICAL = pl.DeviceIdType.LOGICAL
WAYS = ((-1, 0), (1, 0), (0, -1), (0, 1), (-1, -1), (-1, 1), (1, -1), (1, 1))


def stages_of(num_x, num_y):
    if num_x * num_y <= ONE_STAGE:
        return ((num_x, num_y),)
    return ((num_x, 1), (1, num_y))


def kernel(
    num_x, num_y, r_hbm, c_hbm, p_out, w_out, m_out, n_out, r_out, sums_out,
    fresh, x_in, coef, scoef, field, sfield, packed, side_in, corner_in, slots,
    in_sem, halo_send, halo_recv, red_send, red_recv,
):
    _, levels, rows, cols = fresh.shape
    tiles = rows // GROUP
    groups = tiles + 2
    width = LANES // groups
    last = cols - LANES
    me_x = lax.axis_index("gx")
    me_y = lax.axis_index("gy")
    stages = stages_of(num_x, num_y)

    def exists(dx, dy):
        ok = jnp.bool_(True)
        if dx < 0:
            ok = me_x > 0
        if dx > 0:
            ok = me_x < num_x - 1
        if dy < 0:
            ok_y = me_y > 0
            ok = ok_y if dx == 0 else jnp.logical_and(ok, ok_y)
        if dy > 0:
            ok_y = me_y < num_y - 1
            ok = ok_y if dx == 0 else jnp.logical_and(ok, ok_y)
        return ok

    loads = [
        pltpu.make_async_copy(ref, fresh.at[a], in_sem.at[a])
        for a, ref in enumerate((c_hbm, r_hbm))
    ]
    for load in loads:
        load.start()

    def place_in(stage):
        count_x, count_y = stage
        if count_x > 1 and count_y > 1:
            return me_x * num_y + me_y, lambda o: o
        if count_x > 1:
            return me_x, lambda o: o * num_y + me_y
        return me_y, lambda o: me_x * num_y + o

    def each_other(stage, act):
        mine, device = place_in(stage)
        total = stage[0] * stage[1]

        def step(k, state):
            other = mine + k
            act(device(jnp.where(other >= total, other - total, other)))
            return state

        lax.fori_loop(1, total, step, 0)

    barrier = pltpu.get_barrier_semaphore()

    def greet(device):
        pl.semaphore_signal(barrier, inc=1, device_id=device, device_id_type=LOGICAL)

    expected = jnp.int32(0)
    for stage in stages:
        each_other(stage, greet)
        expected = expected + (stage[0] * stage[1] - 1)
    if len(stages) > 1:
        for dx, dy in WAYS[4:]:
            ok = exists(dx, dy)

            @pl.when(ok)
            def _():
                greet((me_x + dx) * num_y + me_y + dy)

            expected = expected + ok.astype(jnp.int32)
    pl.semaphore_wait(barrier, expected)

    def halo_copies(way):
        dx, dy = WAYS[way]
        if dy == 0:
            side = 1 if dx < 0 else 0
            low = 0 if dx < 0 else rows - HALO
            land = 0 if dx < 0 else GROUP - HALO
            pairs = [
                (ref.at[:, pl.ds(low, HALO)], x_in.at[a, side, :, pl.ds(land, HALO)])
                for a, ref in enumerate((c_hbm, r_hbm))
            ]
        elif dx == 0:
            pairs = [(packed.at[0 if dy < 0 else 1], side_in.at[0 if dy < 0 else 1])]
        else:
            pairs = [(
                packed.at[0 if dy < 0 else 1, 0 if dx < 0 else tiles - 1],
                corner_in.at[way - 4],
            )]
        return [
            pltpu.make_async_remote_copy(
                src_ref=one, dst_ref=two,
                send_sem=halo_send.at[way, a], recv_sem=halo_recv.at[way, a],
                device_id=(me_x + dx, me_y + dy), device_id_type=MESH,
            )
            for a, (one, two) in enumerate(pairs)
        ]

    def start(way):
        @pl.when(exists(*WAYS[way]))
        def _():
            for copy in halo_copies(way):
                copy.start()

    for way in (0, 1):
        start(way)

    lane = lax.broadcasted_iota(jnp.int32, (levels, LANES), 1)

    def between(low, high, like):
        at = lax.broadcasted_iota(jnp.int32, (1,) * (len(like) - 1) + (LANES,), len(like) - 1)
        return (at >= low) & (at < high)

    def rolled(v, by):
        if isinstance(by, int):
            by = by % v.shape[-1]
            if by == 0:
                return v
        return pltpu.roll(v, by, v.ndim - 1)

    for load in loads:
        load.wait()

    def arrange(t, state):
        low = pl.multiple_of(t * GROUP, GROUP)
        for a in range(2):
            block = jnp.transpose(fresh[a, :, pl.ds(low, GROUP), :], (1, 0, 2))
            field[a, pl.ds(HALO + low, GROUP)] = block
            for side in range(2):
                offset = 0 if side == 0 else LANES - STRIP
                part = block[:, :, (0 if side == 0 else last) : (LANES if side == 0 else cols)]
                acc = jnp.zeros((levels, LANES), jnp.float32) if a == 0 else packed[side, t]
                for g in range(GROUP):
                    place = (a * GROUP + g) * STRIP
                    moved = rolled(part[g], place - offset)
                    acc = jnp.where((lane >= place) & (lane < place + STRIP), moved, acc)
                packed[side, t] = acc
        return state

    lax.fori_loop(0, tiles, arrange, 0)
    for way in (2, 3, 4, 5, 6, 7):
        start(way)

    for way in range(8):
        dx, dy = WAYS[way]

        @pl.when(jnp.logical_not(exists(-dx, -dy)))
        def _():
            if dy == 0:
                x_in[:, 1 if dx < 0 else 0] = jnp.zeros((2, levels, GROUP, cols), jnp.float32)
            elif dx == 0:
                side_in[0 if dy < 0 else 1] = jnp.zeros((tiles, levels, LANES), jnp.float32)
            else:
                corner_in[way - 4] = jnp.zeros((levels, LANES), jnp.float32)

    def own_strips(a, state):
        for side in range(2):
            acc = jnp.zeros((GROUP, levels, LANES), jnp.float32)
            for g in range(1, tiles + 1):
                low = width * g + HALO * (1 - side)
                block = field[
                    a, HALO + (g - 1) * GROUP : HALO + g * GROUP, :,
                    (0 if side == 0 else last) : (LANES if side == 0 else cols),
                ]
                moved = rolled(block, low + 2 * HALO * side)
                acc = jnp.where(between(low, low + 2 * HALO, block.shape), moved, acc)
            sfield[a, side, 1 : 1 + GROUP] = acc
        return state

    lax.fori_loop(0, 2, own_strips, 0)

    def wrap(f, side):
        sfield[f, side, 0] = rolled(sfield[f, side, GROUP], width)
        sfield[f, side, GROUP + 1] = rolled(sfield[f, side, 1], -width)

    def level_of(shape):
        return lax.broadcasted_iota(jnp.int32, (1, levels, shape[-1]), 1)

    def faces(c, other):
        return jnp.where(jnp.minimum(c, other) > 0.0, 0.5 * (c + other), 0.0)

    def coefficients(low, n, beside):
        c = field[0, pl.ds(low, n)]
        level = level_of(c.shape)
        at = lax.broadcasted_iota(jnp.int32, (1, 1, cols), 2)
        half = 0.5 * c
        inner = jnp.logical_and(level > 0, level < levels - 1)
        kb = jnp.where(inner, 0.0, half)
        if beside:
            for other in (field[0, pl.ds(low - 1, n)], field[0, pl.ds(low + 1, n)]):
                kb = kb + jnp.where(other > 0.0, 0.0, half)
        coef[1, pl.ds(low, n)] = jnp.where(at < cols - 1, half + rolled(half, cols - 1), 0.0)
        coef[5, pl.ds(low, n)] = jnp.where(at > 0, half + rolled(half, 1), 0.0)
        coef[2, pl.ds(low, n)] = jnp.where(
            level < levels - 1, half + pltpu.roll(half, levels - 1, 1), 0.0
        )
        coef[3, pl.ds(low, n)] = kb
        coef[4, pl.ds(low, n)] = kb + shift_1

    def strip_coefficients(side, state):
        c = sfield[0, side, 1 : 1 + GROUP]
        level = level_of(c.shape)
        half = 0.5 * c
        inner = jnp.logical_and(level > 0, level < levels - 1)
        east, west = rolled(c, LANES - 1), rolled(c, 1)
        kb = jnp.where(inner, 0.0, half)
        for other in (east, west, sfield[0, side, 0:GROUP], sfield[0, side, 2 : 2 + GROUP]):
            kb = kb + jnp.where(other > 0.0, 0.0, half)
        scoef[0, side, 0 : GROUP + 1] = faces(
            sfield[0, side, 0 : GROUP + 1], sfield[0, side, 1 : GROUP + 2]
        )
        scoef[1, side, 1 : 1 + GROUP] = faces(c, east)
        scoef[5, side, 1 : 1 + GROUP] = faces(c, west)
        scoef[2, side, 1 : 1 + GROUP] = jnp.where(
            level < levels - 1, half + pltpu.roll(half, levels - 1, 1), 0.0
        )
        scoef[3, side, 1 : 1 + GROUP] = kb
        scoef[4, side, 1 : 1 + GROUP] = kb + shift_1
        return state

    def turned(read, low, n, j):
        v = read(j + 1, low, n)
        down, up = read(j + 1, low - 1, n), read(j + 1, low + 1, n)
        return v, rolled(v, v.shape[-1] - 1), rolled(v, 1), down, up

    def image(read, k, low, n, j, around):
        third = j % 3 if isinstance(j, int) else lax.rem(j, 3)
        shifted = 4 - (third + 1) // 2
        v, east, west, down, up = around
        axis = v.ndim - 1
        across = k(0, low, n) * (v - up)
        back = k(0, low - 1, n) * (down - v)
        fz = k(2, low, n) * (v - pltpu.roll(v, levels - 1, axis - 1))
        rest = (across - back) + ((fz - pltpu.roll(fz, 1, axis - 1)) + k(shifted, low, n) * v)
        if not isinstance(j, int):
            also = jnp.where(third == 1, shift_0, 0.0)
            rest = rest + also * read(jnp.maximum(j, 1), low, n)
        elif third == 1:
            rest = rest + shift_0 * read(j, low, n)
        return rest + (k(1, low, n) * (v - east) + k(5, low, n) * (v - west))

    def images(jobs, j):
        ahead = AHEAD
        around = [turned(read, low, n, j) for read, k, low, n, put in jobs[:ahead]]
        for i, (read, k, low, n, put) in enumerate(jobs):
            if i + ahead < len(jobs):
                other = jobs[i + ahead]
                around.append(turned(other[0], other[2], other[3], j))
            put(j + 2, low, n, image(read, k, low, n, j, around[i]))

    def main(f, low, n):
        return field[f, pl.ds(low, n)]

    def main_k(i, low, n):
        return coef[i, pl.ds(low, n)]

    def main_put(f, low, n, v):
        field[f, pl.ds(low, n)] = v

    def summed(read, low, n, state):
        r, p, w, m, q = (read(f, low, n) for f in (1, 3, 4, 6, 7))
        return tuple(
            s + jnp.sum(t, axis=0) for s, t in zip(state, (r * p, w * p, w * m, q * m))
        )

    STEP = 4

    WIDE = 2 * GROUP

    def own_coefficients(i, state):
        low = HALO + i * WIDE
        coefficients(low, WIDE, False)
        coef[0, pl.ds(low, WIDE)] = 0.5 * (
            field[0, pl.ds(low, WIDE)] + field[0, pl.ds(low + 1, WIDE)]
        )
        return state

    lax.fori_loop(0, rows // WIDE, own_coefficients, 0)

    def own_image(j, state):
        images([(main, main_k, HALO + low, STEP, main_put) for low in range(0, rows, STEP)], j)
        return state

    lax.fori_loop(0, 6, own_image, 0)
    zero = jnp.zeros((levels, cols), jnp.float32)
    acc = lax.fori_loop(
        0, (rows - 2 * HALO) // STEP,
        lambda i, state: summed(main, 2 * HALO + i * STEP, STEP, state), (zero,) * 4,
    )

    for way in range(8):
        dx, dy = WAYS[way]

        @pl.when(exists(-dx, -dy))
        def _():
            for copy in halo_copies(way):
                copy.wait_recv()

    def halo_of(a, state):
        field[a, 0:HALO] = jnp.transpose(x_in[a, 0], (1, 0, 2))[GROUP - HALO : GROUP]
        field[a, HALO + rows : HALO + rows + HALO] = jnp.transpose(x_in[a, 1], (1, 0, 2))[0:HALO]
        for side in range(2):
            edge = (0, LANES) if side == 0 else (last, cols)
            blocks = []
            for g, (row, slot) in ((0, (0, GROUP - HALO)), (groups - 1, (HALO + rows, 0))):
                low = width * g + HALO * (1 - side)
                block = field[a, row : row + HALO, :, edge[0] : edge[1]]
                blocks.append((low, slot, rolled(block, low + 2 * HALO * side)))
            for i in range(GROUP):
                out = sfield[a, side, 1 + i]
                for low, slot, moved in blocks:
                    if 0 <= i - slot < HALO:
                        out = jnp.where((lane >= low) & (lane < low + 2 * HALO), moved[i - slot], out)
                for g in range(groups):
                    if g == 0:
                        if i < GROUP - HALO:
                            continue
                        tile = corner_in[3 - side]
                    elif g == groups - 1:
                        if i >= HALO:
                            continue
                        tile = corner_in[1 - side]
                    else:
                        tile = side_in[1 - side, g - 1]
                    low = width * g + 2 * HALO * side
                    by = low - i * STRIP - (STRIP - HALO) * (1 - side)
                    moved = rolled(tile, by - a * (GROUP * STRIP))
                    out = jnp.where((lane >= low) & (lane < low + HALO), moved, out)
                sfield[a, side, 1 + i] = out
            wrap(a, side)
        return state

    for a in range(2):
        halo_of(a, 0)

    def edges(i, state):
        low = 1 + i * (HALO + rows - 2)
        coefficients(low, HALO, True)
        first = low - 1 + i
        coef[0, pl.ds(first, HALO)] = faces(
            field[0, pl.ds(first, HALO)], field[0, pl.ds(first + 1, HALO)]
        )
        return state

    for i in range(2):
        edges(i, 0)
        strip_coefficients(i, 0)

    PART = 3
    HALF = GROUP // 2

    def strip_job(side, low):
        def read(f, at, n):
            if at == 0:
                first = rolled(sfield[f, side, pl.ds(GROUP, 1)], width)
                return jnp.concatenate([first, sfield[f, side, pl.ds(1, n - 1)]], axis=0)
            if at + n == GROUP + 2:
                last_row = rolled(sfield[f, side, pl.ds(1, 1)], -width)
                return jnp.concatenate([sfield[f, side, pl.ds(at, n - 1)], last_row], axis=0)
            return sfield[f, side, pl.ds(at, n)]

        def k(i, at, n):
            return scoef[i, side, pl.ds(at, n)]

        def put(f, at, n, v):
            sfield[f, side, pl.ds(at, n)] = v

        return read, k, low, HALF, put

    def edge_image(j):
        jobs = []
        for base in (j + 1, rows - 1 - j + HALO):
            jobs += [(main, main_k, low, PART, main_put) for low in (base, base + PART)]
        strips = [strip_job(side, low) for side in range(2) for low in (1, 1 + HALF)]
        images(jobs + strips, j)

    for j in range(6):
        edge_image(j)
    for base in (HALO, rows):
        for low in (base, base + PART):
            acc = summed(main, low, PART, acc)
    sacc = (jnp.zeros((levels, LANES), jnp.float32),) * 4
    for side in range(2):
        sacc = summed(lambda f, low, n: sfield[f, side, pl.ds(low, n)], 1, GROUP, sacc)

    in_strip = jnp.zeros((levels, LANES), jnp.bool_)
    for g in range(1, tiles + 1):
        low = width * g + HALO
        in_strip = jnp.logical_or(in_strip, (lane >= low) & (lane < low + HALO))
    message = jnp.zeros((levels, LANES), jnp.float32)
    share = LANES // 4
    for i in range(4):
        s = jnp.where(in_strip, sacc[i], 0.0)
        for low in range(0, cols, LANES):
            part = acc[i][:, low : low + LANES]
            if low == 0:
                part = jnp.where(lane >= HALO, part, 0.0)
            if low == last:
                part = jnp.where(lane < LANES - HALO, part, 0.0)
            s = s + part
        s = s + rolled(s, 2 * share)
        s = s + rolled(s, share)
        message = jnp.where((lane >= i * share) & (lane < (i + 1) * share), s, message)
    total = jnp.sum(message, axis=0, keepdims=True)

    def finish(t, state):
        low = pl.multiple_of(t * GROUP, GROUP)
        for f, out in ((3, p_out), (4, w_out), (6, m_out), (7, n_out)):
            block = field[f, pl.ds(HALO + low, GROUP)]
            parts = [block[:, :, k : k + LANES] for k in range(0, cols, LANES)]
            for side in range(2):
                strip = sfield[f, side, 1 : 1 + GROUP]
                to = 0 if side == 0 else LANES - HALO
                part = 0 if side == 0 else len(parts) - 1
                by = lax.rem(to - HALO - width + 2 * LANES - width * t, LANES)
                parts[part] = jnp.where(
                    between(to, to + HALO, strip.shape), rolled(strip, by), parts[part]
                )
            for k, part in enumerate(parts):
                out[:, pl.ds(low, GROUP), k * LANES : (k + 1) * LANES] = jnp.transpose(
                    part, (1, 0, 2)
                )
        return state

    base = 0
    sent = []
    for index, stage in enumerate(stages):
        count = stage[0] * stage[1]
        mine = base + place_in(stage)[0]
        slots[pl.ds(mine, 1), :] = total

        def send(device):
            pltpu.make_async_remote_copy(
                src_ref=slots.at[pl.ds(mine, 1)], dst_ref=slots.at[pl.ds(mine, 1)],
                send_sem=red_send.at[index], recv_sem=red_recv.at[index],
                device_id=device, device_id_type=LOGICAL,
            ).start()

        each_other(stage, send)
        if index == 0:
            lax.fori_loop(0, tiles, finish, 0)
            r_out[...] = fresh[1]
            for way in range(8):

                @pl.when(exists(*WAYS[way]))
                def _():
                    for copy in halo_copies(way):
                        copy.wait_send()

        if count > 1:
            whole = slots.at[pl.ds(base, count - 1)]
            pltpu.make_async_copy(whole, whole, red_recv.at[index]).wait()
            sent.append((whole, red_send.at[index]))
        total = jnp.sum(slots[base : base + count], axis=0, keepdims=True)
        base += -(-count // 8) * 8
    sums_out[...] = total
    for whole, sem in sent:
        pltpu.make_async_copy(whole, whole, sem).wait()


def combine(p, w, m, n, r, sums, x_hbm, res_hbm, x_vmem, res_vmem, sem):
    levels = p.shape[0]
    total = sums[...]
    lane = lax.broadcasted_iota(jnp.int32, total.shape, 1)
    share = LANES // 4

    def of(i, scale):
        chosen = (lane >= i * share) & (lane < (i + 1) * share)
        return scale * jnp.sum(jnp.where(chosen, total, 0.0), axis=1, keepdims=True)

    rp, wp, wm, nm = (of(i, power_2 ** (i + 1)) for i in range(4))
    gamma_old = rp
    alpha_old = gamma_old / wp
    gamma = (rp - alpha_old * wp) - alpha_old * (wp - alpha_old * wm)
    delta = (wp - alpha_old * wm) - alpha_old * (wm - alpha_old * nm)
    beta = gamma / gamma_old
    alpha = gamma / (delta - beta * gamma / alpha_old)
    near = power_2 * (alpha_old + alpha * (1.0 + beta))
    far = (power_2 * power_2) * (alpha * alpha_old)
    copies = []
    for z in range(levels):
        x_vmem[z] = near * p[z] - far * m[z]
        res_vmem[z] = (r[z] - near * w[z]) + far * n[z]
        for a, (one, two) in enumerate(((x_vmem, x_hbm), (res_vmem, res_hbm))):
            copies.append(pltpu.make_async_copy(one.at[z], two.at[z], sem.at[a, z]))
            copies[-1].start()
    for copy in copies:
        copy.wait()


def solution(mesh):
    num_x, num_y = mesh.shape["gx"], mesh.shape["gy"]

    def per_device(right_side, conductivity):
        levels, rows, cols = right_side.shape
        high = rows + 2 * HALO
        tiles = rows // GROUP
        stages = stages_of(num_x, num_y)
        deep = sum(-(-(a * b) // 8) * 8 for a, b in stages)

        def body(*refs):
            kernel(num_x, num_y, *refs)

        block = (levels, rows, cols)
        full = (high, levels, cols)
        slim = (2, GROUP + 2, levels, LANES)
        out = jax.ShapeDtypeStruct(block, jnp.float32)
        sums = jax.ShapeDtypeStruct((1, LANES), jnp.float32)
        vmem = lambda shape: pltpu.VMEM(shape, jnp.float32)
        dma = lambda *n: pltpu.SemaphoreType.DMA(n)
        in_vmem = pl.BlockSpec(memory_space=pltpu.VMEM)
        in_hbm = pl.BlockSpec(memory_space=pltpu.HBM)
        parts = pl.pallas_call(
            body,
            out_shape=(out,) * 5 + (sums,),
            in_specs=[in_hbm] * 2,
            out_specs=(in_vmem,) * 6,
            scratch_shapes=[
                vmem((2,) + block), vmem((2, 2, levels, GROUP, cols)),
                vmem((6,) + full), vmem((6,) + slim), vmem((8,) + full), vmem((8,) + slim),
                vmem((2, tiles, levels, LANES)), vmem((2, tiles, levels, LANES)),
                vmem((4, levels, LANES)), vmem((deep, LANES)),
                dma(2), dma(8, 2), dma(8, 2), dma(len(stages)), dma(len(stages)),
            ],
            compiler_params=pltpu.CompilerParams(
                collective_id=0, has_side_effects=True, vmem_limit_bytes=55000000
            ),
        )(right_side, conductivity)
        return pl.pallas_call(
            combine,
            out_shape=(out, out),
            in_specs=[in_vmem] * 6,
            out_specs=(in_hbm,) * 2,
            scratch_shapes=[vmem(block), vmem(block), dma(2, levels)],
            compiler_params=pltpu.CompilerParams(vmem_limit_bytes=4000000),
        )(*parts)

    return jax.shard_map(
        per_device,
        mesh=mesh,
        in_specs=(P(None, "gx", "gy"), P(None, "gx", "gy")),
        out_specs=(P(None, "gx", "gy"), P(None, "gx", "gy")),
        check_vma=False,
    )
```

```python
import jax
import jax.numpy as jnp
from jax import lax
from jax.experimental import pallas as pl
from jax.experimental.pallas import tpu as pltpu
from jax.sharding import PartitionSpec as P

low_bound = 0.4
high_bound = 12.0
cheb_theta = 0.5 * (high_bound + low_bound)
cheb_delta = 0.5 * (high_bound - low_bound)
cheb_sigma = cheb_theta / cheb_delta
rho_first = 1.0 / cheb_sigma
rho_second = 1.0 / (2.0 * cheb_sigma - rho_first)
rho_third = 1.0 / (2.0 * cheb_sigma - rho_second)

step_0 = rho_second * rho_first / cheb_theta + 2.0 * rho_second / cheb_delta
step_1 = 2.0 * rho_second / cheb_delta / cheb_theta
mix_0 = 1.0 + rho_third * rho_second
mix_1 = 2.0 * rho_third / cheb_delta
power_0 = 1.0 / cheb_theta + mix_0 * step_0 + mix_1
power_1 = -mix_0 * step_1 - mix_1 / cheb_theta - mix_1 * step_0
power_2 = mix_1 * step_1
shift_1 = power_1 / power_2
shift_0 = power_0 / power_2

HALO = 6
AHEAD = 2
NEAR = 2
LANES = 128
STRIP = 8
GROUP = 8
ONE_STAGE = 64
MESH = pl.DeviceIdType.MESH
LOGICAL = pl.DeviceIdType.LOGICAL
WAYS = ((-1, 0), (1, 0), (0, -1), (0, 1), (-1, -1), (-1, 1), (1, -1), (1, 1))


def stages_of(num_x, num_y):
    if num_x * num_y <= ONE_STAGE:
        return ((num_x, num_y),)
    return ((num_x, 1), (1, num_y))


def kernel(
    num_x, num_y, r_hbm, c_hbm, p_out, w_out, m_out, n_out, r_out, sums_out,
    fresh, x_in, coef, scoef, field, sfield, packed, side_in, corner_in, slots,
    in_sem, halo_send, halo_recv, red_send, red_recv, relayed,
):
    _, levels, rows, cols = fresh.shape
    tiles = rows // GROUP
    groups = tiles + 2
    width = LANES // groups
    last = cols - LANES
    me_x = lax.axis_index("gx")
    me_y = lax.axis_index("gy")
    stages = stages_of(num_x, num_y)

    def exists(dx, dy):
        ok = jnp.bool_(True)
        if dx < 0:
            ok = me_x > 0
        if dx > 0:
            ok = me_x < num_x - 1
        if dy < 0:
            ok_y = me_y > 0
            ok = ok_y if dx == 0 else jnp.logical_and(ok, ok_y)
        if dy > 0:
            ok_y = me_y < num_y - 1
            ok = ok_y if dx == 0 else jnp.logical_and(ok, ok_y)
        return ok

    loads = [
        pltpu.make_async_copy(ref, fresh.at[a], in_sem.at[a])
        for a, ref in enumerate((c_hbm, r_hbm))
    ]
    for load in loads:
        load.start()

    def place_in(stage):
        count_x, count_y = stage
        if count_x > 1 and count_y > 1:
            return me_x * num_y + me_y, lambda o: o
        if count_x > 1:
            return me_x, lambda o: o * num_y + me_y
        return me_y, lambda o: me_x * num_y + o

    def each_other(stage, act):
        mine, device = place_in(stage)
        total = stage[0] * stage[1]

        def step(k, state):
            other = mine + k
            act(device(jnp.where(other >= total, other - total, other)))
            return state

        lax.fori_loop(1, total, step, 0)

    barrier = pltpu.get_barrier_semaphore()

    def greet(device):
        pl.semaphore_signal(barrier, inc=1, device_id=device, device_id_type=LOGICAL)

    relays = []
    while len(stages) == 1 and NEAR << len(relays) < num_x - 1:
        relays.append(NEAR << len(relays))
    expected = jnp.int32(0)
    if relays:
        mine = me_x * num_y + me_y
        first = (me_x - NEAR) * num_y

        def near(k, count):
            other = first + k
            ok = (other >= 0) & (other < num_x * num_y) & (other != mine)

            @pl.when(ok)
            def _():
                greet(other)

            return count + ok.astype(jnp.int32)

        expected = lax.fori_loop(0, (2 * NEAR + 1) * num_y, near, expected)
    else:
        for stage in stages:
            each_other(stage, greet)
            expected = expected + (stage[0] * stage[1] - 1)
    if len(stages) > 1:
        for dx, dy in WAYS[4:]:
            ok = exists(dx, dy)

            @pl.when(ok)
            def _():
                greet((me_x + dx) * num_y + me_y + dy)

            expected = expected + ok.astype(jnp.int32)

    def relay(index):
        far = relays[index]
        for other, ok in ((me_x - far, me_x >= far), (me_x + far, me_x < num_x - far)):

            @pl.when(ok)
            def _():
                pl.semaphore_signal(
                    relayed.at[index], inc=1, device_id=other * num_y + me_y,
                    device_id_type=LOGICAL,
                )

    def relay_wait(index):
        far = relays[index]
        count = (me_x >= far).astype(jnp.int32) + (me_x < num_x - far).astype(jnp.int32)
        pl.semaphore_wait(relayed.at[index], count)

    def halo_copies(way):
        dx, dy = WAYS[way]
        if dy == 0:
            side = 1 if dx < 0 else 0
            low = 0 if dx < 0 else rows - HALO
            land = 0 if dx < 0 else GROUP - HALO
            pairs = [
                (ref.at[:, pl.ds(low, HALO)], x_in.at[a, side, :, pl.ds(land, HALO)])
                for a, ref in enumerate((c_hbm, r_hbm))
            ]
        elif dx == 0:
            pairs = [(packed.at[0 if dy < 0 else 1], side_in.at[0 if dy < 0 else 1])]
        else:
            pairs = [(
                packed.at[0 if dy < 0 else 1, 0 if dx < 0 else tiles - 1],
                corner_in.at[way - 4],
            )]
        return [
            pltpu.make_async_remote_copy(
                src_ref=one, dst_ref=two,
                send_sem=halo_send.at[way, a], recv_sem=halo_recv.at[way, a],
                device_id=(me_x + dx, me_y + dy), device_id_type=MESH,
            )
            for a, (one, two) in enumerate(pairs)
        ]

    def start(way):
        @pl.when(exists(*WAYS[way]))
        def _():
            for copy in halo_copies(way):
                copy.start()


    lane = lax.broadcasted_iota(jnp.int32, (levels, LANES), 1)

    def between(low, high, like):
        at = lax.broadcasted_iota(jnp.int32, (1,) * (len(like) - 1) + (LANES,), len(like) - 1)
        return (at >= low) & (at < high)

    def rolled(v, by):
        if isinstance(by, int):
            by = by % v.shape[-1]
            if by == 0:
                return v
        return pltpu.roll(v, by, v.ndim - 1)

    for load in loads:
        load.wait()

    def arrange(t, state):
        low = pl.multiple_of(t * GROUP, GROUP)
        for a in range(2):
            block = jnp.transpose(fresh[a, :, pl.ds(low, GROUP), :], (1, 0, 2))
            field[a, pl.ds(HALO + low, GROUP)] = block
            for side in range(2):
                offset = 0 if side == 0 else LANES - STRIP
                part = block[:, :, (0 if side == 0 else last) : (LANES if side == 0 else cols)]
                acc = jnp.zeros((levels, LANES), jnp.float32) if a == 0 else packed[side, t]
                for g in range(GROUP):
                    place = (a * GROUP + g) * STRIP
                    moved = rolled(part[g], place - offset)
                    acc = jnp.where((lane >= place) & (lane < place + STRIP), moved, acc)
                packed[side, t] = acc
        return state

    lax.fori_loop(0, tiles, arrange, 0)
    pl.semaphore_wait(barrier, expected)
    for way in (4, 5, 6, 7, 2, 3, 0, 1):
        start(way)
    if relays:
        relay(0)

    for way in range(8):
        dx, dy = WAYS[way]

        @pl.when(jnp.logical_not(exists(-dx, -dy)))
        def _():
            if dy == 0:
                x_in[:, 1 if dx < 0 else 0] = jnp.zeros((2, levels, GROUP, cols), jnp.float32)
            elif dx == 0:
                side_in[0 if dy < 0 else 1] = jnp.zeros((tiles, levels, LANES), jnp.float32)
            else:
                corner_in[way - 4] = jnp.zeros((levels, LANES), jnp.float32)

    def own_strips(a, state):
        for side in range(2):
            acc = jnp.zeros((GROUP, levels, LANES), jnp.float32)
            for g in range(1, tiles + 1):
                low = width * g + HALO * (1 - side)
                block = field[
                    a, HALO + (g - 1) * GROUP : HALO + g * GROUP, :,
                    (0 if side == 0 else last) : (LANES if side == 0 else cols),
                ]
                moved = rolled(block, low + 2 * HALO * side)
                acc = jnp.where(between(low, low + 2 * HALO, block.shape), moved, acc)
            sfield[a, side, 1 : 1 + GROUP] = acc
        return state

    lax.fori_loop(0, 2, own_strips, 0)

    def wrap(f, side):
        sfield[f, side, 0] = rolled(sfield[f, side, GROUP], width)
        sfield[f, side, GROUP + 1] = rolled(sfield[f, side, 1], -width)

    def level_of(shape):
        return lax.broadcasted_iota(jnp.int32, (1, levels, shape[-1]), 1)

    def faces(c, other):
        return jnp.where(jnp.minimum(c, other) > 0.0, 0.5 * (c + other), 0.0)

    def coefficients(low, n, beside):
        c = field[0, pl.ds(low, n)]
        level = level_of(c.shape)
        at = lax.broadcasted_iota(jnp.int32, (1, 1, cols), 2)
        half = 0.5 * c
        inner = jnp.logical_and(level > 0, level < levels - 1)
        kb = jnp.where(inner, 0.0, half)
        if beside:
            for other in (field[0, pl.ds(low - 1, n)], field[0, pl.ds(low + 1, n)]):
                kb = kb + jnp.where(other > 0.0, 0.0, half)
        coef[1, pl.ds(low, n)] = jnp.where(at < cols - 1, half + rolled(half, cols - 1), 0.0)
        coef[5, pl.ds(low, n)] = jnp.where(at > 0, half + rolled(half, 1), 0.0)
        coef[2, pl.ds(low, n)] = jnp.where(
            level < levels - 1, half + pltpu.roll(half, levels - 1, 1), 0.0
        )
        coef[3, pl.ds(low, n)] = kb
        coef[4, pl.ds(low, n)] = kb + shift_1

    def strip_coefficients(side, state):
        c = sfield[0, side, 1 : 1 + GROUP]
        level = level_of(c.shape)
        half = 0.5 * c
        inner = jnp.logical_and(level > 0, level < levels - 1)
        east, west = rolled(c, LANES - 1), rolled(c, 1)
        kb = jnp.where(inner, 0.0, half)
        for other in (east, west, sfield[0, side, 0:GROUP], sfield[0, side, 2 : 2 + GROUP]):
            kb = kb + jnp.where(other > 0.0, 0.0, half)
        scoef[0, side, 0 : GROUP + 1] = faces(
            sfield[0, side, 0 : GROUP + 1], sfield[0, side, 1 : GROUP + 2]
        )
        scoef[1, side, 1 : 1 + GROUP] = faces(c, east)
        scoef[5, side, 1 : 1 + GROUP] = faces(c, west)
        scoef[2, side, 1 : 1 + GROUP] = jnp.where(
            level < levels - 1, half + pltpu.roll(half, levels - 1, 1), 0.0
        )
        scoef[3, side, 1 : 1 + GROUP] = kb
        scoef[4, side, 1 : 1 + GROUP] = kb + shift_1
        return state

    def turned(read, low, n, j):
        v = read(j + 1, low, n)
        down, up = read(j + 1, low - 1, n), read(j + 1, low + 1, n)
        return v, rolled(v, v.shape[-1] - 1), rolled(v, 1), down, up

    def image(read, k, low, n, j, around):
        third = j % 3 if isinstance(j, int) else lax.rem(j, 3)
        shifted = 4 - (third + 1) // 2
        v, east, west, down, up = around
        axis = v.ndim - 1
        across = k(0, low, n) * (v - up)
        back = k(0, low - 1, n) * (down - v)
        fz = k(2, low, n) * (v - pltpu.roll(v, levels - 1, axis - 1))
        rest = (across - back) + ((fz - pltpu.roll(fz, 1, axis - 1)) + k(shifted, low, n) * v)
        if not isinstance(j, int):
            also = jnp.where(third == 1, shift_0, 0.0)
            rest = rest + also * read(jnp.maximum(j, 1), low, n)
        elif third == 1:
            rest = rest + shift_0 * read(j, low, n)
        return rest + (k(1, low, n) * (v - east) + k(5, low, n) * (v - west))

    def images(jobs, j):
        ahead = AHEAD
        around = [turned(read, low, n, j) for read, k, low, n, put in jobs[:ahead]]
        for i, (read, k, low, n, put) in enumerate(jobs):
            if i + ahead < len(jobs):
                other = jobs[i + ahead]
                around.append(turned(other[0], other[2], other[3], j))
            put(j + 2, low, n, image(read, k, low, n, j, around[i]))

    def main(f, low, n):
        return field[f, pl.ds(low, n)]

    def main_k(i, low, n):
        return coef[i, pl.ds(low, n)]

    def main_put(f, low, n, v):
        field[f, pl.ds(low, n)] = v

    def summed(read, low, n, state):
        r, p, w, m, q = (read(f, low, n) for f in (1, 3, 4, 6, 7))
        return tuple(
            s + jnp.sum(t, axis=0) for s, t in zip(state, (r * p, w * p, w * m, q * m))
        )

    STEP = 4

    WIDE = 2 * GROUP

    def own_coefficients(i, state):
        low = HALO + i * WIDE
        coefficients(low, WIDE, False)
        coef[0, pl.ds(low, WIDE)] = 0.5 * (
            field[0, pl.ds(low, WIDE)] + field[0, pl.ds(low + 1, WIDE)]
        )
        return state

    lax.fori_loop(0, rows // WIDE, own_coefficients, 0)

    def own_image(j, state):
        images([(main, main_k, HALO + low, STEP, main_put) for low in range(0, rows, STEP)], j)
        return state

    lax.fori_loop(0, 6, own_image, 0)
    zero = jnp.zeros((levels, cols), jnp.float32)
    acc = lax.fori_loop(
        0, (rows - 2 * HALO) // STEP,
        lambda i, state: summed(main, 2 * HALO + i * STEP, STEP, state), (zero,) * 4,
    )

    for index in range(len(relays) - 1):
        relay_wait(index)
        relay(index + 1)
    for way in range(8):
        dx, dy = WAYS[way]

        @pl.when(exists(-dx, -dy))
        def _():
            for copy in halo_copies(way):
                copy.wait_recv()

    def halo_of(a, state):
        field[a, 0:HALO] = jnp.transpose(x_in[a, 0], (1, 0, 2))[GROUP - HALO : GROUP]
        field[a, HALO + rows : HALO + rows + HALO] = jnp.transpose(x_in[a, 1], (1, 0, 2))[0:HALO]
        for side in range(2):
            edge = (0, LANES) if side == 0 else (last, cols)
            blocks = []
            for g, (row, slot) in ((0, (0, GROUP - HALO)), (groups - 1, (HALO + rows, 0))):
                low = width * g + HALO * (1 - side)
                block = field[a, row : row + HALO, :, edge[0] : edge[1]]
                blocks.append((low, slot, rolled(block, low + 2 * HALO * side)))
            for i in range(GROUP):
                out = sfield[a, side, 1 + i]
                for low, slot, moved in blocks:
                    if 0 <= i - slot < HALO:
                        out = jnp.where((lane >= low) & (lane < low + 2 * HALO), moved[i - slot], out)
                for g in range(groups):
                    if g == 0:
                        if i < GROUP - HALO:
                            continue
                        tile = corner_in[3 - side]
                    elif g == groups - 1:
                        if i >= HALO:
                            continue
                        tile = corner_in[1 - side]
                    else:
                        tile = side_in[1 - side, g - 1]
                    low = width * g + 2 * HALO * side
                    by = low - i * STRIP - (STRIP - HALO) * (1 - side)
                    moved = rolled(tile, by - a * (GROUP * STRIP))
                    out = jnp.where((lane >= low) & (lane < low + HALO), moved, out)
                sfield[a, side, 1 + i] = out
            wrap(a, side)
        return state

    for a in range(2):
        halo_of(a, 0)

    def edges(i, state):
        low = 1 + i * (HALO + rows - 2)
        coefficients(low, HALO, True)
        first = low - 1 + i
        coef[0, pl.ds(first, HALO)] = faces(
            field[0, pl.ds(first, HALO)], field[0, pl.ds(first + 1, HALO)]
        )
        return state

    for i in range(2):
        edges(i, 0)
        strip_coefficients(i, 0)

    PART = 3
    HALF = GROUP // 2

    def strip_job(side, low):
        def read(f, at, n):
            if at == 0:
                first = rolled(sfield[f, side, pl.ds(GROUP, 1)], width)
                return jnp.concatenate([first, sfield[f, side, pl.ds(1, n - 1)]], axis=0)
            if at + n == GROUP + 2:
                last_row = rolled(sfield[f, side, pl.ds(1, 1)], -width)
                return jnp.concatenate([sfield[f, side, pl.ds(at, n - 1)], last_row], axis=0)
            return sfield[f, side, pl.ds(at, n)]

        def k(i, at, n):
            return scoef[i, side, pl.ds(at, n)]

        def put(f, at, n, v):
            sfield[f, side, pl.ds(at, n)] = v

        return read, k, low, HALF, put

    def edge_image(j):
        jobs = []
        for base in (j + 1, rows - 1 - j + HALO):
            jobs += [(main, main_k, low, PART, main_put) for low in (base, base + PART)]
        strips = [strip_job(side, low) for side in range(2) for low in (1, 1 + HALF)]
        images(jobs + strips, j)

    for j in range(6):
        edge_image(j)
    for base in (HALO, rows):
        for low in (base, base + PART):
            acc = summed(main, low, PART, acc)
    sacc = (jnp.zeros((levels, LANES), jnp.float32),) * 4
    for side in range(2):
        sacc = summed(lambda f, low, n: sfield[f, side, pl.ds(low, n)], 1, GROUP, sacc)

    in_strip = jnp.zeros((levels, LANES), jnp.bool_)
    for g in range(1, tiles + 1):
        low = width * g + HALO
        in_strip = jnp.logical_or(in_strip, (lane >= low) & (lane < low + HALO))
    message = jnp.zeros((levels, LANES), jnp.float32)
    share = LANES // 4
    for i in range(4):
        s = jnp.where(in_strip, sacc[i], 0.0)
        for low in range(0, cols, LANES):
            part = acc[i][:, low : low + LANES]
            if low == 0:
                part = jnp.where(lane >= HALO, part, 0.0)
            if low == last:
                part = jnp.where(lane < LANES - HALO, part, 0.0)
            s = s + part
        s = s + rolled(s, 2 * share)
        s = s + rolled(s, share)
        message = jnp.where((lane >= i * share) & (lane < (i + 1) * share), s, message)
    total = jnp.sum(message, axis=0, keepdims=True)

    def finish(t, state):
        low = pl.multiple_of(t * GROUP, GROUP)
        for f, out in ((3, p_out), (4, w_out), (6, m_out), (7, n_out)):
            block = field[f, pl.ds(HALO + low, GROUP)]
            parts = [block[:, :, k : k + LANES] for k in range(0, cols, LANES)]
            for side in range(2):
                strip = sfield[f, side, 1 : 1 + GROUP]
                to = 0 if side == 0 else LANES - HALO
                part = 0 if side == 0 else len(parts) - 1
                by = lax.rem(to - HALO - width + 2 * LANES - width * t, LANES)
                parts[part] = jnp.where(
                    between(to, to + HALO, strip.shape), rolled(strip, by), parts[part]
                )
            for k, part in enumerate(parts):
                out[:, pl.ds(low, GROUP), k * LANES : (k + 1) * LANES] = jnp.transpose(
                    part, (1, 0, 2)
                )
        return state

    if relays:
        relay_wait(len(relays) - 1)
    base = 0
    sent = []
    for index, stage in enumerate(stages):
        count = stage[0] * stage[1]
        mine = base + place_in(stage)[0]
        slots[pl.ds(mine, 1), :] = total

        def send(device):
            pltpu.make_async_remote_copy(
                src_ref=slots.at[pl.ds(mine, 1)], dst_ref=slots.at[pl.ds(mine, 1)],
                send_sem=red_send.at[index], recv_sem=red_recv.at[index],
                device_id=device, device_id_type=LOGICAL,
            ).start()

        each_other(stage, send)
        if index == 0:
            lax.fori_loop(0, tiles, finish, 0)
            r_out[...] = fresh[1]
            for way in range(8):

                @pl.when(exists(*WAYS[way]))
                def _():
                    for copy in halo_copies(way):
                        copy.wait_send()

        if count > 1:
            whole = slots.at[pl.ds(base, count - 1)]
            pltpu.make_async_copy(whole, whole, red_recv.at[index]).wait()
            sent.append((whole, red_send.at[index]))
        total = jnp.sum(slots[base : base + count], axis=0, keepdims=True)
        base += -(-count // 8) * 8
    sums_out[...] = total
    for whole, sem in sent:
        pltpu.make_async_copy(whole, whole, sem).wait()


def combine(p, w, m, n, r, sums, x_hbm, res_hbm, x_vmem, res_vmem, sem):
    levels = p.shape[0]
    total = sums[...]
    lane = lax.broadcasted_iota(jnp.int32, total.shape, 1)
    share = LANES // 4

    def of(i, scale):
        chosen = (lane >= i * share) & (lane < (i + 1) * share)
        return scale * jnp.sum(jnp.where(chosen, total, 0.0), axis=1, keepdims=True)

    rp, wp, wm, nm = (of(i, power_2 ** (i + 1)) for i in range(4))
    gamma_old = rp
    alpha_old = gamma_old / wp
    gamma = (rp - alpha_old * wp) - alpha_old * (wp - alpha_old * wm)
    delta = (wp - alpha_old * wm) - alpha_old * (wm - alpha_old * nm)
    beta = gamma / gamma_old
    alpha = gamma / (delta - beta * gamma / alpha_old)
    near = power_2 * (alpha_old + alpha * (1.0 + beta))
    far = (power_2 * power_2) * (alpha * alpha_old)
    copies = []
    for z in range(levels):
        x_vmem[z] = near * p[z] - far * m[z]
        res_vmem[z] = (r[z] - near * w[z]) + far * n[z]
        for a, (one, two) in enumerate(((x_vmem, x_hbm), (res_vmem, res_hbm))):
            copies.append(pltpu.make_async_copy(one.at[z], two.at[z], sem.at[a, z]))
            copies[-1].start()
    for copy in copies:
        copy.wait()


def solution(mesh):
    num_x, num_y = mesh.shape["gx"], mesh.shape["gy"]

    def per_device(right_side, conductivity):
        levels, rows, cols = right_side.shape
        high = rows + 2 * HALO
        tiles = rows // GROUP
        stages = stages_of(num_x, num_y)
        deep = sum(-(-(a * b) // 8) * 8 for a, b in stages)

        def body(*refs):
            kernel(num_x, num_y, *refs)

        block = (levels, rows, cols)
        full = (high, levels, cols)
        slim = (2, GROUP + 2, levels, LANES)
        out = jax.ShapeDtypeStruct(block, jnp.float32)
        sums = jax.ShapeDtypeStruct((1, LANES), jnp.float32)
        vmem = lambda shape: pltpu.VMEM(shape, jnp.float32)
        dma = lambda *n: pltpu.SemaphoreType.DMA(n)
        in_vmem = pl.BlockSpec(memory_space=pltpu.VMEM)
        in_hbm = pl.BlockSpec(memory_space=pltpu.HBM)
        parts = pl.pallas_call(
            body,
            out_shape=(out,) * 5 + (sums,),
            in_specs=[in_hbm] * 2,
            out_specs=(in_vmem,) * 6,
            scratch_shapes=[
                vmem((2,) + block), vmem((2, 2, levels, GROUP, cols)),
                vmem((6,) + full), vmem((6,) + slim), vmem((8,) + full), vmem((8,) + slim),
                vmem((2, tiles, levels, LANES)), vmem((2, tiles, levels, LANES)),
                vmem((4, levels, LANES)), vmem((deep, LANES)),
                dma(2), dma(8, 2), dma(8, 2), dma(len(stages)), dma(len(stages)),
                pltpu.SemaphoreType.REGULAR((8,)),
            ],
            compiler_params=pltpu.CompilerParams(
                collective_id=0, has_side_effects=True, vmem_limit_bytes=55000000
            ),
        )(right_side, conductivity)
        return pl.pallas_call(
            combine,
            out_shape=(out, out),
            in_specs=[in_vmem] * 6,
            out_specs=(in_hbm,) * 2,
            scratch_shapes=[vmem(block), vmem(block), dma(2, levels)],
            compiler_params=pltpu.CompilerParams(vmem_limit_bytes=4000000),
        )(*parts)

    return jax.shard_map(
        per_device,
        mesh=mesh,
        in_specs=(P(None, "gx", "gy"), P(None, "gx", "gy")),
        out_specs=(P(None, "gx", "gy"), P(None, "gx", "gy")),
        check_vma=False,
    )
```

```python
import jax
import jax.numpy as jnp
from jax import lax
from jax.experimental import pallas as pl
from jax.experimental.pallas import tpu as pltpu
from jax.sharding import PartitionSpec as P

low_bound = 0.4
high_bound = 12.0
cheb_theta = 0.5 * (high_bound + low_bound)
cheb_delta = 0.5 * (high_bound - low_bound)
cheb_sigma = cheb_theta / cheb_delta
rho_first = 1.0 / cheb_sigma
rho_second = 1.0 / (2.0 * cheb_sigma - rho_first)
rho_third = 1.0 / (2.0 * cheb_sigma - rho_second)

step_0 = rho_second * rho_first / cheb_theta + 2.0 * rho_second / cheb_delta
step_1 = 2.0 * rho_second / cheb_delta / cheb_theta
mix_0 = 1.0 + rho_third * rho_second
mix_1 = 2.0 * rho_third / cheb_delta
power_0 = 1.0 / cheb_theta + mix_0 * step_0 + mix_1
power_1 = -mix_0 * step_1 - mix_1 / cheb_theta - mix_1 * step_0
power_2 = mix_1 * step_1
shift_1 = power_1 / power_2
shift_0 = power_0 / power_2

HALO = 6
AHEAD = 2
PLANE = 2
LANES = 128
STRIP = 8
GROUP = 8
ONE_STAGE = 64
MESH = pl.DeviceIdType.MESH
LOGICAL = pl.DeviceIdType.LOGICAL
WAYS = ((-1, 0), (1, 0), (0, -1), (0, 1), (-1, -1), (-1, 1), (1, -1), (1, 1))


def stages_of(num_x, num_y):
    if num_x * num_y <= ONE_STAGE:
        return ((num_x, num_y),)
    return ((num_x, 1), (1, num_y))


def kernel(
    num_x, num_y, r_hbm, c_hbm, p_out, w_out, m_out, n_out, r_out, sums_out,
    fresh, x_in, coef, scoef, field, sfield, packed, side_in, corner_in, slots,
    in_sem, halo_send, halo_recv, red_send, red_recv, relayed,
):
    _, levels, rows, cols = fresh.shape
    tiles = rows // GROUP
    groups = tiles + 2
    width = LANES // groups
    last = cols - LANES
    me_x = lax.axis_index("gx")
    me_y = lax.axis_index("gy")
    stages = stages_of(num_x, num_y)

    def exists(dx, dy):
        ok = jnp.bool_(True)
        if dx < 0:
            ok = me_x > 0
        if dx > 0:
            ok = me_x < num_x - 1
        if dy < 0:
            ok_y = me_y > 0
            ok = ok_y if dx == 0 else jnp.logical_and(ok, ok_y)
        if dy > 0:
            ok_y = me_y < num_y - 1
            ok = ok_y if dx == 0 else jnp.logical_and(ok, ok_y)
        return ok

    loads = [
        pltpu.make_async_copy(ref, fresh.at[a], in_sem.at[a])
        for a, ref in enumerate((c_hbm, r_hbm))
    ]
    for load in loads:
        load.start()

    def place_in(stage):
        count_x, count_y = stage
        if count_x > 1 and count_y > 1:
            return me_x * num_y + me_y, lambda o: o
        if count_x > 1:
            return me_x, lambda o: o * num_y + me_y
        return me_y, lambda o: me_x * num_y + o

    def each_other(stage, act):
        mine, device = place_in(stage)
        total = stage[0] * stage[1]

        flip = mine < total // 2
        start_at = jnp.where(flip, total - 1 - mine, mine)

        def step(k, state):
            other = jnp.where(k > start_at, k, k - 1)
            act(device(jnp.where(flip, total - 1 - other, other)))
            return state

        lax.fori_loop(1, total, step, 0)

    barrier = pltpu.get_barrier_semaphore()

    def greet(device):
        pl.semaphore_signal(barrier, inc=1, device_id=device, device_id_type=LOGICAL)

    planes = len(stages) == 1 and num_x % PLANE == 0
    plane = me_x // PLANE * PLANE
    expected = jnp.int32(0)
    if planes:
        mine = me_x * num_y + me_y
        begin = me_x == plane

        for dy in (0, -1, 1):
            down = jnp.logical_and(begin, exists(-1, dy))
            up = jnp.logical_and(me_x == plane + PLANE - 1, exists(1, dy))

            @pl.when(down)
            def _():
                greet(mine - num_y + dy)

            expected = expected + up.astype(jnp.int32)

        def onward(other, state):
            @pl.when(other != mine)
            def _():
                greet(other)

            return state

        lax.fori_loop(plane * num_y, num_x * num_y, onward, 0)
        expected = expected + ((plane + PLANE) * num_y - 1)
    else:
        for stage in stages:
            each_other(stage, greet)
            expected = expected + (stage[0] * stage[1] - 1)
    if len(stages) > 1:
        for dx, dy in WAYS[4:]:
            ok = exists(dx, dy)

            @pl.when(ok)
            def _():
                greet((me_x + dx) * num_y + me_y + dy)

            expected = expected + ok.astype(jnp.int32)

    def relay():
        def tell(k, state):
            pl.semaphore_signal(
                relayed, inc=1, device_id=(me_x - k * PLANE) * num_y + me_y, device_id_type=LOGICAL
            )
            return state

        lax.fori_loop(1, me_x // PLANE + 1, tell, 0)

    def relay_wait():
        @pl.when(me_x < num_x - PLANE)
        def _():
            pl.semaphore_wait(relayed, (num_x - 1 - me_x) // PLANE)

    def halo_copies(way):
        dx, dy = WAYS[way]
        if dy == 0:
            side = 1 if dx < 0 else 0
            low = 0 if dx < 0 else rows - HALO
            land = 0 if dx < 0 else GROUP - HALO
            pairs = [
                (ref.at[:, pl.ds(low, HALO)], x_in.at[a, side, :, pl.ds(land, HALO)])
                for a, ref in enumerate((c_hbm, r_hbm))
            ]
        elif dx == 0:
            pairs = [(packed.at[0 if dy < 0 else 1], side_in.at[0 if dy < 0 else 1])]
        else:
            pairs = [(
                packed.at[0 if dy < 0 else 1, 0 if dx < 0 else tiles - 1],
                corner_in.at[way - 4],
            )]
        return [
            pltpu.make_async_remote_copy(
                src_ref=one, dst_ref=two,
                send_sem=halo_send.at[way, a], recv_sem=halo_recv.at[way, a],
                device_id=(me_x + dx, me_y + dy), device_id_type=MESH,
            )
            for a, (one, two) in enumerate(pairs)
        ]

    def start(way):
        @pl.when(exists(*WAYS[way]))
        def _():
            for copy in halo_copies(way):
                copy.start()


    lane = lax.broadcasted_iota(jnp.int32, (levels, LANES), 1)

    def between(low, high, like):
        at = lax.broadcasted_iota(jnp.int32, (1,) * (len(like) - 1) + (LANES,), len(like) - 1)
        return (at >= low) & (at < high)

    def rolled(v, by):
        if isinstance(by, int):
            by = by % v.shape[-1]
            if by == 0:
                return v
        return pltpu.roll(v, by, v.ndim - 1)

    for load in loads:
        load.wait()

    def arrange(t):
        low = t * GROUP
        acc = [jnp.zeros((levels, LANES), jnp.float32)] * 2
        for a in range(2):
            block = jnp.transpose(fresh[a, :, low : low + GROUP, :], (1, 0, 2))
            field[a, HALO + low : HALO + low + GROUP] = block
            for side in range(2):
                offset = 0 if side == 0 else LANES - STRIP
                part = block[:, :, (0 if side == 0 else last) : (LANES if side == 0 else cols)]
                for g in range(GROUP):
                    place = (a * GROUP + g) * STRIP
                    moved = rolled(part[g], place - offset)
                    acc[side] = jnp.where(
                        (lane >= place) & (lane < place + STRIP), moved, acc[side]
                    )
        for side in range(2):
            packed[side, t] = acc[side]

    for t in sorted({0, tiles - 1}):
        arrange(t)
    pl.semaphore_wait(barrier, expected)
    for way in (4, 5, 6, 7, 0, 1):
        start(way)
    for t in range(1, tiles - 1):
        arrange(t)
    for way in (2, 3):
        start(way)
    if planes:
        relay()

    for way in range(8):
        dx, dy = WAYS[way]

        @pl.when(jnp.logical_not(exists(-dx, -dy)))
        def _():
            if dy == 0:
                x_in[:, 1 if dx < 0 else 0] = jnp.zeros((2, levels, GROUP, cols), jnp.float32)
            elif dx == 0:
                side_in[0 if dy < 0 else 1] = jnp.zeros((tiles, levels, LANES), jnp.float32)
            else:
                corner_in[way - 4] = jnp.zeros((levels, LANES), jnp.float32)

    def own_strips(a, state):
        for side in range(2):
            acc = jnp.zeros((GROUP, levels, LANES), jnp.float32)
            for g in range(1, tiles + 1):
                low = width * g + HALO * (1 - side)
                block = field[
                    a, HALO + (g - 1) * GROUP : HALO + g * GROUP, :,
                    (0 if side == 0 else last) : (LANES if side == 0 else cols),
                ]
                moved = rolled(block, low + 2 * HALO * side)
                acc = jnp.where(between(low, low + 2 * HALO, block.shape), moved, acc)
            sfield[a, side, 1 : 1 + GROUP] = acc
        return state

    lax.fori_loop(0, 2, own_strips, 0)

    def wrap(f, side):
        sfield[f, side, 0] = rolled(sfield[f, side, GROUP], width)
        sfield[f, side, GROUP + 1] = rolled(sfield[f, side, 1], -width)

    def level_of(shape):
        return lax.broadcasted_iota(jnp.int32, (1, levels, shape[-1]), 1)

    def faces(c, other):
        return jnp.where(jnp.minimum(c, other) > 0.0, 0.5 * (c + other), 0.0)

    def coefficients(low, n, beside):
        c = field[0, pl.ds(low, n)]
        level = level_of(c.shape)
        at = lax.broadcasted_iota(jnp.int32, (1, 1, cols), 2)
        half = 0.5 * c
        inner = jnp.logical_and(level > 0, level < levels - 1)
        kb = jnp.where(inner, 0.0, half)
        if beside:
            for other in (field[0, pl.ds(low - 1, n)], field[0, pl.ds(low + 1, n)]):
                kb = kb + jnp.where(other > 0.0, 0.0, half)
        coef[1, pl.ds(low, n)] = jnp.where(at < cols - 1, half + rolled(half, cols - 1), 0.0)
        coef[5, pl.ds(low, n)] = jnp.where(at > 0, half + rolled(half, 1), 0.0)
        coef[2, pl.ds(low, n)] = jnp.where(
            level < levels - 1, half + pltpu.roll(half, levels - 1, 1), 0.0
        )
        coef[3, pl.ds(low, n)] = kb
        coef[4, pl.ds(low, n)] = kb + shift_1

    def strip_coefficients(side):
        c = sfield[0, side, 1 : 1 + GROUP]
        level = level_of(c.shape)
        half = 0.5 * c
        inner = jnp.logical_and(level > 0, level < levels - 1)
        east, west = rolled(c, LANES - 1), rolled(c, 1)
        kb = jnp.where(inner, 0.0, half)
        for other in (east, west, sfield[0, side, 0:GROUP], sfield[0, side, 2 : 2 + GROUP]):
            kb = kb + jnp.where(other > 0.0, 0.0, half)
        scoef[0, side, 0 : GROUP + 1] = faces(
            sfield[0, side, 0 : GROUP + 1], sfield[0, side, 1 : GROUP + 2]
        )
        scoef[1, side, 1 : 1 + GROUP] = faces(c, east)
        scoef[5, side, 1 : 1 + GROUP] = faces(c, west)
        scoef[2, side, 1 : 1 + GROUP] = jnp.where(
            level < levels - 1, half + pltpu.roll(half, levels - 1, 1), 0.0
        )
        scoef[3, side, 1 : 1 + GROUP] = kb
        scoef[4, side, 1 : 1 + GROUP] = kb + shift_1

    def turned(read, low, n, j):
        v = read(j + 1, low, n)
        down, up = read(j + 1, low - 1, n), read(j + 1, low + 1, n)
        return v, rolled(v, v.shape[-1] - 1), rolled(v, 1), down, up

    def image(read, k, low, n, j, around):
        third = j % 3 if isinstance(j, int) else lax.rem(j, 3)
        shifted = 4 - (third + 1) // 2
        v, east, west, down, up = around
        axis = v.ndim - 1
        across = k(0, low, n) * (v - up)
        back = k(0, low - 1, n) * (down - v)
        fz = k(2, low, n) * (v - pltpu.roll(v, levels - 1, axis - 1))
        rest = (across - back) + ((fz - pltpu.roll(fz, 1, axis - 1)) + k(shifted, low, n) * v)
        if not isinstance(j, int):
            also = jnp.where(third == 1, shift_0, 0.0)
            rest = rest + also * read(jnp.maximum(j, 1), low, n)
        elif third == 1:
            rest = rest + shift_0 * read(j, low, n)
        return rest + (k(1, low, n) * (v - east) + k(5, low, n) * (v - west))

    def images(jobs, j):
        ahead = AHEAD
        around = [turned(read, low, n, j) for read, k, low, n, put in jobs[:ahead]]
        for i, (read, k, low, n, put) in enumerate(jobs):
            if i + ahead < len(jobs):
                other = jobs[i + ahead]
                around.append(turned(other[0], other[2], other[3], j))
            put(j + 2, low, n, image(read, k, low, n, j, around[i]))

    def main(f, low, n):
        return field[f, pl.ds(low, n)]

    def main_k(i, low, n):
        return coef[i, pl.ds(low, n)]

    def main_put(f, low, n, v):
        field[f, pl.ds(low, n)] = v

    def summed(read, low, n, state):
        r, p, w, m, q = (read(f, low, n) for f in (1, 3, 4, 6, 7))
        return tuple(
            s + jnp.sum(t, axis=0) for s, t in zip(state, (r * p, w * p, w * m, q * m))
        )

    STEP = 4

    WIDE = 2 * GROUP

    def own_coefficients(i, state):
        low = HALO + i * WIDE
        coefficients(low, WIDE, False)
        coef[0, pl.ds(low, WIDE)] = 0.5 * (
            field[0, pl.ds(low, WIDE)] + field[0, pl.ds(low + 1, WIDE)]
        )
        return state

    lax.fori_loop(0, rows // WIDE, own_coefficients, 0)

    def own_image(j, state):
        images([(main, main_k, HALO + low, STEP, main_put) for low in range(0, rows, STEP)], j)
        return state

    lax.fori_loop(0, 6, own_image, 0)
    zero = jnp.zeros((levels, cols), jnp.float32)
    acc = lax.fori_loop(
        0, (rows - 2 * HALO) // STEP,
        lambda i, state: summed(main, 2 * HALO + i * STEP, STEP, state), (zero,) * 4,
    )


    def arrived(ways):
        for way in ways:
            dx, dy = WAYS[way]

            @pl.when(exists(-dx, -dy))
            def _():
                for copy in halo_copies(way):
                    copy.wait_recv()

    arrived((2, 3, 4, 5, 6, 7))
    for a in range(2):
        for side in range(2):
            for i in range(GROUP):
                out = sfield[a, side, 1 + i]
                for g in range(groups):
                    if g == 0:
                        if i < GROUP - HALO:
                            continue
                        tile = corner_in[3 - side]
                    elif g == groups - 1:
                        if i >= HALO:
                            continue
                        tile = corner_in[1 - side]
                    else:
                        tile = side_in[1 - side, g - 1]
                    low = width * g + 2 * HALO * side
                    by = low - i * STRIP - (STRIP - HALO) * (1 - side)
                    moved = rolled(tile, by - a * (GROUP * STRIP))
                    out = jnp.where((lane >= low) & (lane < low + HALO), moved, out)
                sfield[a, side, 1 + i] = out

    arrived((0, 1))
    for a in range(2):
        lower = jnp.transpose(x_in[a, 0], (1, 0, 2))[GROUP - HALO : GROUP]
        upper = jnp.transpose(x_in[a, 1], (1, 0, 2))[0:HALO]
        field[a, 0:HALO] = lower
        field[a, HALO + rows : HALO + rows + HALO] = upper
        for side in range(2):
            edge = (0, LANES) if side == 0 else (last, cols)
            for g, block, slot in ((0, lower, GROUP - HALO), (groups - 1, upper, 0)):
                low = width * g + HALO * (1 - side)
                moved = rolled(block[:, :, edge[0] : edge[1]], low + 2 * HALO * side)
                slots_of = pl.ds(1 + slot, HALO)
                sfield[a, side, slots_of] = jnp.where(
                    between(low, low + 2 * HALO, moved.shape), moved, sfield[a, side, slots_of]
                )
            wrap(a, side)

    def edges(i):
        low = 1 + i * (HALO + rows - 2)
        coefficients(low, HALO, True)
        first = low - 1 + i
        coef[0, pl.ds(first, HALO)] = faces(
            field[0, pl.ds(first, HALO)], field[0, pl.ds(first + 1, HALO)]
        )

    for i in range(2):
        edges(i)
    for side in range(2):
        strip_coefficients(side)

    PART = 3
    HALF = GROUP // 2

    def strip_job(side, low):
        def read(f, at, n):
            if at == 0:
                first = rolled(sfield[f, side, pl.ds(GROUP, 1)], width)
                return jnp.concatenate([first, sfield[f, side, pl.ds(1, n - 1)]], axis=0)
            if at + n == GROUP + 2:
                last_row = rolled(sfield[f, side, pl.ds(1, 1)], -width)
                return jnp.concatenate([sfield[f, side, pl.ds(at, n - 1)], last_row], axis=0)
            return sfield[f, side, pl.ds(at, n)]

        def k(i, at, n):
            return scoef[i, side, pl.ds(at, n)]

        def put(f, at, n, v):
            sfield[f, side, pl.ds(at, n)] = v

        return read, k, low, HALF, put

    def edge_image(j):
        jobs = []
        for base in (j + 1, rows - 1 - j + HALO):
            jobs += [(main, main_k, low, PART, main_put) for low in (base, base + PART)]
        strips = [strip_job(side, low) for side in range(2) for low in (1, 1 + HALF)]
        images(jobs + strips, j)

    for j in range(6):
        edge_image(j)
    for base in (HALO, rows):
        for low in (base, base + PART):
            acc = summed(main, low, PART, acc)
    sacc = (jnp.zeros((levels, LANES), jnp.float32),) * 4
    for side in range(2):
        sacc = summed(lambda f, low, n: sfield[f, side, pl.ds(low, n)], 1, GROUP, sacc)

    in_strip = jnp.zeros((levels, LANES), jnp.bool_)
    for g in range(1, tiles + 1):
        low = width * g + HALO
        in_strip = jnp.logical_or(in_strip, (lane >= low) & (lane < low + HALO))
    message = jnp.zeros((levels, LANES), jnp.float32)
    share = LANES // 4
    for i in range(4):
        s = jnp.where(in_strip, sacc[i], 0.0)
        for low in range(0, cols, LANES):
            part = acc[i][:, low : low + LANES]
            if low == 0:
                part = jnp.where(lane >= HALO, part, 0.0)
            if low == last:
                part = jnp.where(lane < LANES - HALO, part, 0.0)
            s = s + part
        s = s + rolled(s, 2 * share)
        s = s + rolled(s, share)
        message = jnp.where((lane >= i * share) & (lane < (i + 1) * share), s, message)
    total = jnp.sum(message, axis=0, keepdims=True)

    def finish(t, state):
        low = pl.multiple_of(t * GROUP, GROUP)
        for f, out in ((3, p_out), (4, w_out), (6, m_out), (7, n_out)):
            block = field[f, pl.ds(HALO + low, GROUP)]
            parts = [block[:, :, k : k + LANES] for k in range(0, cols, LANES)]
            for side in range(2):
                strip = sfield[f, side, 1 : 1 + GROUP]
                to = 0 if side == 0 else LANES - HALO
                part = 0 if side == 0 else len(parts) - 1
                by = lax.rem(to - HALO - width + 2 * LANES - width * t, LANES)
                parts[part] = jnp.where(
                    between(to, to + HALO, strip.shape), rolled(strip, by), parts[part]
                )
            for k, part in enumerate(parts):
                out[:, pl.ds(low, GROUP), k * LANES : (k + 1) * LANES] = jnp.transpose(
                    part, (1, 0, 2)
                )
        return state

    if planes:
        relay_wait()
    base = 0
    sent = []
    for index, stage in enumerate(stages):
        count = stage[0] * stage[1]
        mine = base + place_in(stage)[0]
        slots[pl.ds(mine, 1), :] = total

        def send(device):
            pltpu.make_async_remote_copy(
                src_ref=slots.at[pl.ds(mine, 1)], dst_ref=slots.at[pl.ds(mine, 1)],
                send_sem=red_send.at[index], recv_sem=red_recv.at[index],
                device_id=device, device_id_type=LOGICAL,
            ).start()

        each_other(stage, send)
        if index == 0:
            lax.fori_loop(0, tiles, finish, 0)
            r_out[...] = fresh[1]
            for way in range(8):

                @pl.when(exists(*WAYS[way]))
                def _():
                    for copy in halo_copies(way):
                        copy.wait_send()

        if count > 1:
            whole = slots.at[pl.ds(base, count - 1)]
            pltpu.make_async_copy(whole, whole, red_recv.at[index]).wait()
            sent.append((whole, red_send.at[index]))
        total = jnp.sum(slots[base : base + count], axis=0, keepdims=True)
        base += -(-count // 8) * 8
    sums_out[...] = total
    for whole, sem in sent:
        pltpu.make_async_copy(whole, whole, sem).wait()


def combine(p, w, m, n, r, sums, x_hbm, res_hbm, x_vmem, res_vmem, sem):
    levels = p.shape[0]
    total = sums[...]
    lane = lax.broadcasted_iota(jnp.int32, total.shape, 1)
    share = LANES // 4

    def of(i, scale):
        chosen = (lane >= i * share) & (lane < (i + 1) * share)
        return scale * jnp.sum(jnp.where(chosen, total, 0.0), axis=1, keepdims=True)

    rp, wp, wm, nm = (of(i, power_2 ** (i + 1)) for i in range(4))
    gamma_old = rp
    alpha_old = gamma_old / wp
    gamma = (rp - alpha_old * wp) - alpha_old * (wp - alpha_old * wm)
    delta = (wp - alpha_old * wm) - alpha_old * (wm - alpha_old * nm)
    beta = gamma / gamma_old
    alpha = gamma / (delta - beta * gamma / alpha_old)
    near = power_2 * (alpha_old + alpha * (1.0 + beta))
    far = (power_2 * power_2) * (alpha * alpha_old)
    copies = []
    for z in range(levels):
        x_vmem[z] = near * p[z] - far * m[z]
        res_vmem[z] = (r[z] - near * w[z]) + far * n[z]
        for a, (one, two) in enumerate(((x_vmem, x_hbm), (res_vmem, res_hbm))):
            copies.append(pltpu.make_async_copy(one.at[z], two.at[z], sem.at[a, z]))
            copies[-1].start()
    for copy in copies:
        copy.wait()


def solution(mesh):
    num_x, num_y = mesh.shape["gx"], mesh.shape["gy"]

    def per_device(right_side, conductivity):
        levels, rows, cols = right_side.shape
        high = rows + 2 * HALO
        tiles = rows // GROUP
        stages = stages_of(num_x, num_y)
        deep = sum(-(-(a * b) // 8) * 8 for a, b in stages)

        def body(*refs):
            kernel(num_x, num_y, *refs)

        block = (levels, rows, cols)
        full = (high, levels, cols)
        slim = (2, GROUP + 2, levels, LANES)
        out = jax.ShapeDtypeStruct(block, jnp.float32)
        sums = jax.ShapeDtypeStruct((1, LANES), jnp.float32)
        vmem = lambda shape: pltpu.VMEM(shape, jnp.float32)
        dma = lambda *n: pltpu.SemaphoreType.DMA(n)
        in_vmem = pl.BlockSpec(memory_space=pltpu.VMEM)
        in_hbm = pl.BlockSpec(memory_space=pltpu.HBM)
        parts = pl.pallas_call(
            body,
            out_shape=(out,) * 5 + (sums,),
            in_specs=[in_hbm] * 2,
            out_specs=(in_vmem,) * 6,
            scratch_shapes=[
                vmem((2,) + block), vmem((2, 2, levels, GROUP, cols)),
                vmem((6,) + full), vmem((6,) + slim), vmem((8,) + full), vmem((8,) + slim),
                vmem((2, tiles, levels, LANES)), vmem((2, tiles, levels, LANES)),
                vmem((4, levels, LANES)), vmem((deep, LANES)),
                dma(2), dma(8, 2), dma(8, 2), dma(len(stages)), dma(len(stages)),
                pltpu.SemaphoreType.REGULAR,
            ],
            compiler_params=pltpu.CompilerParams(
                collective_id=0, has_side_effects=True, vmem_limit_bytes=55000000
            ),
        )(right_side, conductivity)
        return pl.pallas_call(
            combine,
            out_shape=(out, out),
            in_specs=[in_vmem] * 6,
            out_specs=(in_hbm,) * 2,
            scratch_shapes=[vmem(block), vmem(block), dma(2, levels)],
            compiler_params=pltpu.CompilerParams(vmem_limit_bytes=4000000),
        )(*parts)

    return jax.shard_map(
        per_device,
        mesh=mesh,
        in_specs=(P(None, "gx", "gy"), P(None, "gx", "gy")),
        out_specs=(P(None, "gx", "gy"), P(None, "gx", "gy")),
        check_vma=False,
    )
```

```python
import jax
import jax.numpy as jnp
from jax import lax
from jax.experimental import pallas as pl
from jax.experimental.pallas import tpu as pltpu
from jax.sharding import PartitionSpec as P

low_bound = 0.4
high_bound = 12.0
cheb_theta = 0.5 * (high_bound + low_bound)
cheb_delta = 0.5 * (high_bound - low_bound)
cheb_sigma = cheb_theta / cheb_delta
rho_first = 1.0 / cheb_sigma
rho_second = 1.0 / (2.0 * cheb_sigma - rho_first)
rho_third = 1.0 / (2.0 * cheb_sigma - rho_second)

step_0 = rho_second * rho_first / cheb_theta + 2.0 * rho_second / cheb_delta
step_1 = 2.0 * rho_second / cheb_delta / cheb_theta
mix_0 = 1.0 + rho_third * rho_second
mix_1 = 2.0 * rho_third / cheb_delta
power_0 = 1.0 / cheb_theta + mix_0 * step_0 + mix_1
power_1 = -mix_0 * step_1 - mix_1 / cheb_theta - mix_1 * step_0
power_2 = mix_1 * step_1
shift_1 = power_1 / power_2
shift_0 = power_0 / power_2

HALO = 6
AHEAD = 2
PLANE = 2
LANES = 128
STRIP = 8
GROUP = 8
ONE_STAGE = 64
MESH = pl.DeviceIdType.MESH
LOGICAL = pl.DeviceIdType.LOGICAL
WAYS = ((-1, 0), (1, 0), (0, -1), (0, 1), (-1, -1), (-1, 1), (1, -1), (1, 1))


def stages_of(num_x, num_y):
    if num_x * num_y <= ONE_STAGE:
        return ((num_x, num_y),)
    return ((num_x, 1), (1, num_y))


def kernel(
    num_x, num_y, r_hbm, c_hbm, p_out, w_out, m_out, n_out, r_out, sums_out,
    fresh, x_in, coef, scoef, field, sfield, packed, side_in, corner_in, slots,
    in_sem, halo_send, halo_recv, red_send, red_recv, relayed,
):
    _, levels, rows, cols = fresh.shape
    tiles = rows // GROUP
    groups = tiles + 2
    width = LANES // groups
    last = cols - LANES
    me_x = lax.axis_index("gx")
    me_y = lax.axis_index("gy")
    stages = stages_of(num_x, num_y)

    def exists(dx, dy):
        ok = jnp.bool_(True)
        if dx < 0:
            ok = me_x > 0
        if dx > 0:
            ok = me_x < num_x - 1
        if dy < 0:
            ok_y = me_y > 0
            ok = ok_y if dx == 0 else jnp.logical_and(ok, ok_y)
        if dy > 0:
            ok_y = me_y < num_y - 1
            ok = ok_y if dx == 0 else jnp.logical_and(ok, ok_y)
        return ok

    loads = [
        pltpu.make_async_copy(ref, fresh.at[a], in_sem.at[a])
        for a, ref in enumerate((c_hbm, r_hbm))
    ]
    for load in loads:
        load.start()

    def place_in(stage):
        count_x, count_y = stage
        if count_x > 1 and count_y > 1:
            return me_x * num_y + me_y, lambda o: o
        if count_x > 1:
            return me_x, lambda o: o * num_y + me_y
        return me_y, lambda o: me_x * num_y + o

    def each_other(stage, act):
        mine, device = place_in(stage)
        total = stage[0] * stage[1]

        flip = mine < total // 2
        start_at = jnp.where(flip, total - 1 - mine, mine)

        def step(k, state):
            other = jnp.where(k > start_at, k, k - 1)
            act(device(jnp.where(flip, total - 1 - other, other)))
            return state

        lax.fori_loop(1, total, step, 0)

    barrier = pltpu.get_barrier_semaphore()

    def greet(device):
        pl.semaphore_signal(barrier, inc=1, device_id=device, device_id_type=LOGICAL)

    planes = len(stages) == 1 and num_x % PLANE == 0
    plane = me_x // PLANE * PLANE
    expected = jnp.int32(0)
    if planes:
        mine = me_x * num_y + me_y
        begin = me_x == plane

        for dy in (0, -1, 1):
            down = jnp.logical_and(begin, exists(-1, dy))
            up = jnp.logical_and(me_x == plane + PLANE - 1, exists(1, dy))

            @pl.when(down)
            def _():
                greet(mine - num_y + dy)

            expected = expected + up.astype(jnp.int32)

        def onward(other, state):
            @pl.when(other != mine)
            def _():
                greet(other)

            return state

        lax.fori_loop(plane * num_y, num_x * num_y, onward, 0)
        expected = expected + ((plane + PLANE) * num_y - 1)
    else:
        for stage in stages:
            each_other(stage, greet)
            expected = expected + (stage[0] * stage[1] - 1)
    if len(stages) > 1:
        for dx, dy in WAYS[4:]:
            ok = exists(dx, dy)

            @pl.when(ok)
            def _():
                greet((me_x + dx) * num_y + me_y + dy)

            expected = expected + ok.astype(jnp.int32)

    def relay():
        def tell(k, state):
            pl.semaphore_signal(
                relayed, inc=1, device_id=(me_x - k * PLANE) * num_y + me_y, device_id_type=LOGICAL
            )
            return state

        lax.fori_loop(1, me_x // PLANE + 1, tell, 0)

    def relay_wait():
        @pl.when(me_x < num_x - PLANE)
        def _():
            pl.semaphore_wait(relayed, (num_x - 1 - me_x) // PLANE)

    def halo_copies(way):
        dx, dy = WAYS[way]
        if dy == 0:
            side = 1 if dx < 0 else 0
            low = 0 if dx < 0 else rows - HALO
            land = 0 if dx < 0 else GROUP - HALO
            pairs = [
                (fresh.at[a, :, pl.ds(low, HALO)], x_in.at[a, side, :, pl.ds(land, HALO)])
                for a in range(2)
            ]
        elif dx == 0:
            pairs = [(packed.at[0 if dy < 0 else 1], side_in.at[0 if dy < 0 else 1])]
        else:
            pairs = [(
                packed.at[0 if dy < 0 else 1, 0 if dx < 0 else tiles - 1],
                corner_in.at[way - 4],
            )]
        return [
            pltpu.make_async_remote_copy(
                src_ref=one, dst_ref=two,
                send_sem=halo_send.at[way, a], recv_sem=halo_recv.at[way, a],
                device_id=(me_x + dx, me_y + dy), device_id_type=MESH,
            )
            for a, (one, two) in enumerate(pairs)
        ]

    def start(way):
        @pl.when(exists(*WAYS[way]))
        def _():
            for copy in halo_copies(way):
                copy.start()


    lane = lax.broadcasted_iota(jnp.int32, (levels, LANES), 1)

    def between(low, high, like):
        at = lax.broadcasted_iota(jnp.int32, (1,) * (len(like) - 1) + (LANES,), len(like) - 1)
        return (at >= low) & (at < high)

    def rolled(v, by):
        if isinstance(by, int):
            by = by % v.shape[-1]
            if by == 0:
                return v
        return pltpu.roll(v, by, v.ndim - 1)

    for load in loads:
        load.wait()

    def arrange(t):
        low = t * GROUP
        acc = [jnp.zeros((levels, LANES), jnp.float32)] * 2
        for a in range(2):
            block = jnp.transpose(fresh[a, :, low : low + GROUP, :], (1, 0, 2))
            field[a, HALO + low : HALO + low + GROUP] = block
            for side in range(2):
                offset = 0 if side == 0 else LANES - STRIP
                part = block[:, :, (0 if side == 0 else last) : (LANES if side == 0 else cols)]
                for g in range(GROUP):
                    place = (a * GROUP + g) * STRIP
                    moved = rolled(part[g], place - offset)
                    acc[side] = jnp.where(
                        (lane >= place) & (lane < place + STRIP), moved, acc[side]
                    )
        for side in range(2):
            packed[side, t] = acc[side]

    for t in sorted({0, tiles - 1}):
        arrange(t)
    pl.semaphore_wait(barrier, expected)
    for way in (4, 5, 6, 7, 0, 1):
        start(way)
    for t in range(1, tiles - 1):
        arrange(t)
    for way in (2, 3):
        start(way)
    if planes:
        relay()

    for way in range(8):
        dx, dy = WAYS[way]

        @pl.when(jnp.logical_not(exists(-dx, -dy)))
        def _():
            if dy == 0:
                x_in[:, 1 if dx < 0 else 0] = jnp.zeros((2, levels, GROUP, cols), jnp.float32)
            elif dx == 0:
                side_in[0 if dy < 0 else 1] = jnp.zeros((tiles, levels, LANES), jnp.float32)
            else:
                corner_in[way - 4] = jnp.zeros((levels, LANES), jnp.float32)

    def own_strips(a, state):
        for side in range(2):
            acc = jnp.zeros((GROUP, levels, LANES), jnp.float32)
            for g in range(1, tiles + 1):
                low = width * g + HALO * (1 - side)
                block = field[
                    a, HALO + (g - 1) * GROUP : HALO + g * GROUP, :,
                    (0 if side == 0 else last) : (LANES if side == 0 else cols),
                ]
                moved = rolled(block, low + 2 * HALO * side)
                acc = jnp.where(between(low, low + 2 * HALO, block.shape), moved, acc)
            sfield[a, side, 1 : 1 + GROUP] = acc
        return state

    lax.fori_loop(0, 2, own_strips, 0)

    def wrap(f, side):
        sfield[f, side, 0] = rolled(sfield[f, side, GROUP], width)
        sfield[f, side, GROUP + 1] = rolled(sfield[f, side, 1], -width)

    def level_of(shape):
        return lax.broadcasted_iota(jnp.int32, (1, levels, shape[-1]), 1)

    def faces(c, other):
        return jnp.where(jnp.minimum(c, other) > 0.0, 0.5 * (c + other), 0.0)

    def coefficients(low, n, beside):
        c = field[0, pl.ds(low, n)]
        level = level_of(c.shape)
        at = lax.broadcasted_iota(jnp.int32, (1, 1, cols), 2)
        half = 0.5 * c
        inner = jnp.logical_and(level > 0, level < levels - 1)
        kb = jnp.where(inner, 0.0, half)
        if beside:
            for other in (field[0, pl.ds(low - 1, n)], field[0, pl.ds(low + 1, n)]):
                kb = kb + jnp.where(other > 0.0, 0.0, half)
        coef[1, pl.ds(low, n)] = jnp.where(at < cols - 1, half + rolled(half, cols - 1), 0.0)
        coef[5, pl.ds(low, n)] = jnp.where(at > 0, half + rolled(half, 1), 0.0)
        coef[2, pl.ds(low, n)] = jnp.where(
            level < levels - 1, half + pltpu.roll(half, levels - 1, 1), 0.0
        )
        coef[3, pl.ds(low, n)] = kb
        coef[4, pl.ds(low, n)] = kb + shift_1

    def strip_coefficients(side):
        c = sfield[0, side, 1 : 1 + GROUP]
        level = level_of(c.shape)
        half = 0.5 * c
        inner = jnp.logical_and(level > 0, level < levels - 1)
        east, west = rolled(c, LANES - 1), rolled(c, 1)
        kb = jnp.where(inner, 0.0, half)
        for other in (east, west, sfield[0, side, 0:GROUP], sfield[0, side, 2 : 2 + GROUP]):
            kb = kb + jnp.where(other > 0.0, 0.0, half)
        scoef[0, side, 0 : GROUP + 1] = faces(
            sfield[0, side, 0 : GROUP + 1], sfield[0, side, 1 : GROUP + 2]
        )
        scoef[1, side, 1 : 1 + GROUP] = faces(c, east)
        scoef[5, side, 1 : 1 + GROUP] = faces(c, west)
        scoef[2, side, 1 : 1 + GROUP] = jnp.where(
            level < levels - 1, half + pltpu.roll(half, levels - 1, 1), 0.0
        )
        scoef[3, side, 1 : 1 + GROUP] = kb
        scoef[4, side, 1 : 1 + GROUP] = kb + shift_1

    def turned(read, low, n, j):
        v = read(j + 1, low, n)
        down, up = read(j + 1, low - 1, n), read(j + 1, low + 1, n)
        return v, rolled(v, v.shape[-1] - 1), rolled(v, 1), down, up

    def image(read, k, low, n, j, around):
        third = j % 3 if isinstance(j, int) else lax.rem(j, 3)
        shifted = 4 - (third + 1) // 2
        v, east, west, down, up = around
        axis = v.ndim - 1
        across = k(0, low, n) * (v - up)
        back = k(0, low - 1, n) * (down - v)
        fz = k(2, low, n) * (v - pltpu.roll(v, levels - 1, axis - 1))
        rest = (across - back) + ((fz - pltpu.roll(fz, 1, axis - 1)) + k(shifted, low, n) * v)
        if not isinstance(j, int):
            also = jnp.where(third == 1, shift_0, 0.0)
            rest = rest + also * read(jnp.maximum(j, 1), low, n)
        elif third == 1:
            rest = rest + shift_0 * read(j, low, n)
        return rest + (k(1, low, n) * (v - east) + k(5, low, n) * (v - west))

    def images(jobs, j):
        ahead = AHEAD
        around = [turned(read, low, n, j) for read, k, low, n, put in jobs[:ahead]]
        for i, (read, k, low, n, put) in enumerate(jobs):
            if i + ahead < len(jobs):
                other = jobs[i + ahead]
                around.append(turned(other[0], other[2], other[3], j))
            put(j + 2, low, n, image(read, k, low, n, j, around[i]))

    def main(f, low, n):
        return field[f, pl.ds(low, n)]

    def main_k(i, low, n):
        return coef[i, pl.ds(low, n)]

    def main_put(f, low, n, v):
        field[f, pl.ds(low, n)] = v

    def summed(read, low, n, state):
        r, p, w, m, q = (read(f, low, n) for f in (1, 3, 4, 6, 7))
        return tuple(
            s + jnp.sum(t, axis=0) for s, t in zip(state, (r * p, w * p, w * m, q * m))
        )

    STEP = 4

    WIDE = 2 * GROUP

    def own_coefficients(i, state):
        low = HALO + i * WIDE
        coefficients(low, WIDE, False)
        coef[0, pl.ds(low, WIDE)] = 0.5 * (
            field[0, pl.ds(low, WIDE)] + field[0, pl.ds(low + 1, WIDE)]
        )
        return state

    lax.fori_loop(0, rows // WIDE, own_coefficients, 0)

    def own_image(j, state):
        images([(main, main_k, HALO + low, STEP, main_put) for low in range(0, rows, STEP)], j)
        return state

    lax.fori_loop(0, 6, own_image, 0)
    zero = jnp.zeros((levels, cols), jnp.float32)
    acc = lax.fori_loop(
        0, (rows - 2 * HALO) // STEP,
        lambda i, state: summed(main, 2 * HALO + i * STEP, STEP, state), (zero,) * 4,
    )


    def arrived(ways):
        for way in ways:
            dx, dy = WAYS[way]

            @pl.when(exists(-dx, -dy))
            def _():
                for copy in halo_copies(way):
                    copy.wait_recv()

    arrived((2, 3, 4, 5, 6, 7))
    for a in range(2):
        for side in range(2):
            for i in range(GROUP):
                out = sfield[a, side, 1 + i]
                for g in range(groups):
                    if g == 0:
                        if i < GROUP - HALO:
                            continue
                        tile = corner_in[3 - side]
                    elif g == groups - 1:
                        if i >= HALO:
                            continue
                        tile = corner_in[1 - side]
                    else:
                        tile = side_in[1 - side, g - 1]
                    low = width * g + 2 * HALO * side
                    by = low - i * STRIP - (STRIP - HALO) * (1 - side)
                    moved = rolled(tile, by - a * (GROUP * STRIP))
                    out = jnp.where((lane >= low) & (lane < low + HALO), moved, out)
                sfield[a, side, 1 + i] = out

    arrived((0, 1))
    for a in range(2):
        lower = jnp.transpose(x_in[a, 0], (1, 0, 2))[GROUP - HALO : GROUP]
        upper = jnp.transpose(x_in[a, 1], (1, 0, 2))[0:HALO]
        field[a, 0:HALO] = lower
        field[a, HALO + rows : HALO + rows + HALO] = upper
        for side in range(2):
            edge = (0, LANES) if side == 0 else (last, cols)
            for g, block, slot in ((0, lower, GROUP - HALO), (groups - 1, upper, 0)):
                low = width * g + HALO * (1 - side)
                moved = rolled(block[:, :, edge[0] : edge[1]], low + 2 * HALO * side)
                slots_of = pl.ds(1 + slot, HALO)
                sfield[a, side, slots_of] = jnp.where(
                    between(low, low + 2 * HALO, moved.shape), moved, sfield[a, side, slots_of]
                )
            wrap(a, side)

    def edges(i):
        low = 1 + i * (HALO + rows - 2)
        coefficients(low, HALO, True)
        first = low - 1 + i
        coef[0, pl.ds(first, HALO)] = faces(
            field[0, pl.ds(first, HALO)], field[0, pl.ds(first + 1, HALO)]
        )

    for i in range(2):
        edges(i)
    for side in range(2):
        strip_coefficients(side)

    PART = 3
    HALF = GROUP // 2

    def strip_job(side, low):
        def read(f, at, n):
            if at == 0:
                first = rolled(sfield[f, side, pl.ds(GROUP, 1)], width)
                return jnp.concatenate([first, sfield[f, side, pl.ds(1, n - 1)]], axis=0)
            if at + n == GROUP + 2:
                last_row = rolled(sfield[f, side, pl.ds(1, 1)], -width)
                return jnp.concatenate([sfield[f, side, pl.ds(at, n - 1)], last_row], axis=0)
            return sfield[f, side, pl.ds(at, n)]

        def k(i, at, n):
            return scoef[i, side, pl.ds(at, n)]

        def put(f, at, n, v):
            sfield[f, side, pl.ds(at, n)] = v

        return read, k, low, HALF, put

    def edge_image(j):
        jobs = []
        for base in (j + 1, rows - 1 - j + HALO):
            jobs += [(main, main_k, low, PART, main_put) for low in (base, base + PART)]
        strips = [strip_job(side, low) for side in range(2) for low in (1, 1 + HALF)]
        images(jobs + strips, j)

    for j in range(6):
        edge_image(j)
    for base in (HALO, rows):
        for low in (base, base + PART):
            acc = summed(main, low, PART, acc)
    sacc = (jnp.zeros((levels, LANES), jnp.float32),) * 4
    for side in range(2):
        sacc = summed(lambda f, low, n: sfield[f, side, pl.ds(low, n)], 1, GROUP, sacc)

    in_strip = jnp.zeros((levels, LANES), jnp.bool_)
    for g in range(1, tiles + 1):
        low = width * g + HALO
        in_strip = jnp.logical_or(in_strip, (lane >= low) & (lane < low + HALO))
    message = jnp.zeros((levels, LANES), jnp.float32)
    share = LANES // 4
    for i in range(4):
        s = jnp.where(in_strip, sacc[i], 0.0)
        for low in range(0, cols, LANES):
            part = acc[i][:, low : low + LANES]
            if low == 0:
                part = jnp.where(lane >= HALO, part, 0.0)
            if low == last:
                part = jnp.where(lane < LANES - HALO, part, 0.0)
            s = s + part
        s = (s + rolled(s, share)) + (rolled(s, 2 * share) + rolled(s, 3 * share))
        message = jnp.where((lane >= i * share) & (lane < (i + 1) * share), s, message)
    total = jnp.sum(message, axis=0, keepdims=True)

    def finish(t, state):
        low = pl.multiple_of(t * GROUP, GROUP)
        for f, out in ((3, p_out), (4, w_out), (6, m_out), (7, n_out)):
            block = field[f, pl.ds(HALO + low, GROUP)]
            parts = [block[:, :, k : k + LANES] for k in range(0, cols, LANES)]
            for side in range(2):
                strip = sfield[f, side, 1 : 1 + GROUP]
                to = 0 if side == 0 else LANES - HALO
                part = 0 if side == 0 else len(parts) - 1
                by = lax.rem(to - HALO - width + 2 * LANES - width * t, LANES)
                parts[part] = jnp.where(
                    between(to, to + HALO, strip.shape), rolled(strip, by), parts[part]
                )
            for k, part in enumerate(parts):
                out[:, pl.ds(low, GROUP), k * LANES : (k + 1) * LANES] = jnp.transpose(
                    part, (1, 0, 2)
                )
        return state

    if planes:
        relay_wait()
    base = 0
    sent = []
    for index, stage in enumerate(stages):
        count = stage[0] * stage[1]
        mine = base + place_in(stage)[0]
        slots[pl.ds(mine, 1), :] = total

        def send(device):
            pltpu.make_async_remote_copy(
                src_ref=slots.at[pl.ds(mine, 1)], dst_ref=slots.at[pl.ds(mine, 1)],
                send_sem=red_send.at[index], recv_sem=red_recv.at[index],
                device_id=device, device_id_type=LOGICAL,
            ).start()

        each_other(stage, send)
        if index == 0:
            lax.fori_loop(0, tiles, finish, 0)
            r_out[...] = fresh[1]
            for way in range(8):

                @pl.when(exists(*WAYS[way]))
                def _():
                    for copy in halo_copies(way):
                        copy.wait_send()

        if count > 1:
            whole = slots.at[pl.ds(base, count - 1)]
            pltpu.make_async_copy(whole, whole, red_recv.at[index]).wait()
            sent.append((whole, red_send.at[index]))
        total = jnp.sum(slots[base : base + count], axis=0, keepdims=True)
        base += -(-count // 8) * 8
    sums_out[...] = total
    for whole, sem in sent:
        pltpu.make_async_copy(whole, whole, sem).wait()


def combine(p, w, m, n, r, sums, x_hbm, res_hbm, x_vmem, res_vmem, sem):
    levels = p.shape[0]
    total = sums[...]
    lane = lax.broadcasted_iota(jnp.int32, total.shape, 1)
    share = LANES // 4

    def of(i, scale):
        chosen = (lane >= i * share) & (lane < (i + 1) * share)
        return scale * jnp.sum(jnp.where(chosen, total, 0.0), axis=1, keepdims=True)

    rp, wp, wm, nm = (of(i, power_2 ** (i + 1)) for i in range(4))
    gamma_old = rp
    alpha_old = gamma_old / wp
    gamma = (rp - alpha_old * wp) - alpha_old * (wp - alpha_old * wm)
    delta = (wp - alpha_old * wm) - alpha_old * (wm - alpha_old * nm)
    beta = gamma / gamma_old
    alpha = gamma / (delta - beta * gamma / alpha_old)
    near = power_2 * (alpha_old + alpha * (1.0 + beta))
    far = (power_2 * power_2) * (alpha * alpha_old)
    copies = []
    for z in range(levels):
        x_vmem[z] = near * p[z] - far * m[z]
        res_vmem[z] = (r[z] - near * w[z]) + far * n[z]
        for a, (one, two) in enumerate(((x_vmem, x_hbm), (res_vmem, res_hbm))):
            copies.append(pltpu.make_async_copy(one.at[z], two.at[z], sem.at[a, z]))
            copies[-1].start()
    for copy in copies:
        copy.wait()


def solution(mesh):
    num_x, num_y = mesh.shape["gx"], mesh.shape["gy"]

    def per_device(right_side, conductivity):
        levels, rows, cols = right_side.shape
        high = rows + 2 * HALO
        tiles = rows // GROUP
        stages = stages_of(num_x, num_y)
        deep = sum(-(-(a * b) // 8) * 8 for a, b in stages)

        def body(*refs):
            kernel(num_x, num_y, *refs)

        block = (levels, rows, cols)
        full = (high, levels, cols)
        slim = (2, GROUP + 2, levels, LANES)
        out = jax.ShapeDtypeStruct(block, jnp.float32)
        sums = jax.ShapeDtypeStruct((1, LANES), jnp.float32)
        vmem = lambda shape: pltpu.VMEM(shape, jnp.float32)
        dma = lambda *n: pltpu.SemaphoreType.DMA(n)
        in_vmem = pl.BlockSpec(memory_space=pltpu.VMEM)
        in_hbm = pl.BlockSpec(memory_space=pltpu.HBM)
        parts = pl.pallas_call(
            body,
            out_shape=(out,) * 5 + (sums,),
            in_specs=[in_hbm] * 2,
            out_specs=(in_vmem,) * 6,
            scratch_shapes=[
                vmem((2,) + block), vmem((2, 2, levels, GROUP, cols)),
                vmem((6,) + full), vmem((6,) + slim), vmem((8,) + full), vmem((8,) + slim),
                vmem((2, tiles, levels, LANES)), vmem((2, tiles, levels, LANES)),
                vmem((4, levels, LANES)), vmem((deep, LANES)),
                dma(2), dma(8, 2), dma(8, 2), dma(len(stages)), dma(len(stages)),
                pltpu.SemaphoreType.REGULAR,
            ],
            compiler_params=pltpu.CompilerParams(
                collective_id=0, has_side_effects=True, vmem_limit_bytes=55000000
            ),
        )(right_side, conductivity)
        return pl.pallas_call(
            combine,
            out_shape=(out, out),
            in_specs=[in_vmem] * 6,
            out_specs=(in_hbm,) * 2,
            scratch_shapes=[vmem(block), vmem(block), dma(2, levels)],
            compiler_params=pltpu.CompilerParams(vmem_limit_bytes=4000000),
        )(*parts)

    return jax.shard_map(
        per_device,
        mesh=mesh,
        in_specs=(P(None, "gx", "gy"), P(None, "gx", "gy")),
        out_specs=(P(None, "gx", "gy"), P(None, "gx", "gy")),
        check_vma=False,
    )
```

```python
import jax
import jax.numpy as jnp
from jax import lax
from jax.experimental import pallas as pl
from jax.experimental.pallas import tpu as pltpu
from jax.sharding import PartitionSpec as P

low_bound = 0.4
high_bound = 12.0
cheb_theta = 0.5 * (high_bound + low_bound)
cheb_delta = 0.5 * (high_bound - low_bound)
cheb_sigma = cheb_theta / cheb_delta
rho_first = 1.0 / cheb_sigma
rho_second = 1.0 / (2.0 * cheb_sigma - rho_first)
rho_third = 1.0 / (2.0 * cheb_sigma - rho_second)

step_0 = rho_second * rho_first / cheb_theta + 2.0 * rho_second / cheb_delta
step_1 = 2.0 * rho_second / cheb_delta / cheb_theta
mix_0 = 1.0 + rho_third * rho_second
mix_1 = 2.0 * rho_third / cheb_delta
power_0 = 1.0 / cheb_theta + mix_0 * step_0 + mix_1
power_1 = -mix_0 * step_1 - mix_1 / cheb_theta - mix_1 * step_0
power_2 = mix_1 * step_1
shift_1 = power_1 / power_2
shift_0 = power_0 / power_2

HALO = 6
AHEAD = 2
PLANE = 2
LANES = 128
STRIP = 8
GROUP = 8
ONE_STAGE = 64
MESH = pl.DeviceIdType.MESH
LOGICAL = pl.DeviceIdType.LOGICAL
WAYS = ((-1, 0), (1, 0), (0, -1), (0, 1), (-1, -1), (-1, 1), (1, -1), (1, 1))


def stages_of(num_x, num_y):
    if num_x * num_y <= ONE_STAGE:
        return ((num_x, num_y),)
    return ((num_x, 1), (1, num_y))


def kernel(
    num_x, num_y, r_hbm, c_hbm, p_out, w_out, m_out, n_out, r_out, sums_out,
    fresh, x_in, coef, scoef, field, sfield, packed, side_in, corner_in, slots,
    in_sem, halo_send, halo_recv, red_send, red_recv, relayed,
):
    _, levels, rows, cols = fresh.shape
    tiles = rows // GROUP
    groups = tiles + 2
    width = LANES // groups
    last = cols - LANES
    me_x = lax.axis_index("gx")
    me_y = lax.axis_index("gy")
    stages = stages_of(num_x, num_y)

    def exists(dx, dy):
        ok = jnp.bool_(True)
        if dx < 0:
            ok = me_x > 0
        if dx > 0:
            ok = me_x < num_x - 1
        if dy < 0:
            ok_y = me_y > 0
            ok = ok_y if dx == 0 else jnp.logical_and(ok, ok_y)
        if dy > 0:
            ok_y = me_y < num_y - 1
            ok = ok_y if dx == 0 else jnp.logical_and(ok, ok_y)
        return ok

    loads = [
        pltpu.make_async_copy(ref, fresh.at[a], in_sem.at[a])
        for a, ref in enumerate((c_hbm, r_hbm))
    ]
    for load in loads:
        load.start()

    def place_in(stage):
        count_x, count_y = stage
        if count_x > 1 and count_y > 1:
            return me_x * num_y + me_y, lambda o: o
        if count_x > 1:
            return me_x, lambda o: o * num_y + me_y
        return me_y, lambda o: me_x * num_y + o

    def each_other(stage, act):
        mine, device = place_in(stage)
        total = stage[0] * stage[1]

        flip = mine < total // 2
        start_at = jnp.where(flip, total - 1 - mine, mine)

        def step(k, state):
            other = jnp.where(k > start_at, k, k - 1)
            act(device(jnp.where(flip, total - 1 - other, other)))
            return state

        lax.fori_loop(1, total, step, 0)

    barrier = pltpu.get_barrier_semaphore()

    def greet(device):
        pl.semaphore_signal(barrier, inc=1, device_id=device, device_id_type=LOGICAL)

    planes = len(stages) == 1 and num_x % PLANE == 0
    plane = me_x // PLANE * PLANE
    expected = jnp.int32(0)
    if planes:
        mine = me_x * num_y + me_y
        begin = me_x == plane

        for dy in (0, -1, 1):
            down = jnp.logical_and(begin, exists(-1, dy))
            up = jnp.logical_and(me_x == plane + PLANE - 1, exists(1, dy))

            @pl.when(down)
            def _():
                greet(mine - num_y + dy)

            expected = expected + up.astype(jnp.int32)

        def onward(other, state):
            @pl.when(other != mine)
            def _():
                greet(other)

            return state

        lax.fori_loop(plane * num_y, num_x * num_y, onward, 0)
        expected = expected + ((plane + PLANE) * num_y - 1)
    else:
        for stage in stages:
            each_other(stage, greet)
            expected = expected + (stage[0] * stage[1] - 1)
    if len(stages) > 1:
        for dx, dy in WAYS[4:]:
            ok = exists(dx, dy)

            @pl.when(ok)
            def _():
                greet((me_x + dx) * num_y + me_y + dy)

            expected = expected + ok.astype(jnp.int32)

    def relay():
        def tell(k, state):
            pl.semaphore_signal(
                relayed, inc=1, device_id=(me_x - k * PLANE) * num_y + me_y, device_id_type=LOGICAL
            )
            return state

        lax.fori_loop(1, me_x // PLANE + 1, tell, 0)

    def relay_wait():
        @pl.when(me_x < num_x - PLANE)
        def _():
            pl.semaphore_wait(relayed, (num_x - 1 - me_x) // PLANE)

    def halo_copies(way):
        dx, dy = WAYS[way]
        if dy == 0:
            side = 1 if dx < 0 else 0
            low = 0 if dx < 0 else rows - HALO
            land = 0 if dx < 0 else GROUP - HALO
            pairs = [
                (fresh.at[a, :, pl.ds(low, HALO)], x_in.at[a, side, :, pl.ds(land, HALO)])
                for a in range(2)
            ]
        elif dx == 0:
            pairs = [(packed.at[0 if dy < 0 else 1], side_in.at[0 if dy < 0 else 1])]
        else:
            pairs = [(
                packed.at[0 if dy < 0 else 1, 0 if dx < 0 else tiles - 1],
                corner_in.at[way - 4],
            )]
        return [
            pltpu.make_async_remote_copy(
                src_ref=one, dst_ref=two,
                send_sem=halo_send.at[way, a], recv_sem=halo_recv.at[way, a],
                device_id=(me_x + dx, me_y + dy), device_id_type=MESH,
            )
            for a, (one, two) in enumerate(pairs)
        ]

    def start(way, number=0):
        @pl.when(exists(*WAYS[way]))
        def _():
            halo_copies(way)[number].start()


    lane = lax.broadcasted_iota(jnp.int32, (levels, LANES), 1)

    def between(low, high, like):
        at = lax.broadcasted_iota(jnp.int32, (1,) * (len(like) - 1) + (LANES,), len(like) - 1)
        return (at >= low) & (at < high)

    def rolled(v, by):
        if isinstance(by, int):
            by = by % v.shape[-1]
            if by == 0:
                return v
        return pltpu.roll(v, by, v.ndim - 1)

    for load in loads:
        load.wait()

    def arrange(t):
        low = t * GROUP
        acc = [jnp.zeros((levels, LANES), jnp.float32)] * 2
        for a in range(2):
            block = jnp.transpose(fresh[a, :, low : low + GROUP, :], (1, 0, 2))
            field[a, HALO + low : HALO + low + GROUP] = block
            for side in range(2):
                offset = 0 if side == 0 else LANES - STRIP
                part = block[:, :, (0 if side == 0 else last) : (LANES if side == 0 else cols)]
                for g in range(GROUP):
                    place = (a * GROUP + g) * STRIP
                    moved = rolled(part[g], place - offset)
                    acc[side] = jnp.where(
                        (lane >= place) & (lane < place + STRIP), moved, acc[side]
                    )
        for side in range(2):
            packed[side, t] = acc[side]

    for t in sorted({0, tiles - 1}):
        arrange(t)
    pl.semaphore_wait(barrier, expected)
    for way in (4, 5, 6, 7):
        start(way)
    for number in range(2):
        for way in (0, 1):
            start(way, number)
    for t in range(1, tiles - 1):
        arrange(t)
    for way in (2, 3):
        start(way)
    if planes:
        relay()

    for way in range(8):
        dx, dy = WAYS[way]

        @pl.when(jnp.logical_not(exists(-dx, -dy)))
        def _():
            if dy == 0:
                x_in[:, 1 if dx < 0 else 0] = jnp.zeros((2, levels, GROUP, cols), jnp.float32)
            elif dx == 0:
                side_in[0 if dy < 0 else 1] = jnp.zeros((tiles, levels, LANES), jnp.float32)
            else:
                corner_in[way - 4] = jnp.zeros((levels, LANES), jnp.float32)

    def own_strips(a, state):
        for side in range(2):
            acc = jnp.zeros((GROUP, levels, LANES), jnp.float32)
            for g in range(1, tiles + 1):
                low = width * g + HALO * (1 - side)
                block = field[
                    a, HALO + (g - 1) * GROUP : HALO + g * GROUP, :,
                    (0 if side == 0 else last) : (LANES if side == 0 else cols),
                ]
                moved = rolled(block, low + 2 * HALO * side)
                acc = jnp.where(between(low, low + 2 * HALO, block.shape), moved, acc)
            sfield[a, side, 1 : 1 + GROUP] = acc
        return state

    lax.fori_loop(0, 2, own_strips, 0)

    def wrap(f, side):
        sfield[f, side, 0] = rolled(sfield[f, side, GROUP], width)
        sfield[f, side, GROUP + 1] = rolled(sfield[f, side, 1], -width)

    def level_of(shape):
        return lax.broadcasted_iota(jnp.int32, (1, levels, shape[-1]), 1)

    def faces(c, other):
        return jnp.where(jnp.minimum(c, other) > 0.0, 0.5 * (c + other), 0.0)

    def coefficients(low, n, beside):
        c = field[0, pl.ds(low, n)]
        level = level_of(c.shape)
        at = lax.broadcasted_iota(jnp.int32, (1, 1, cols), 2)
        half = 0.5 * c
        inner = jnp.logical_and(level > 0, level < levels - 1)
        kb = jnp.where(inner, 0.0, half)
        if beside:
            for other in (field[0, pl.ds(low - 1, n)], field[0, pl.ds(low + 1, n)]):
                kb = kb + jnp.where(other > 0.0, 0.0, half)
        ke = jnp.where(at < cols - 1, half + rolled(half, cols - 1), 0.0)
        kw = jnp.where(at > 0, half + rolled(half, 1), 0.0)
        kb = kb + (ke + kw)
        coef[1, pl.ds(low, n)] = ke
        coef[5, pl.ds(low, n)] = kw
        coef[2, pl.ds(low, n)] = jnp.where(
            level < levels - 1, half + pltpu.roll(half, levels - 1, 1), 0.0
        )
        coef[3, pl.ds(low, n)] = kb
        coef[4, pl.ds(low, n)] = kb + shift_1

    def strip_coefficients(side):
        c = sfield[0, side, 1 : 1 + GROUP]
        level = level_of(c.shape)
        half = 0.5 * c
        inner = jnp.logical_and(level > 0, level < levels - 1)
        east, west = rolled(c, LANES - 1), rolled(c, 1)
        kb = jnp.where(inner, 0.0, half)
        for other in (east, west, sfield[0, side, 0:GROUP], sfield[0, side, 2 : 2 + GROUP]):
            kb = kb + jnp.where(other > 0.0, 0.0, half)
        scoef[0, side, 0 : GROUP + 1] = faces(
            sfield[0, side, 0 : GROUP + 1], sfield[0, side, 1 : GROUP + 2]
        )
        ke, kw = faces(c, east), faces(c, west)
        kb = kb + (ke + kw)
        scoef[1, side, 1 : 1 + GROUP] = ke
        scoef[5, side, 1 : 1 + GROUP] = kw
        scoef[2, side, 1 : 1 + GROUP] = jnp.where(
            level < levels - 1, half + pltpu.roll(half, levels - 1, 1), 0.0
        )
        scoef[3, side, 1 : 1 + GROUP] = kb
        scoef[4, side, 1 : 1 + GROUP] = kb + shift_1

    def turned(read, low, n, j):
        v = read(j + 1, low, n)
        down, up = read(j + 1, low - 1, n), read(j + 1, low + 1, n)
        parts = [v[..., at : at + LANES] for at in range(0, v.shape[-1], LANES)]
        ons = [rolled(part, LANES - 1) for part in parts]
        backs = [rolled(part, 1) for part in parts]
        count = len(parts)
        east = [
            jnp.where(between(LANES - 1, LANES, v.shape), ons[i + 1], ons[i]) if i + 1 < count else ons[i]
            for i in range(count)
        ]
        west = [
            jnp.where(between(0, 1, v.shape), backs[i - 1], backs[i]) if i else backs[i]
            for i in range(count)
        ]
        east, west = (
            jnp.concatenate(x, axis=-1) if count > 1 else x[0] for x in (east, west)
        )
        return v, east, west, down, up

    def image(read, k, low, n, j, around):
        third = j % 3 if isinstance(j, int) else lax.rem(j, 3)
        shifted = 4 - (third + 1) // 2
        v, east, west, down, up = around
        axis = v.ndim - 1
        rows_of = jnp.concatenate([down[:1], v, up[n - 1 :]], axis=0)
        across = k(0, low - 1, n + 1) * (rows_of[: n + 1] - rows_of[1:])
        fz = k(2, low, n) * (v - pltpu.roll(v, levels - 1, axis - 1))
        rest = (across[1:] - across[:n]) + ((fz - pltpu.roll(fz, 1, axis - 1)) + k(shifted, low, n) * v)
        if not isinstance(j, int):
            also = jnp.where(third == 1, shift_0, 0.0)
            rest = rest + also * read(jnp.maximum(j, 1), low, n)
        elif third == 1:
            rest = rest + shift_0 * read(j, low, n)
        return rest - (k(1, low, n) * east + k(5, low, n) * west)

    def images(jobs, j):
        ahead = AHEAD
        around = [turned(read, low, n, j) for read, k, low, n, put in jobs[:ahead]]
        for i, (read, k, low, n, put) in enumerate(jobs):
            if i + ahead < len(jobs):
                other = jobs[i + ahead]
                around.append(turned(other[0], other[2], other[3], j))
            put(j + 2, low, n, image(read, k, low, n, j, around[i]))

    def main(f, low, n):
        return field[f, pl.ds(low, n)]

    def main_k(i, low, n):
        return coef[i, pl.ds(low, n)]

    def main_put(f, low, n, v):
        field[f, pl.ds(low, n)] = v

    def summed(read, low, n, state):
        r, p, w, m, q = (read(f, low, n) for f in (1, 3, 4, 6, 7))
        return tuple(
            s + jnp.sum(t, axis=0) for s, t in zip(state, (r * p, w * p, w * m, q * m))
        )

    STEP = 4

    WIDE = 2 * GROUP

    def own_coefficients(i, state):
        low = HALO + i * WIDE
        coefficients(low, WIDE, False)
        coef[0, pl.ds(low, WIDE)] = 0.5 * (
            field[0, pl.ds(low, WIDE)] + field[0, pl.ds(low + 1, WIDE)]
        )
        return state

    lax.fori_loop(0, rows // WIDE, own_coefficients, 0)

    def own_image(j, state):
        images([(main, main_k, HALO + low, STEP, main_put) for low in range(0, rows, STEP)], j)
        return state

    lax.fori_loop(0, 6, own_image, 0)
    zero = jnp.zeros((levels, cols), jnp.float32)
    acc = lax.fori_loop(
        0, (rows - 2 * HALO) // STEP,
        lambda i, state: summed(main, 2 * HALO + i * STEP, STEP, state), (zero,) * 4,
    )


    def arrived(ways, number):
        for way in ways:
            dx, dy = WAYS[way]

            @pl.when(exists(-dx, -dy))
            def _():
                halo_copies(way)[number].wait_recv()

    arrived((2, 3, 4, 5, 6, 7), 0)
    for a in range(2):
        for side in range(2):
            for i in range(GROUP):
                out = sfield[a, side, 1 + i]
                for g in range(groups):
                    if g == 0:
                        if i < GROUP - HALO:
                            continue
                        tile = corner_in[3 - side]
                    elif g == groups - 1:
                        if i >= HALO:
                            continue
                        tile = corner_in[1 - side]
                    else:
                        tile = side_in[1 - side, g - 1]
                    low = width * g + 2 * HALO * side
                    by = low - i * STRIP - (STRIP - HALO) * (1 - side)
                    moved = rolled(tile, by - a * (GROUP * STRIP))
                    out = jnp.where((lane >= low) & (lane < low + HALO), moved, out)
                sfield[a, side, 1 + i] = out

    def edges(i):
        low = 1 + i * (HALO + rows - 2)
        coefficients(low, HALO, True)
        first = low - 1 + i
        coef[0, pl.ds(first, HALO)] = faces(
            field[0, pl.ds(first, HALO)], field[0, pl.ds(first + 1, HALO)]
        )

    for a in range(2):
        arrived((0, 1), a)
        lower = jnp.transpose(x_in[a, 0], (1, 0, 2))[GROUP - HALO : GROUP]
        upper = jnp.transpose(x_in[a, 1], (1, 0, 2))[0:HALO]
        field[a, 0:HALO] = lower
        field[a, HALO + rows : HALO + rows + HALO] = upper
        for side in range(2):
            edge = (0, LANES) if side == 0 else (last, cols)
            for g, block, slot in ((0, lower, GROUP - HALO), (groups - 1, upper, 0)):
                low = width * g + HALO * (1 - side)
                moved = rolled(block[:, :, edge[0] : edge[1]], low + 2 * HALO * side)
                slots_of = pl.ds(1 + slot, HALO)
                sfield[a, side, slots_of] = jnp.where(
                    between(low, low + 2 * HALO, moved.shape), moved, sfield[a, side, slots_of]
                )
            wrap(a, side)
        if a == 0:
            for i in range(2):
                edges(i)
            for side in range(2):
                strip_coefficients(side)

    PART = 6
    HALF = GROUP // 2

    def strip_job(side, low):
        def read(f, at, n):
            if at == 0:
                first = rolled(sfield[f, side, pl.ds(GROUP, 1)], width)
                return jnp.concatenate([first, sfield[f, side, pl.ds(1, n - 1)]], axis=0)
            if at + n == GROUP + 2:
                last_row = rolled(sfield[f, side, pl.ds(1, 1)], -width)
                return jnp.concatenate([sfield[f, side, pl.ds(at, n - 1)], last_row], axis=0)
            return sfield[f, side, pl.ds(at, n)]

        def k(i, at, n):
            return scoef[i, side, pl.ds(at, n)]

        def put(f, at, n, v):
            sfield[f, side, pl.ds(at, n)] = v

        return read, k, low, HALF, put

    def edge_image(j):
        jobs = []
        for base in (j + 1, rows - 1 - j + HALO):
            jobs += [(main, main_k, low, PART, main_put) for low in (base,)]
        strips = [strip_job(side, low) for side in range(2) for low in (1, 1 + HALF)]
        images(jobs + strips, j)

    for j in range(6):
        edge_image(j)
    for base in (HALO, rows):
        for low in (base,):
            acc = summed(main, low, PART, acc)
    sacc = (jnp.zeros((levels, LANES), jnp.float32),) * 4
    for side in range(2):
        sacc = summed(lambda f, low, n: sfield[f, side, pl.ds(low, n)], 1, GROUP, sacc)

    in_strip = jnp.zeros((levels, LANES), jnp.bool_)
    for g in range(1, tiles + 1):
        low = width * g + HALO
        in_strip = jnp.logical_or(in_strip, (lane >= low) & (lane < low + HALO))
    message = jnp.zeros((levels, LANES), jnp.float32)
    share = LANES // 4
    for i in range(4):
        s = jnp.where(in_strip, sacc[i], 0.0)
        for low in range(0, cols, LANES):
            part = acc[i][:, low : low + LANES]
            if low == 0:
                part = jnp.where(lane >= HALO, part, 0.0)
            if low == last:
                part = jnp.where(lane < LANES - HALO, part, 0.0)
            s = s + part
        s = (s + rolled(s, share)) + (rolled(s, 2 * share) + rolled(s, 3 * share))
        message = jnp.where((lane >= i * share) & (lane < (i + 1) * share), s, message)
    total = jnp.sum(message, axis=0, keepdims=True)

    def finish(t, state):
        low = pl.multiple_of(t * GROUP, GROUP)
        for f, out in ((3, p_out), (4, w_out), (6, m_out), (7, n_out)):
            block = field[f, pl.ds(HALO + low, GROUP)]
            parts = [block[:, :, k : k + LANES] for k in range(0, cols, LANES)]
            for side in range(2):
                strip = sfield[f, side, 1 : 1 + GROUP]
                to = 0 if side == 0 else LANES - HALO
                part = 0 if side == 0 else len(parts) - 1
                by = lax.rem(to - HALO - width + 2 * LANES - width * t, LANES)
                parts[part] = jnp.where(
                    between(to, to + HALO, strip.shape), rolled(strip, by), parts[part]
                )
            for k, part in enumerate(parts):
                out[:, pl.ds(low, GROUP), k * LANES : (k + 1) * LANES] = jnp.transpose(
                    part, (1, 0, 2)
                )
        return state

    if planes:
        relay_wait()
    base = 0
    sent = []
    for index, stage in enumerate(stages):
        count = stage[0] * stage[1]
        mine = base + place_in(stage)[0]
        slots[pl.ds(mine, 1), :] = total

        def send(device):
            pltpu.make_async_remote_copy(
                src_ref=slots.at[pl.ds(mine, 1)], dst_ref=slots.at[pl.ds(mine, 1)],
                send_sem=red_send.at[index], recv_sem=red_recv.at[index],
                device_id=device, device_id_type=LOGICAL,
            ).start()

        each_other(stage, send)
        if index == 0:
            lax.fori_loop(0, tiles, finish, 0)
            r_out[...] = fresh[1]
            for way in range(8):

                @pl.when(exists(*WAYS[way]))
                def _():
                    for copy in halo_copies(way):
                        copy.wait_send()

        if count > 1:
            whole = slots.at[pl.ds(base, count - 1)]
            pltpu.make_async_copy(whole, whole, red_recv.at[index]).wait()
            sent.append((whole, red_send.at[index]))
        total = jnp.sum(slots[base : base + count], axis=0, keepdims=True)
        base += -(-count // 8) * 8
    sums_out[...] = total
    for whole, sem in sent:
        pltpu.make_async_copy(whole, whole, sem).wait()


def combine(p, w, m, n, r, sums, x_hbm, res_hbm, x_vmem, res_vmem, sem):
    levels = p.shape[0]
    total = sums[...]
    lane = lax.broadcasted_iota(jnp.int32, total.shape, 1)
    share = LANES // 4

    def of(i, scale):
        chosen = (lane >= i * share) & (lane < (i + 1) * share)
        return scale * jnp.sum(jnp.where(chosen, total, 0.0), axis=1, keepdims=True)

    rp, wp, wm, nm = (of(i, power_2 ** (i + 1)) for i in range(4))
    gamma_old = rp
    alpha_old = gamma_old / wp
    gamma = (rp - alpha_old * wp) - alpha_old * (wp - alpha_old * wm)
    delta = (wp - alpha_old * wm) - alpha_old * (wm - alpha_old * nm)
    beta = gamma / gamma_old
    alpha = gamma / (delta - beta * gamma / alpha_old)
    near = power_2 * (alpha_old + alpha * (1.0 + beta))
    far = (power_2 * power_2) * (alpha * alpha_old)
    copies = []
    for z in range(levels):
        x_vmem[z] = near * p[z] - far * m[z]
        res_vmem[z] = (r[z] - near * w[z]) + far * n[z]
        for a, (one, two) in enumerate(((x_vmem, x_hbm), (res_vmem, res_hbm))):
            copies.append(pltpu.make_async_copy(one.at[z], two.at[z], sem.at[a]))
            copies[-1].start()
    for a, (one, two) in enumerate(((x_vmem, x_hbm), (res_vmem, res_hbm))):
        pltpu.make_async_copy(one, two, sem.at[a]).wait()


def solution(mesh):
    num_x, num_y = mesh.shape["gx"], mesh.shape["gy"]

    def per_device(right_side, conductivity):
        levels, rows, cols = right_side.shape
        high = rows + 2 * HALO
        tiles = rows // GROUP
        stages = stages_of(num_x, num_y)
        deep = sum(-(-(a * b) // 8) * 8 for a, b in stages)

        def body(*refs):
            kernel(num_x, num_y, *refs)

        block = (levels, rows, cols)
        full = (high, levels, cols)
        slim = (2, GROUP + 2, levels, LANES)
        out = jax.ShapeDtypeStruct(block, jnp.float32)
        sums = jax.ShapeDtypeStruct((1, LANES), jnp.float32)
        vmem = lambda shape: pltpu.VMEM(shape, jnp.float32)
        dma = lambda *n: pltpu.SemaphoreType.DMA(n)
        in_vmem = pl.BlockSpec(memory_space=pltpu.VMEM)
        in_hbm = pl.BlockSpec(memory_space=pltpu.HBM)
        parts = pl.pallas_call(
            body,
            out_shape=(out,) * 5 + (sums,),
            in_specs=[in_hbm] * 2,
            out_specs=(in_vmem,) * 6,
            scratch_shapes=[
                vmem((2,) + block), vmem((2, 2, levels, GROUP, cols)),
                vmem((6,) + full), vmem((6,) + slim), vmem((8,) + full), vmem((8,) + slim),
                vmem((2, tiles, levels, LANES)), vmem((2, tiles, levels, LANES)),
                vmem((4, levels, LANES)), vmem((deep, LANES)),
                dma(2), dma(8, 2), dma(8, 2), dma(len(stages)), dma(len(stages)),
                pltpu.SemaphoreType.REGULAR,
            ],
            compiler_params=pltpu.CompilerParams(
                collective_id=0, has_side_effects=True, vmem_limit_bytes=55000000
            ),
        )(right_side, conductivity)
        return pl.pallas_call(
            combine,
            out_shape=(out, out),
            in_specs=[in_vmem] * 6,
            out_specs=(in_hbm,) * 2,
            scratch_shapes=[vmem(block), vmem(block), dma(2)],
            compiler_params=pltpu.CompilerParams(vmem_limit_bytes=4000000),
        )(*parts)

    return jax.shard_map(
        per_device,
        mesh=mesh,
        in_specs=(P(None, "gx", "gy"), P(None, "gx", "gy")),
        out_specs=(P(None, "gx", "gy"), P(None, "gx", "gy")),
        check_vma=False,
    )
```

```python
import jax
import jax.numpy as jnp
from jax import lax
from jax.experimental import pallas as pl
from jax.experimental.pallas import tpu as pltpu
from jax.sharding import PartitionSpec as P

low_bound = 0.4
high_bound = 12.0
cheb_theta = 0.5 * (high_bound + low_bound)
cheb_delta = 0.5 * (high_bound - low_bound)
cheb_sigma = cheb_theta / cheb_delta
rho_first = 1.0 / cheb_sigma
rho_second = 1.0 / (2.0 * cheb_sigma - rho_first)
rho_third = 1.0 / (2.0 * cheb_sigma - rho_second)

step_0 = rho_second * rho_first / cheb_theta + 2.0 * rho_second / cheb_delta
step_1 = 2.0 * rho_second / cheb_delta / cheb_theta
mix_0 = 1.0 + rho_third * rho_second
mix_1 = 2.0 * rho_third / cheb_delta
power_0 = 1.0 / cheb_theta + mix_0 * step_0 + mix_1
power_1 = -mix_0 * step_1 - mix_1 / cheb_theta - mix_1 * step_0
power_2 = mix_1 * step_1
shift_1 = power_1 / power_2
shift_0 = power_0 / power_2

HALO = 6
AHEAD = 2
PLANE = 2
LANES = 128
STRIP = 8
GROUP = 8
ONE_STAGE = 64
MESH = pl.DeviceIdType.MESH
LOGICAL = pl.DeviceIdType.LOGICAL
WAYS = ((-1, 0), (1, 0), (0, -1), (0, 1), (-1, -1), (-1, 1), (1, -1), (1, 1))


def stages_of(num_x, num_y):
    if num_x * num_y <= ONE_STAGE:
        return ((num_x, num_y),)
    return ((num_x, 1), (1, num_y))


def kernel(
    num_x, num_y, r_hbm, c_hbm, p_out, w_out, m_out, n_out, r_out, sums_out,
    fresh, x_in, coef, scoef, field, sfield, packed, side_in, corner_in, slots,
    in_sem, halo_send, halo_recv, red_send, red_recv, relayed,
):
    _, levels, rows, cols = fresh.shape
    tiles = rows // GROUP
    groups = tiles + 2
    width = LANES // groups
    last = cols - LANES
    me_x = lax.axis_index("gx")
    me_y = lax.axis_index("gy")
    stages = stages_of(num_x, num_y)

    def exists(dx, dy):
        ok = jnp.bool_(True)
        if dx < 0:
            ok = me_x > 0
        if dx > 0:
            ok = me_x < num_x - 1
        if dy < 0:
            ok_y = me_y > 0
            ok = ok_y if dx == 0 else jnp.logical_and(ok, ok_y)
        if dy > 0:
            ok_y = me_y < num_y - 1
            ok = ok_y if dx == 0 else jnp.logical_and(ok, ok_y)
        return ok

    loads = [
        pltpu.make_async_copy(ref, fresh.at[a], in_sem.at[a])
        for a, ref in enumerate((c_hbm, r_hbm))
    ]
    for load in loads:
        load.start()

    def place_in(stage):
        count_x, count_y = stage
        if count_x > 1 and count_y > 1:
            return me_x * num_y + me_y, lambda o: o
        if count_x > 1:
            return me_x, lambda o: o * num_y + me_y
        return me_y, lambda o: me_x * num_y + o

    def each_other(stage, act):
        mine, device = place_in(stage)
        total = stage[0] * stage[1]

        flip = mine < total // 2
        start_at = jnp.where(flip, total - 1 - mine, mine)

        def step(k, state):
            other = jnp.where(k > start_at, k, k - 1)
            act(device(jnp.where(flip, total - 1 - other, other)))
            return state

        lax.fori_loop(1, total, step, 0)

    barrier = pltpu.get_barrier_semaphore()

    def greet(device):
        pl.semaphore_signal(barrier, inc=1, device_id=device, device_id_type=LOGICAL)

    planes = len(stages) == 1 and num_x % PLANE == 0
    plane = me_x // PLANE * PLANE
    expected = jnp.int32(0)
    if planes:
        mine = me_x * num_y + me_y
        begin = me_x == plane

        for dy in (0, -1, 1):
            down = jnp.logical_and(begin, exists(-1, dy))
            up = jnp.logical_and(me_x == plane + PLANE - 1, exists(1, dy))

            @pl.when(down)
            def _():
                greet(mine - num_y + dy)

            expected = expected + up.astype(jnp.int32)

        def onward(other, state):
            @pl.when(other != mine)
            def _():
                greet(other)

            return state

        lax.fori_loop(plane * num_y, num_x * num_y, onward, 0)
        expected = expected + ((plane + PLANE) * num_y - 1)
    else:
        for stage in stages:
            each_other(stage, greet)
            expected = expected + (stage[0] * stage[1] - 1)
    if len(stages) > 1:
        for dx, dy in WAYS[4:]:
            ok = exists(dx, dy)

            @pl.when(ok)
            def _():
                greet((me_x + dx) * num_y + me_y + dy)

            expected = expected + ok.astype(jnp.int32)

    def relay():
        def tell(k, state):
            pl.semaphore_signal(
                relayed, inc=1, device_id=(me_x - k * PLANE) * num_y + me_y, device_id_type=LOGICAL
            )
            return state

        lax.fori_loop(1, me_x // PLANE + 1, tell, 0)

    def relay_wait():
        @pl.when(me_x < num_x - PLANE)
        def _():
            pl.semaphore_wait(relayed, (num_x - 1 - me_x) // PLANE)

    def halo_copies(way):
        dx, dy = WAYS[way]
        if dy == 0:
            side = 1 if dx < 0 else 0
            low = 0 if dx < 0 else rows - HALO
            land = 0 if dx < 0 else GROUP - HALO
            pairs = [
                (fresh.at[a, :, pl.ds(low, HALO)], x_in.at[a, side, :, pl.ds(land, HALO)])
                for a in range(2)
            ]
        elif dx == 0:
            pairs = [(packed.at[0 if dy < 0 else 1], side_in.at[0 if dy < 0 else 1])]
        else:
            pairs = [(
                packed.at[0 if dy < 0 else 1, 0 if dx < 0 else tiles - 1],
                corner_in.at[way - 4],
            )]
        return [
            pltpu.make_async_remote_copy(
                src_ref=one, dst_ref=two,
                send_sem=halo_send.at[way, a], recv_sem=halo_recv.at[way, a],
                device_id=(me_x + dx, me_y + dy), device_id_type=MESH,
            )
            for a, (one, two) in enumerate(pairs)
        ]

    def start(way, number=0):
        @pl.when(exists(*WAYS[way]))
        def _():
            halo_copies(way)[number].start()


    lane = lax.broadcasted_iota(jnp.int32, (levels, LANES), 1)

    def between(low, high, like):
        at = lax.broadcasted_iota(jnp.int32, (1,) * (len(like) - 1) + (LANES,), len(like) - 1)
        return (at >= low) & (at < high)

    def rolled(v, by):
        if isinstance(by, int):
            by = by % v.shape[-1]
            if by == 0:
                return v
        return pltpu.roll(v, by, v.ndim - 1)

    for load in loads:
        load.wait()

    def arrange(t):
        low = t * GROUP
        acc = [jnp.zeros((levels, LANES), jnp.float32)] * 2
        for a in range(2):
            block = jnp.transpose(fresh[a, :, low : low + GROUP, :], (1, 0, 2))
            field[a, HALO + low : HALO + low + GROUP] = block
            for side in range(2):
                offset = 0 if side == 0 else LANES - STRIP
                part = block[:, :, (0 if side == 0 else last) : (LANES if side == 0 else cols)]
                for g in range(GROUP):
                    place = (a * GROUP + g) * STRIP
                    moved = rolled(part[g], place - offset)
                    acc[side] = jnp.where(
                        (lane >= place) & (lane < place + STRIP), moved, acc[side]
                    )
        for side in range(2):
            packed[side, t] = acc[side]

    for t in sorted({0, tiles - 1}):
        arrange(t)
    pl.semaphore_wait(barrier, expected)
    for way in (4, 5, 6, 7):
        start(way)
    for number in range(2):
        for way in (0, 1):
            start(way, number)
    for t in range(1, tiles - 1):
        arrange(t)
    for way in (2, 3):
        start(way)
    if planes:
        relay()

    for way in range(8):
        dx, dy = WAYS[way]

        @pl.when(jnp.logical_not(exists(-dx, -dy)))
        def _():
            if dy == 0:
                x_in[:, 1 if dx < 0 else 0] = jnp.zeros((2, levels, GROUP, cols), jnp.float32)
            elif dx == 0:
                side_in[0 if dy < 0 else 1] = jnp.zeros((tiles, levels, LANES), jnp.float32)
            else:
                corner_in[way - 4] = jnp.zeros((levels, LANES), jnp.float32)

    def own_strips(a, state):
        for side in range(2):
            acc = jnp.zeros((GROUP, levels, LANES), jnp.float32)
            for g in range(1, tiles + 1):
                low = width * g + HALO * (1 - side)
                block = field[
                    a, HALO + (g - 1) * GROUP : HALO + g * GROUP, :,
                    (0 if side == 0 else last) : (LANES if side == 0 else cols),
                ]
                moved = rolled(block, low + 2 * HALO * side)
                acc = jnp.where(between(low, low + 2 * HALO, block.shape), moved, acc)
            sfield[a, side, 1 : 1 + GROUP] = acc
        return state

    lax.fori_loop(0, 2, own_strips, 0)

    def wrap(f, side):
        sfield[f, side, 0] = rolled(sfield[f, side, GROUP], width)
        sfield[f, side, GROUP + 1] = rolled(sfield[f, side, 1], -width)

    def level_of(shape):
        return lax.broadcasted_iota(jnp.int32, (1, levels, shape[-1]), 1)

    def faces(c, other):
        return jnp.where(jnp.minimum(c, other) > 0.0, 0.5 * (c + other), 0.0)

    def coefficients(low, n, beside):
        c = field[0, pl.ds(low, n)]
        level = level_of(c.shape)
        at = lax.broadcasted_iota(jnp.int32, (1, 1, cols), 2)
        half = 0.5 * c
        inner = jnp.logical_and(level > 0, level < levels - 1)
        kb = jnp.where(inner, 0.0, half)
        if beside:
            for other in (field[0, pl.ds(low - 1, n)], field[0, pl.ds(low + 1, n)]):
                kb = kb + jnp.where(other > 0.0, 0.0, half)
        ke = jnp.where(at < cols - 1, half + rolled(half, cols - 1), 0.0)
        kw = jnp.where(at > 0, half + rolled(half, 1), 0.0)
        kb = kb + (ke + kw)
        coef[1, pl.ds(low, n)] = ke
        coef[5, pl.ds(low, n)] = kw
        coef[2, pl.ds(low, n)] = jnp.where(
            level < levels - 1, half + pltpu.roll(half, levels - 1, 1), 0.0
        )
        coef[3, pl.ds(low, n)] = kb
        coef[4, pl.ds(low, n)] = kb + shift_1

    def strip_coefficients(side):
        c = sfield[0, side, 1 : 1 + GROUP]
        level = level_of(c.shape)
        half = 0.5 * c
        inner = jnp.logical_and(level > 0, level < levels - 1)
        east, west = rolled(c, LANES - 1), rolled(c, 1)
        kb = jnp.where(inner, 0.0, half)
        for other in (east, west, sfield[0, side, 0:GROUP], sfield[0, side, 2 : 2 + GROUP]):
            kb = kb + jnp.where(other > 0.0, 0.0, half)
        scoef[0, side, 0 : GROUP + 1] = faces(
            sfield[0, side, 0 : GROUP + 1], sfield[0, side, 1 : GROUP + 2]
        )
        ke, kw = faces(c, east), faces(c, west)
        kb = kb + (ke + kw)
        scoef[1, side, 1 : 1 + GROUP] = ke
        scoef[5, side, 1 : 1 + GROUP] = kw
        scoef[2, side, 1 : 1 + GROUP] = jnp.where(
            level < levels - 1, half + pltpu.roll(half, levels - 1, 1), 0.0
        )
        scoef[3, side, 1 : 1 + GROUP] = kb
        scoef[4, side, 1 : 1 + GROUP] = kb + shift_1

    def turned(read, low, n, j):
        v = read(j + 1, low, n)
        down, up = read(j + 1, low - 1, n), read(j + 1, low + 1, n)
        parts = [v[..., at : at + LANES] for at in range(0, v.shape[-1], LANES)]
        ons = [rolled(part, LANES - 1) for part in parts]
        backs = [rolled(part, 1) for part in parts]
        count = len(parts)
        east = [
            jnp.where(between(LANES - 1, LANES, v.shape), ons[i + 1], ons[i]) if i + 1 < count else ons[i]
            for i in range(count)
        ]
        west = [
            jnp.where(between(0, 1, v.shape), backs[i - 1], backs[i]) if i else backs[i]
            for i in range(count)
        ]
        east, west = (
            jnp.concatenate(x, axis=-1) if count > 1 else x[0] for x in (east, west)
        )
        return v, east, west, down, up

    def image(read, k, low, n, j, around):
        third = j % 3 if isinstance(j, int) else lax.rem(j, 3)
        shifted = 4 - (third + 1) // 2
        v, east, west, down, up = around
        axis = v.ndim - 1
        rows_of = jnp.concatenate([down[:1], v, up[n - 1 :]], axis=0)
        across = k(0, low - 1, n + 1) * (rows_of[: n + 1] - rows_of[1:])
        fz = k(2, low, n) * (v - pltpu.roll(v, levels - 1, axis - 1))
        rest = (across[1:] - across[:n]) + ((fz - pltpu.roll(fz, 1, axis - 1)) + k(shifted, low, n) * v)
        if not isinstance(j, int):
            also = jnp.where(third == 1, shift_0, 0.0)
            rest = rest + also * read(jnp.maximum(j, 1), low, n)
        elif third == 1:
            rest = rest + shift_0 * read(j, low, n)
        return rest - (k(1, low, n) * east + k(5, low, n) * west)

    def images(jobs, j):
        ahead = AHEAD
        around = [turned(read, low, n, j) for read, k, low, n, put in jobs[:ahead]]
        for i, (read, k, low, n, put) in enumerate(jobs):
            if i + ahead < len(jobs):
                other = jobs[i + ahead]
                around.append(turned(other[0], other[2], other[3], j))
            put(j + 2, low, n, image(read, k, low, n, j, around[i]))

    def main(f, low, n):
        return field[f, pl.ds(low, n)]

    def main_k(i, low, n):
        return coef[i, pl.ds(low, n)]

    def main_put(f, low, n, v):
        field[f, pl.ds(low, n)] = v

    def summed(read, low, n, state):
        r, p, w, m, q = (read(f, low, n) for f in (1, 3, 4, 6, 7))
        return tuple(
            s + jnp.sum(t, axis=0) for s, t in zip(state, (r * p, w * p, w * m, q * m))
        )

    STEP = 4

    WIDE = 2 * GROUP

    def own_coefficients(i, state):
        low = HALO + i * WIDE
        coefficients(low, WIDE, False)
        coef[0, pl.ds(low, WIDE)] = 0.5 * (
            field[0, pl.ds(low, WIDE)] + field[0, pl.ds(low + 1, WIDE)]
        )
        return state

    lax.fori_loop(0, rows // WIDE, own_coefficients, 0)

    def own_image(j, state):
        images([(main, main_k, HALO + low, STEP, main_put) for low in range(0, rows, STEP)], j)
        return state

    lax.fori_loop(0, 6, own_image, 0)
    zero = jnp.zeros((levels, cols), jnp.float32)
    acc = lax.fori_loop(
        0, (rows - 2 * HALO) // STEP,
        lambda i, state: summed(main, 2 * HALO + i * STEP, STEP, state), (zero,) * 4,
    )


    def arrived(ways, number):
        for way in ways:
            dx, dy = WAYS[way]

            @pl.when(exists(-dx, -dy))
            def _():
                halo_copies(way)[number].wait_recv()

    def strips_halo():
        arrived((2, 3, 4, 5, 6, 7), 0)
        for a in range(2):
            for side in range(2):
                for i in range(GROUP):
                    out = sfield[a, side, 1 + i]
                    for g in range(groups):
                        if g == 0:
                            if i < GROUP - HALO:
                                continue
                            tile = corner_in[3 - side]
                        elif g == groups - 1:
                            if i >= HALO:
                                continue
                            tile = corner_in[1 - side]
                        else:
                            tile = side_in[1 - side, g - 1]
                        low = width * g + 2 * HALO * side
                        by = low - i * STRIP - (STRIP - HALO) * (1 - side)
                        moved = rolled(tile, by - a * (GROUP * STRIP))
                        out = jnp.where((lane >= low) & (lane < low + HALO), moved, out)
                    sfield[a, side, 1 + i] = out

    def edges(i):
        low = 1 + i * (HALO + rows - 2)
        coefficients(low, HALO, True)
        first = low - 1 + i
        coef[0, pl.ds(first, HALO)] = faces(
            field[0, pl.ds(first, HALO)], field[0, pl.ds(first + 1, HALO)]
        )

    for a in range(2):
        arrived((0, 1), a)
        lower = jnp.transpose(x_in[a, 0], (1, 0, 2))[GROUP - HALO : GROUP]
        upper = jnp.transpose(x_in[a, 1], (1, 0, 2))[0:HALO]
        field[a, 0:HALO] = lower
        field[a, HALO + rows : HALO + rows + HALO] = upper
        for side in range(2):
            edge = (0, LANES) if side == 0 else (last, cols)
            for g, block, slot in ((0, lower, GROUP - HALO), (groups - 1, upper, 0)):
                low = width * g + HALO * (1 - side)
                moved = rolled(block[:, :, edge[0] : edge[1]], low + 2 * HALO * side)
                slots_of = pl.ds(1 + slot, HALO)
                sfield[a, side, slots_of] = jnp.where(
                    between(low, low + 2 * HALO, moved.shape), moved, sfield[a, side, slots_of]
                )
        if a == 0:
            for i in range(2):
                edges(i)
            strips_halo()
        for side in range(2):
            wrap(a, side)
            if a == 0:
                strip_coefficients(side)

    PART = 6
    HALF = GROUP // 2

    def strip_job(side, low):
        def read(f, at, n):
            if at == 0:
                first = rolled(sfield[f, side, pl.ds(GROUP, 1)], width)
                return jnp.concatenate([first, sfield[f, side, pl.ds(1, n - 1)]], axis=0)
            if at + n == GROUP + 2:
                last_row = rolled(sfield[f, side, pl.ds(1, 1)], -width)
                return jnp.concatenate([sfield[f, side, pl.ds(at, n - 1)], last_row], axis=0)
            return sfield[f, side, pl.ds(at, n)]

        def k(i, at, n):
            return scoef[i, side, pl.ds(at, n)]

        def put(f, at, n, v):
            sfield[f, side, pl.ds(at, n)] = v

        return read, k, low, HALF, put

    def edge_image(j):
        jobs = []
        for base in (j + 1, rows - 1 - j + HALO):
            jobs += [(main, main_k, low, PART, main_put) for low in (base,)]
        strips = [strip_job(side, low) for side in range(2) for low in (1, 1 + HALF)]
        images(jobs + strips, j)

    for j in range(6):
        edge_image(j)
    for base in (HALO, rows):
        for low in (base,):
            acc = summed(main, low, PART, acc)
    sacc = (jnp.zeros((levels, LANES), jnp.float32),) * 4
    for side in range(2):
        sacc = summed(lambda f, low, n: sfield[f, side, pl.ds(low, n)], 1, GROUP, sacc)

    in_strip = jnp.zeros((levels, LANES), jnp.bool_)
    for g in range(1, tiles + 1):
        low = width * g + HALO
        in_strip = jnp.logical_or(in_strip, (lane >= low) & (lane < low + HALO))
    message = jnp.zeros((levels, LANES), jnp.float32)
    share = LANES // 4
    for i in range(4):
        s = jnp.where(in_strip, sacc[i], 0.0)
        for low in range(0, cols, LANES):
            part = acc[i][:, low : low + LANES]
            if low == 0:
                part = jnp.where(lane >= HALO, part, 0.0)
            if low == last:
                part = jnp.where(lane < LANES - HALO, part, 0.0)
            s = s + part
        s = (s + rolled(s, share)) + (rolled(s, 2 * share) + rolled(s, 3 * share))
        message = jnp.where((lane >= i * share) & (lane < (i + 1) * share), s, message)
    total = jnp.sum(message, axis=0, keepdims=True)

    def finish(t, state):
        low = pl.multiple_of(t * GROUP, GROUP)
        for f, out in ((3, p_out), (4, w_out), (6, m_out), (7, n_out)):
            block = field[f, pl.ds(HALO + low, GROUP)]
            parts = [block[:, :, k : k + LANES] for k in range(0, cols, LANES)]
            for side in range(2):
                strip = sfield[f, side, 1 : 1 + GROUP]
                to = 0 if side == 0 else LANES - HALO
                part = 0 if side == 0 else len(parts) - 1
                by = lax.rem(to - HALO - width + 2 * LANES - width * t, LANES)
                parts[part] = jnp.where(
                    between(to, to + HALO, strip.shape), rolled(strip, by), parts[part]
                )
            for k, part in enumerate(parts):
                out[:, pl.ds(low, GROUP), k * LANES : (k + 1) * LANES] = jnp.transpose(
                    part, (1, 0, 2)
                )
        return state

    if planes:
        relay_wait()
    base = 0
    sent = []
    for index, stage in enumerate(stages):
        count = stage[0] * stage[1]
        mine = base + place_in(stage)[0]
        slots[pl.ds(mine, 1), :] = total

        def send(device):
            pltpu.make_async_remote_copy(
                src_ref=slots.at[pl.ds(mine, 1)], dst_ref=slots.at[pl.ds(mine, 1)],
                send_sem=red_send.at[index], recv_sem=red_recv.at[index],
                device_id=device, device_id_type=LOGICAL,
            ).start()

        each_other(stage, send)
        if index == 0:
            lax.fori_loop(0, tiles, finish, 0)
            r_out[...] = fresh[1]
            for way in range(8):

                @pl.when(exists(*WAYS[way]))
                def _():
                    for copy in halo_copies(way):
                        copy.wait_send()

        if count > 1:
            whole = slots.at[pl.ds(base, count - 1)]
            pltpu.make_async_copy(whole, whole, red_recv.at[index]).wait()
            sent.append((whole, red_send.at[index]))
        total = jnp.sum(slots[base : base + count], axis=0, keepdims=True)
        base += -(-count // 8) * 8
    sums_out[...] = total
    for whole, sem in sent:
        pltpu.make_async_copy(whole, whole, sem).wait()


def combine(p, w, m, n, r, sums, x_hbm, res_hbm, x_vmem, res_vmem, sem):
    levels = p.shape[0]
    total = sums[...]
    lane = lax.broadcasted_iota(jnp.int32, total.shape, 1)
    share = LANES // 4

    def of(i, scale):
        chosen = (lane >= i * share) & (lane < (i + 1) * share)
        return scale * jnp.sum(jnp.where(chosen, total, 0.0), axis=1, keepdims=True)

    rp, wp, wm, nm = (of(i, power_2 ** (i + 1)) for i in range(4))
    gamma_old = rp
    alpha_old = gamma_old / wp
    gamma = (rp - alpha_old * wp) - alpha_old * (wp - alpha_old * wm)
    delta = (wp - alpha_old * wm) - alpha_old * (wm - alpha_old * nm)
    beta = gamma / gamma_old
    alpha = gamma / (delta - beta * gamma / alpha_old)
    near = power_2 * (alpha_old + alpha * (1.0 + beta))
    far = (power_2 * power_2) * (alpha * alpha_old)
    copies = []
    for z in range(levels):
        x_vmem[z] = near * p[z] - far * m[z]
        res_vmem[z] = (r[z] - near * w[z]) + far * n[z]
        for a, (one, two) in enumerate(((x_vmem, x_hbm), (res_vmem, res_hbm))):
            copies.append(pltpu.make_async_copy(one.at[z], two.at[z], sem.at[a]))
            copies[-1].start()
    for a, (one, two) in enumerate(((x_vmem, x_hbm), (res_vmem, res_hbm))):
        pltpu.make_async_copy(one, two, sem.at[a]).wait()


def solution(mesh):
    num_x, num_y = mesh.shape["gx"], mesh.shape["gy"]

    def per_device(right_side, conductivity):
        levels, rows, cols = right_side.shape
        high = rows + 2 * HALO
        tiles = rows // GROUP
        stages = stages_of(num_x, num_y)
        deep = sum(-(-(a * b) // 8) * 8 for a, b in stages)

        def body(*refs):
            kernel(num_x, num_y, *refs)

        block = (levels, rows, cols)
        full = (high, levels, cols)
        slim = (2, GROUP + 2, levels, LANES)
        out = jax.ShapeDtypeStruct(block, jnp.float32)
        sums = jax.ShapeDtypeStruct((1, LANES), jnp.float32)
        vmem = lambda shape: pltpu.VMEM(shape, jnp.float32)
        dma = lambda *n: pltpu.SemaphoreType.DMA(n)
        in_vmem = pl.BlockSpec(memory_space=pltpu.VMEM)
        in_hbm = pl.BlockSpec(memory_space=pltpu.HBM)
        parts = pl.pallas_call(
            body,
            out_shape=(out,) * 5 + (sums,),
            in_specs=[in_hbm] * 2,
            out_specs=(in_vmem,) * 6,
            scratch_shapes=[
                vmem((2,) + block), vmem((2, 2, levels, GROUP, cols)),
                vmem((6,) + full), vmem((6,) + slim), vmem((8,) + full), vmem((8,) + slim),
                vmem((2, tiles, levels, LANES)), vmem((2, tiles, levels, LANES)),
                vmem((4, levels, LANES)), vmem((deep, LANES)),
                dma(2), dma(8, 2), dma(8, 2), dma(len(stages)), dma(len(stages)),
                pltpu.SemaphoreType.REGULAR,
            ],
            compiler_params=pltpu.CompilerParams(
                collective_id=0, has_side_effects=True, vmem_limit_bytes=55000000
            ),
        )(right_side, conductivity)
        return pl.pallas_call(
            combine,
            out_shape=(out, out),
            in_specs=[in_vmem] * 6,
            out_specs=(in_hbm,) * 2,
            scratch_shapes=[vmem(block), vmem(block), dma(2)],
            compiler_params=pltpu.CompilerParams(vmem_limit_bytes=4000000),
        )(*parts)

    return jax.shard_map(
        per_device,
        mesh=mesh,
        in_specs=(P(None, "gx", "gy"), P(None, "gx", "gy")),
        out_specs=(P(None, "gx", "gy"), P(None, "gx", "gy")),
        check_vma=False,
    )
```

```python
import jax
import jax.numpy as jnp
from jax import lax
from jax.experimental import pallas as pl
from jax.experimental.pallas import tpu as pltpu
from jax.sharding import PartitionSpec as P

low_bound = 0.4
high_bound = 12.0
cheb_theta = 0.5 * (high_bound + low_bound)
cheb_delta = 0.5 * (high_bound - low_bound)
cheb_sigma = cheb_theta / cheb_delta
rho_first = 1.0 / cheb_sigma
rho_second = 1.0 / (2.0 * cheb_sigma - rho_first)
rho_third = 1.0 / (2.0 * cheb_sigma - rho_second)

step_0 = rho_second * rho_first / cheb_theta + 2.0 * rho_second / cheb_delta
step_1 = 2.0 * rho_second / cheb_delta / cheb_theta
mix_0 = 1.0 + rho_third * rho_second
mix_1 = 2.0 * rho_third / cheb_delta
power_0 = 1.0 / cheb_theta + mix_0 * step_0 + mix_1
power_1 = -mix_0 * step_1 - mix_1 / cheb_theta - mix_1 * step_0
power_2 = mix_1 * step_1
shift_1 = power_1 / power_2
shift_0 = power_0 / power_2

HALO = 6
AHEAD = 2
PLANE = 2
LANES = 128
STRIP = 8
GROUP = 8
ONE_STAGE = 64
MESH = pl.DeviceIdType.MESH
LOGICAL = pl.DeviceIdType.LOGICAL
WAYS = ((-1, 0), (1, 0), (0, -1), (0, 1), (-1, -1), (-1, 1), (1, -1), (1, 1))


def stages_of(num_x, num_y):
    if num_x * num_y <= ONE_STAGE:
        return ((num_x, num_y),)
    return ((num_x, 1), (1, num_y))


def kernel(
    num_x, num_y, r_hbm, c_hbm, p_out, w_out, m_out, n_out, r_out, sums_out,
    fresh, x_in, coef, scoef, field, sfield, packed, side_in, corner_in, slots,
    in_sem, halo_send, halo_recv, red_send, red_recv, relayed,
):
    _, levels, rows, cols = fresh.shape
    tiles = rows // GROUP
    groups = tiles + 2
    width = LANES // groups
    last = cols - LANES
    me_x = lax.axis_index("gx")
    me_y = lax.axis_index("gy")
    stages = stages_of(num_x, num_y)

    def exists(dx, dy):
        ok = jnp.bool_(True)
        if dx < 0:
            ok = me_x > 0
        if dx > 0:
            ok = me_x < num_x - 1
        if dy < 0:
            ok_y = me_y > 0
            ok = ok_y if dx == 0 else jnp.logical_and(ok, ok_y)
        if dy > 0:
            ok_y = me_y < num_y - 1
            ok = ok_y if dx == 0 else jnp.logical_and(ok, ok_y)
        return ok

    loads = [
        pltpu.make_async_copy(ref, fresh.at[a], in_sem.at[a])
        for a, ref in enumerate((c_hbm, r_hbm))
    ]
    for load in loads:
        load.start()

    def place_in(stage):
        count_x, count_y = stage
        if count_x > 1 and count_y > 1:
            return me_x * num_y + me_y, lambda o: o
        if count_x > 1:
            return me_x, lambda o: o * num_y + me_y
        return me_y, lambda o: me_x * num_y + o

    def each_other(stage, act):
        mine, device = place_in(stage)
        total = stage[0] * stage[1]

        flip = mine < total // 2
        start_at = jnp.where(flip, total - 1 - mine, mine)

        def step(k, state):
            other = jnp.where(k > start_at, k, k - 1)
            act(device(jnp.where(flip, total - 1 - other, other)))
            return state

        lax.fori_loop(1, total, step, 0)

    barrier = pltpu.get_barrier_semaphore()

    def greet(device):
        pl.semaphore_signal(barrier, inc=1, device_id=device, device_id_type=LOGICAL)

    planes = len(stages) == 1 and num_x % PLANE == 0
    plane = me_x // PLANE * PLANE
    expected = jnp.int32(0)
    if planes:
        mine = me_x * num_y + me_y
        begin = me_x == plane

        for dy in (0, -1, 1):
            down = jnp.logical_and(begin, exists(-1, dy))
            up = jnp.logical_and(me_x == plane + PLANE - 1, exists(1, dy))

            @pl.when(down)
            def _():
                greet(mine - num_y + dy)

            expected = expected + up.astype(jnp.int32)

        def onward(other, state):
            @pl.when(other != mine)
            def _():
                greet(other)

            return state

        lax.fori_loop(plane * num_y, num_x * num_y, onward, 0)
        expected = expected + ((plane + PLANE) * num_y - 1)
    else:
        for stage in stages:
            each_other(stage, greet)
            expected = expected + (stage[0] * stage[1] - 1)
    if len(stages) > 1:
        for dx, dy in WAYS[4:]:
            ok = exists(dx, dy)

            @pl.when(ok)
            def _():
                greet((me_x + dx) * num_y + me_y + dy)

            expected = expected + ok.astype(jnp.int32)

    def relay():
        def tell(k, state):
            pl.semaphore_signal(
                relayed, inc=1, device_id=(me_x - k * PLANE) * num_y + me_y, device_id_type=LOGICAL
            )
            return state

        lax.fori_loop(1, me_x // PLANE + 1, tell, 0)

    def relay_wait():
        @pl.when(me_x < num_x - PLANE)
        def _():
            pl.semaphore_wait(relayed, (num_x - 1 - me_x) // PLANE)

    def halo_copies(way):
        dx, dy = WAYS[way]
        if dy == 0:
            side = 1 if dx < 0 else 0
            low = 0 if dx < 0 else rows - HALO
            land = 0 if dx < 0 else GROUP - HALO
            pairs = [
                (fresh.at[a, :, pl.ds(low, HALO)], x_in.at[a, side, :, pl.ds(land, HALO)])
                for a in range(2)
            ]
        elif dx == 0:
            pairs = [(packed.at[0 if dy < 0 else 1], side_in.at[0 if dy < 0 else 1])]
        else:
            pairs = [(
                packed.at[0 if dy < 0 else 1, 0 if dx < 0 else tiles - 1],
                corner_in.at[way - 4],
            )]
        return [
            pltpu.make_async_remote_copy(
                src_ref=one, dst_ref=two,
                send_sem=halo_send.at[way, a], recv_sem=halo_recv.at[way, a],
                device_id=(me_x + dx, me_y + dy), device_id_type=MESH,
            )
            for a, (one, two) in enumerate(pairs)
        ]

    def start(way, number=0):
        @pl.when(exists(*WAYS[way]))
        def _():
            halo_copies(way)[number].start()


    lane = lax.broadcasted_iota(jnp.int32, (levels, LANES), 1)

    def between(low, high, like):
        at = lax.broadcasted_iota(jnp.int32, (1,) * (len(like) - 1) + (LANES,), len(like) - 1)
        return (at >= low) & (at < high)

    def rolled(v, by):
        if isinstance(by, int):
            by = by % v.shape[-1]
            if by == 0:
                return v
        return pltpu.roll(v, by, v.ndim - 1)

    for load in loads:
        load.wait()

    def arrange(t):
        low = t * GROUP
        acc = [jnp.zeros((levels, LANES), jnp.float32)] * 2
        for a in range(2):
            block = jnp.transpose(fresh[a, :, low : low + GROUP, :], (1, 0, 2))
            field[a, HALO + low : HALO + low + GROUP] = block
            for side in range(2):
                offset = 0 if side == 0 else LANES - STRIP
                part = block[:, :, (0 if side == 0 else last) : (LANES if side == 0 else cols)]
                for g in range(GROUP):
                    place = (a * GROUP + g) * STRIP
                    moved = rolled(part[g], place - offset)
                    acc[side] = jnp.where(
                        (lane >= place) & (lane < place + STRIP), moved, acc[side]
                    )
        for side in range(2):
            packed[side, t] = acc[side]

    for t in sorted({0, tiles - 1}):
        arrange(t)
    pl.semaphore_wait(barrier, expected)
    for way in (4, 5, 6, 7):
        start(way)
    for number in range(2):
        for way in (0, 1):
            start(way, number)
    for t in range(1, tiles - 1):
        arrange(t)
    for way in (2, 3):
        start(way)
    if planes:
        relay()

    for way in range(8):
        dx, dy = WAYS[way]

        @pl.when(jnp.logical_not(exists(-dx, -dy)))
        def _():
            if dy == 0:
                x_in[:, 1 if dx < 0 else 0] = jnp.zeros((2, levels, GROUP, cols), jnp.float32)
            elif dx == 0:
                side_in[0 if dy < 0 else 1] = jnp.zeros((tiles, levels, LANES), jnp.float32)
            else:
                corner_in[way - 4] = jnp.zeros((levels, LANES), jnp.float32)

    def own_strips(a, state):
        for side in range(2):
            acc = jnp.zeros((GROUP, levels, LANES), jnp.float32)
            for g in range(1, tiles + 1):
                low = width * g + HALO * (1 - side)
                block = field[
                    a, HALO + (g - 1) * GROUP : HALO + g * GROUP, :,
                    (0 if side == 0 else last) : (LANES if side == 0 else cols),
                ]
                moved = rolled(block, low + 2 * HALO * side)
                acc = jnp.where(between(low, low + 2 * HALO, block.shape), moved, acc)
            sfield[a, side, 1 : 1 + GROUP] = acc
        return state

    lax.fori_loop(0, 2, own_strips, 0)

    def wrap(f, side):
        sfield[f, side, 0] = rolled(sfield[f, side, GROUP], width)
        sfield[f, side, GROUP + 1] = rolled(sfield[f, side, 1], -width)

    def level_of(shape):
        return lax.broadcasted_iota(jnp.int32, (1, levels, shape[-1]), 1)

    def faces(c, other):
        return jnp.where(jnp.minimum(c, other) > 0.0, 0.5 * (c + other), 0.0)

    def coefficients(low, n, beside):
        c = field[0, pl.ds(low, n)]
        level = level_of(c.shape)
        at = lax.broadcasted_iota(jnp.int32, (1, 1, cols), 2)
        half = 0.5 * c
        inner = jnp.logical_and(level > 0, level < levels - 1)
        kb = jnp.where(inner, 0.0, half)
        if beside:
            for other in (field[0, pl.ds(low - 1, n)], field[0, pl.ds(low + 1, n)]):
                kb = kb + jnp.where(other > 0.0, 0.0, half)
        ke = jnp.where(at < cols - 1, half + rolled(half, cols - 1), 0.0)
        kw = jnp.where(at > 0, half + rolled(half, 1), 0.0)
        kb = kb + (ke + kw)
        coef[1, pl.ds(low, n)] = ke
        coef[5, pl.ds(low, n)] = kw
        coef[2, pl.ds(low, n)] = jnp.where(
            level < levels - 1, half + pltpu.roll(half, levels - 1, 1), 0.0
        )
        coef[3, pl.ds(low, n)] = kb
        coef[4, pl.ds(low, n)] = kb + shift_1

    def strip_coefficients(side):
        c = sfield[0, side, 1 : 1 + GROUP]
        level = level_of(c.shape)
        half = 0.5 * c
        inner = jnp.logical_and(level > 0, level < levels - 1)
        east, west = rolled(c, LANES - 1), rolled(c, 1)
        kb = jnp.where(inner, 0.0, half)
        for other in (east, west, sfield[0, side, 0:GROUP], sfield[0, side, 2 : 2 + GROUP]):
            kb = kb + jnp.where(other > 0.0, 0.0, half)
        scoef[0, side, 0 : GROUP + 1] = faces(
            sfield[0, side, 0 : GROUP + 1], sfield[0, side, 1 : GROUP + 2]
        )
        ke, kw = faces(c, east), faces(c, west)
        kb = kb + (ke + kw)
        scoef[1, side, 1 : 1 + GROUP] = ke
        scoef[5, side, 1 : 1 + GROUP] = kw
        scoef[2, side, 1 : 1 + GROUP] = jnp.where(
            level < levels - 1, half + pltpu.roll(half, levels - 1, 1), 0.0
        )
        scoef[3, side, 1 : 1 + GROUP] = kb
        scoef[4, side, 1 : 1 + GROUP] = kb + shift_1

    def turned(read, low, n, j):
        v = read(j + 1, low, n)
        down, up = read(j + 1, low - 1, n), read(j + 1, low + 1, n)
        parts = [v[..., at : at + LANES] for at in range(0, v.shape[-1], LANES)]
        ons = [rolled(part, LANES - 1) for part in parts]
        backs = [rolled(part, 1) for part in parts]
        count = len(parts)
        east = [
            jnp.where(between(LANES - 1, LANES, v.shape), ons[i + 1], ons[i]) if i + 1 < count else ons[i]
            for i in range(count)
        ]
        west = [
            jnp.where(between(0, 1, v.shape), backs[i - 1], backs[i]) if i else backs[i]
            for i in range(count)
        ]
        east, west = (
            jnp.concatenate(x, axis=-1) if count > 1 else x[0] for x in (east, west)
        )
        return v, east, west, down, up

    def image(read, k, low, n, j, around):
        third = j % 3 if isinstance(j, int) else lax.rem(j, 3)
        shifted = 4 - (third + 1) // 2
        v, east, west, down, up = around
        axis = v.ndim - 1
        rows_of = jnp.concatenate([down[:1], v, up[n - 1 :]], axis=0)
        across = k(0, low - 1, n + 1) * (rows_of[: n + 1] - rows_of[1:])
        fz = k(2, low, n) * (v - pltpu.roll(v, levels - 1, axis - 1))
        rest = (across[1:] - across[:n]) + ((fz - pltpu.roll(fz, 1, axis - 1)) + k(shifted, low, n) * v)
        if not isinstance(j, int):
            also = jnp.where(third == 1, shift_0, 0.0)
            rest = rest + also * read(jnp.maximum(j, 1), low, n)
        elif third == 1:
            rest = rest + shift_0 * read(j, low, n)
        return rest - (k(1, low, n) * east + k(5, low, n) * west)

    def images(jobs, j):
        ahead = AHEAD
        around = [turned(read, low, n, j) for read, k, low, n, put in jobs[:ahead]]
        for i, (read, k, low, n, put) in enumerate(jobs):
            if i + ahead < len(jobs):
                other = jobs[i + ahead]
                around.append(turned(other[0], other[2], other[3], j))
            put(j + 2, low, n, image(read, k, low, n, j, around[i]))

    def main(f, low, n):
        return field[f, pl.ds(low, n)]

    def main_k(i, low, n):
        return coef[i, pl.ds(low, n)]

    def main_put(f, low, n, v):
        field[f, pl.ds(low, n)] = v

    def summed(read, low, n, state):
        r, p, w, m, q = (read(f, low, n) for f in (1, 3, 4, 6, 7))
        return tuple(
            s + jnp.sum(t, axis=0) for s, t in zip(state, (r * p, w * p, w * m, q * m))
        )

    STEP = 4

    WIDE = 2 * GROUP

    def own_coefficients(i, state):
        low = HALO + i * WIDE
        coefficients(low, WIDE, False)
        coef[0, pl.ds(low, WIDE)] = 0.5 * (
            field[0, pl.ds(low, WIDE)] + field[0, pl.ds(low + 1, WIDE)]
        )
        return state

    lax.fori_loop(0, rows // WIDE, own_coefficients, 0)

    def own_image(j, state):
        images([(main, main_k, HALO + low, STEP, main_put) for low in range(0, rows, STEP)], j)
        return state

    lax.fori_loop(0, 6, own_image, 0)
    zero = jnp.zeros((levels, cols), jnp.float32)
    acc = lax.fori_loop(
        0, (rows - 2 * HALO) // STEP,
        lambda i, state: summed(main, 2 * HALO + i * STEP, STEP, state), (zero,) * 4,
    )


    def arrived(ways, number):
        for way in ways:
            dx, dy = WAYS[way]

            @pl.when(exists(-dx, -dy))
            def _():
                halo_copies(way)[number].wait_recv()

    def strips_halo():
        arrived((2, 3, 4, 5, 6, 7), 0)
        for a in range(2):
            for side in range(2):
                for i in range(GROUP):
                    out = sfield[a, side, 1 + i]
                    for g in range(groups):
                        if g == 0:
                            if i < GROUP - HALO:
                                continue
                            tile = corner_in[3 - side]
                        elif g == groups - 1:
                            if i >= HALO:
                                continue
                            tile = corner_in[1 - side]
                        else:
                            tile = side_in[1 - side, g - 1]
                        low = width * g + 2 * HALO * side
                        by = low - i * STRIP - (STRIP - HALO) * (1 - side)
                        moved = rolled(tile, by - a * (GROUP * STRIP))
                        out = jnp.where((lane >= low) & (lane < low + HALO), moved, out)
                    sfield[a, side, 1 + i] = out

    def edges(i):
        low = 1 + i * (HALO + rows - 2)
        coefficients(low, HALO, True)
        first = low - 1 + i
        coef[0, pl.ds(first, HALO)] = faces(
            field[0, pl.ds(first, HALO)], field[0, pl.ds(first + 1, HALO)]
        )

    for a in range(2):
        arrived((0, 1), a)
        lower = jnp.transpose(x_in[a, 0], (1, 0, 2))[GROUP - HALO : GROUP]
        upper = jnp.transpose(x_in[a, 1], (1, 0, 2))[0:HALO]
        field[a, 0:HALO] = lower
        field[a, HALO + rows : HALO + rows + HALO] = upper
        for side in range(2):
            edge = (0, LANES) if side == 0 else (last, cols)
            for g, block, slot in ((0, lower, GROUP - HALO), (groups - 1, upper, 0)):
                low = width * g + HALO * (1 - side)
                moved = rolled(block[:, :, edge[0] : edge[1]], low + 2 * HALO * side)
                slots_of = pl.ds(1 + slot, HALO)
                sfield[a, side, slots_of] = jnp.where(
                    between(low, low + 2 * HALO, moved.shape), moved, sfield[a, side, slots_of]
                )
        if a == 0:
            for i in range(2):
                edges(i)
    strips_halo()
    for side in range(2):
        wrap(0, side)
        strip_coefficients(side)
        wrap(1, side)

    PART = 6
    HALF = GROUP // 2

    def strip_job(side, low):
        def read(f, at, n):
            if at == 0:
                first = rolled(sfield[f, side, pl.ds(GROUP, 1)], width)
                return jnp.concatenate([first, sfield[f, side, pl.ds(1, n - 1)]], axis=0)
            if at + n == GROUP + 2:
                last_row = rolled(sfield[f, side, pl.ds(1, 1)], -width)
                return jnp.concatenate([sfield[f, side, pl.ds(at, n - 1)], last_row], axis=0)
            return sfield[f, side, pl.ds(at, n)]

        def k(i, at, n):
            return scoef[i, side, pl.ds(at, n)]

        def put(f, at, n, v):
            sfield[f, side, pl.ds(at, n)] = v

        return read, k, low, HALF, put

    def edge_image(j):
        jobs = []
        for base in (j + 1, rows - 1 - j + HALO):
            jobs += [(main, main_k, low, PART, main_put) for low in (base,)]
        strips = [strip_job(side, low) for side in range(2) for low in (1, 1 + HALF)]
        images(jobs + strips, j)

    for j in range(6):
        edge_image(j)
    for base in (HALO, rows):
        for low in (base,):
            acc = summed(main, low, PART, acc)
    sacc = (jnp.zeros((levels, LANES), jnp.float32),) * 4
    for side in range(2):
        sacc = summed(lambda f, low, n: sfield[f, side, pl.ds(low, n)], 1, GROUP, sacc)

    in_strip = jnp.zeros((levels, LANES), jnp.bool_)
    for g in range(1, tiles + 1):
        low = width * g + HALO
        in_strip = jnp.logical_or(in_strip, (lane >= low) & (lane < low + HALO))
    message = jnp.zeros((levels, LANES), jnp.float32)
    share = LANES // 4
    for i in range(4):
        s = jnp.where(in_strip, sacc[i], 0.0)
        for low in range(0, cols, LANES):
            part = acc[i][:, low : low + LANES]
            if low == 0:
                part = jnp.where(lane >= HALO, part, 0.0)
            if low == last:
                part = jnp.where(lane < LANES - HALO, part, 0.0)
            s = s + part
        s = (s + rolled(s, share)) + (rolled(s, 2 * share) + rolled(s, 3 * share))
        message = jnp.where((lane >= i * share) & (lane < (i + 1) * share), s, message)
    total = jnp.sum(message, axis=0, keepdims=True)

    def finish(t, state):
        low = pl.multiple_of(t * GROUP, GROUP)
        for f, out in ((3, p_out), (4, w_out), (6, m_out), (7, n_out)):
            block = field[f, pl.ds(HALO + low, GROUP)]
            parts = [block[:, :, k : k + LANES] for k in range(0, cols, LANES)]
            for side in range(2):
                strip = sfield[f, side, 1 : 1 + GROUP]
                to = 0 if side == 0 else LANES - HALO
                part = 0 if side == 0 else len(parts) - 1
                by = lax.rem(to - HALO - width + 2 * LANES - width * t, LANES)
                parts[part] = jnp.where(
                    between(to, to + HALO, strip.shape), rolled(strip, by), parts[part]
                )
            for k, part in enumerate(parts):
                out[:, pl.ds(low, GROUP), k * LANES : (k + 1) * LANES] = jnp.transpose(
                    part, (1, 0, 2)
                )
        return state

    if planes:
        relay_wait()
    base = 0
    sent = []
    for index, stage in enumerate(stages):
        count = stage[0] * stage[1]
        mine = base + place_in(stage)[0]
        slots[pl.ds(mine, 1), :] = total

        def send(device):
            pltpu.make_async_remote_copy(
                src_ref=slots.at[pl.ds(mine, 1)], dst_ref=slots.at[pl.ds(mine, 1)],
                send_sem=red_send.at[index], recv_sem=red_recv.at[index],
                device_id=device, device_id_type=LOGICAL,
            ).start()

        each_other(stage, send)
        if index == 0:
            lax.fori_loop(0, tiles, finish, 0)
            r_out[...] = fresh[1]
            for way in range(8):

                @pl.when(exists(*WAYS[way]))
                def _():
                    for copy in halo_copies(way):
                        copy.wait_send()

        if count > 1:
            whole = slots.at[pl.ds(base, count - 1)]
            pltpu.make_async_copy(whole, whole, red_recv.at[index]).wait()
            sent.append((whole, red_send.at[index]))
        total = jnp.sum(slots[base : base + count], axis=0, keepdims=True)
        base += -(-count // 8) * 8
    sums_out[...] = total
    for whole, sem in sent:
        pltpu.make_async_copy(whole, whole, sem).wait()


def combine(p, w, m, n, r, sums, x_hbm, res_hbm, x_vmem, res_vmem, sem):
    levels = p.shape[0]
    total = sums[...]
    lane = lax.broadcasted_iota(jnp.int32, total.shape, 1)
    share = LANES // 4

    def of(i, scale):
        chosen = (lane >= i * share) & (lane < (i + 1) * share)
        return scale * jnp.sum(jnp.where(chosen, total, 0.0), axis=1, keepdims=True)

    rp, wp, wm, nm = (of(i, power_2 ** (i + 1)) for i in range(4))
    gamma_old = rp
    alpha_old = gamma_old / wp
    gamma = (rp - alpha_old * wp) - alpha_old * (wp - alpha_old * wm)
    delta = (wp - alpha_old * wm) - alpha_old * (wm - alpha_old * nm)
    beta = gamma / gamma_old
    alpha = gamma / (delta - beta * gamma / alpha_old)
    near = power_2 * (alpha_old + alpha * (1.0 + beta))
    far = (power_2 * power_2) * (alpha * alpha_old)
    copies = []
    for z in range(levels):
        x_vmem[z] = near * p[z] - far * m[z]
        res_vmem[z] = (r[z] - near * w[z]) + far * n[z]
        for a, (one, two) in enumerate(((x_vmem, x_hbm), (res_vmem, res_hbm))):
            copies.append(pltpu.make_async_copy(one.at[z], two.at[z], sem.at[a]))
            copies[-1].start()
    for a, (one, two) in enumerate(((x_vmem, x_hbm), (res_vmem, res_hbm))):
        pltpu.make_async_copy(one, two, sem.at[a]).wait()


def solution(mesh):
    num_x, num_y = mesh.shape["gx"], mesh.shape["gy"]

    def per_device(right_side, conductivity):
        levels, rows, cols = right_side.shape
        high = rows + 2 * HALO
        tiles = rows // GROUP
        stages = stages_of(num_x, num_y)
        deep = sum(-(-(a * b) // 8) * 8 for a, b in stages)

        def body(*refs):
            kernel(num_x, num_y, *refs)

        block = (levels, rows, cols)
        full = (high, levels, cols)
        slim = (2, GROUP + 2, levels, LANES)
        out = jax.ShapeDtypeStruct(block, jnp.float32)
        sums = jax.ShapeDtypeStruct((1, LANES), jnp.float32)
        vmem = lambda shape: pltpu.VMEM(shape, jnp.float32)
        dma = lambda *n: pltpu.SemaphoreType.DMA(n)
        in_vmem = pl.BlockSpec(memory_space=pltpu.VMEM)
        in_hbm = pl.BlockSpec(memory_space=pltpu.HBM)
        parts = pl.pallas_call(
            body,
            out_shape=(out,) * 5 + (sums,),
            in_specs=[in_hbm] * 2,
            out_specs=(in_vmem,) * 6,
            scratch_shapes=[
                vmem((2,) + block), vmem((2, 2, levels, GROUP, cols)),
                vmem((6,) + full), vmem((6,) + slim), vmem((8,) + full), vmem((8,) + slim),
                vmem((2, tiles, levels, LANES)), vmem((2, tiles, levels, LANES)),
                vmem((4, levels, LANES)), vmem((deep, LANES)),
                dma(2), dma(8, 2), dma(8, 2), dma(len(stages)), dma(len(stages)),
                pltpu.SemaphoreType.REGULAR,
            ],
            compiler_params=pltpu.CompilerParams(
                collective_id=0, has_side_effects=True, vmem_limit_bytes=55000000
            ),
        )(right_side, conductivity)
        return pl.pallas_call(
            combine,
            out_shape=(out, out),
            in_specs=[in_vmem] * 6,
            out_specs=(in_hbm,) * 2,
            scratch_shapes=[vmem(block), vmem(block), dma(2)],
            compiler_params=pltpu.CompilerParams(vmem_limit_bytes=4000000),
        )(*parts)

    return jax.shard_map(
        per_device,
        mesh=mesh,
        in_specs=(P(None, "gx", "gy"), P(None, "gx", "gy")),
        out_specs=(P(None, "gx", "gy"), P(None, "gx", "gy")),
        check_vma=False,
    )
```

```python
import jax
import jax.numpy as jnp
from jax import lax
from jax.experimental import pallas as pl
from jax.experimental.pallas import tpu as pltpu
from jax.sharding import PartitionSpec as P

low_bound = 0.4
high_bound = 12.0
cheb_theta = 0.5 * (high_bound + low_bound)
cheb_delta = 0.5 * (high_bound - low_bound)
cheb_sigma = cheb_theta / cheb_delta
rho_first = 1.0 / cheb_sigma
rho_second = 1.0 / (2.0 * cheb_sigma - rho_first)
rho_third = 1.0 / (2.0 * cheb_sigma - rho_second)

step_0 = rho_second * rho_first / cheb_theta + 2.0 * rho_second / cheb_delta
step_1 = 2.0 * rho_second / cheb_delta / cheb_theta
mix_0 = 1.0 + rho_third * rho_second
mix_1 = 2.0 * rho_third / cheb_delta
power_0 = 1.0 / cheb_theta + mix_0 * step_0 + mix_1
power_1 = -mix_0 * step_1 - mix_1 / cheb_theta - mix_1 * step_0
power_2 = mix_1 * step_1
shift_1 = power_1 / power_2
shift_0 = power_0 / power_2

HALO = 6
AHEAD = 2
PLANE = 2
LANES = 128
STRIP = 8
GROUP = 8
ONE_STAGE = 64
MESH = pl.DeviceIdType.MESH
LOGICAL = pl.DeviceIdType.LOGICAL
WAYS = ((-1, 0), (1, 0), (0, -1), (0, 1), (-1, -1), (-1, 1), (1, -1), (1, 1))


def stages_of(num_x, num_y):
    if num_x * num_y <= ONE_STAGE:
        return ((num_x, num_y),)
    return ((num_x, 1), (1, num_y))


def kernel(
    num_x, num_y, r_hbm, c_hbm, p_out, w_out, m_out, n_out, r_out, sums_out,
    fresh, x_in, coef, scoef, field, sfield, packed, side_in, corner_in, slots,
    in_sem, halo_send, halo_recv, red_send, red_recv, relayed,
):
    _, levels, rows, cols = fresh.shape
    tiles = rows // GROUP
    groups = tiles + 2
    width = LANES // groups
    last = cols - LANES
    me_x = lax.axis_index("gx")
    me_y = lax.axis_index("gy")
    stages = stages_of(num_x, num_y)

    def exists(dx, dy):
        ok = jnp.bool_(True)
        if dx < 0:
            ok = me_x > 0
        if dx > 0:
            ok = me_x < num_x - 1
        if dy < 0:
            ok_y = me_y > 0
            ok = ok_y if dx == 0 else jnp.logical_and(ok, ok_y)
        if dy > 0:
            ok_y = me_y < num_y - 1
            ok = ok_y if dx == 0 else jnp.logical_and(ok, ok_y)
        return ok

    loads = [
        pltpu.make_async_copy(ref, fresh.at[a], in_sem.at[a])
        for a, ref in enumerate((c_hbm, r_hbm))
    ]
    for load in loads:
        load.start()

    def place_in(stage):
        count_x, count_y = stage
        if count_x > 1 and count_y > 1:
            return me_x * num_y + me_y, lambda o: o
        if count_x > 1:
            return me_x, lambda o: o * num_y + me_y
        return me_y, lambda o: me_x * num_y + o

    def each_other(stage, act):
        mine, device = place_in(stage)
        total = stage[0] * stage[1]

        flip = mine < total // 2
        start_at = jnp.where(flip, total - 1 - mine, mine)

        def step(k, state):
            other = jnp.where(k > start_at, k, k - 1)
            act(device(jnp.where(flip, total - 1 - other, other)))
            return state

        lax.fori_loop(1, total, step, 0)

    barrier = pltpu.get_barrier_semaphore()

    def greet(device):
        pl.semaphore_signal(barrier, inc=1, device_id=device, device_id_type=LOGICAL)

    planes = len(stages) == 1 and num_x % PLANE == 0
    plane = me_x // PLANE * PLANE
    expected = jnp.int32(0)
    if planes:
        mine = me_x * num_y + me_y
        begin = me_x == plane

        for dy in (0, -1, 1):
            down = jnp.logical_and(begin, exists(-1, dy))
            up = jnp.logical_and(me_x == plane + PLANE - 1, exists(1, dy))

            @pl.when(down)
            def _():
                greet(mine - num_y + dy)

            expected = expected + up.astype(jnp.int32)

        def onward(other, state):
            @pl.when(other != mine)
            def _():
                greet(other)

            return state

        lax.fori_loop(plane * num_y, num_x * num_y, onward, 0)
        expected = expected + ((plane + PLANE) * num_y - 1)
    else:
        for stage in stages:
            each_other(stage, greet)
            expected = expected + (stage[0] * stage[1] - 1)
    if len(stages) > 1:
        for dx, dy in WAYS[4:]:
            ok = exists(dx, dy)

            @pl.when(ok)
            def _():
                greet((me_x + dx) * num_y + me_y + dy)

            expected = expected + ok.astype(jnp.int32)

    def relay():
        def tell(k, state):
            pl.semaphore_signal(
                relayed, inc=1, device_id=(me_x - k * PLANE) * num_y + me_y, device_id_type=LOGICAL
            )
            return state

        lax.fori_loop(1, me_x // PLANE + 1, tell, 0)

    def relay_wait():
        @pl.when(me_x < num_x - PLANE)
        def _():
            pl.semaphore_wait(relayed, (num_x - 1 - me_x) // PLANE)

    def halo_copies(way):
        dx, dy = WAYS[way]
        if dy == 0:
            side = 1 if dx < 0 else 0
            low = 0 if dx < 0 else rows - HALO
            land = 0 if dx < 0 else GROUP - HALO
            pairs = [
                (fresh.at[a, :, pl.ds(low, HALO)], x_in.at[a, side, :, pl.ds(land, HALO)])
                for a in range(2)
            ]
        elif dx == 0:
            pairs = [(packed.at[0 if dy < 0 else 1], side_in.at[0 if dy < 0 else 1])]
        else:
            pairs = [(
                packed.at[0 if dy < 0 else 1, 0 if dx < 0 else tiles - 1],
                corner_in.at[way - 4],
            )]
        return [
            pltpu.make_async_remote_copy(
                src_ref=one, dst_ref=two,
                send_sem=halo_send.at[way, a], recv_sem=halo_recv.at[way, a],
                device_id=(me_x + dx, me_y + dy), device_id_type=MESH,
            )
            for a, (one, two) in enumerate(pairs)
        ]

    def start(way, number=0):
        @pl.when(exists(*WAYS[way]))
        def _():
            halo_copies(way)[number].start()


    lane = lax.broadcasted_iota(jnp.int32, (levels, LANES), 1)

    def between(low, high, like):
        at = lax.broadcasted_iota(jnp.int32, (1,) * (len(like) - 1) + (LANES,), len(like) - 1)
        return (at >= low) & (at < high)

    def rolled(v, by):
        if isinstance(by, int):
            by = by % v.shape[-1]
            if by == 0:
                return v
        return pltpu.roll(v, by, v.ndim - 1)

    for load in loads:
        load.wait()

    def arrange(t):
        low = t * GROUP
        acc = [jnp.zeros((levels, LANES), jnp.float32)] * 2
        for a in range(2):
            block = jnp.transpose(fresh[a, :, low : low + GROUP, :], (1, 0, 2))
            field[a, HALO + low : HALO + low + GROUP] = block
            for side in range(2):
                offset = 0 if side == 0 else LANES - STRIP
                part = block[:, :, (0 if side == 0 else last) : (LANES if side == 0 else cols)]
                for g in range(GROUP):
                    place = (a * GROUP + g) * STRIP
                    moved = rolled(part[g], place - offset)
                    acc[side] = jnp.where(
                        (lane >= place) & (lane < place + STRIP), moved, acc[side]
                    )
        for side in range(2):
            packed[side, t] = acc[side]

    for t in sorted({0, tiles - 1}):
        arrange(t)
    pl.semaphore_wait(barrier, expected)
    for way in (4, 5, 6, 7):
        start(way)
    for number in range(2):
        for way in (0, 1):
            start(way, number)
    for t in range(1, tiles - 1):
        arrange(t)
    for way in (2, 3):
        start(way)
    if planes:
        relay()

    for way in range(8):
        dx, dy = WAYS[way]

        @pl.when(jnp.logical_not(exists(-dx, -dy)))
        def _():
            if dy == 0:
                x_in[:, 1 if dx < 0 else 0] = jnp.zeros((2, levels, GROUP, cols), jnp.float32)
            elif dx == 0:
                side_in[0 if dy < 0 else 1] = jnp.zeros((tiles, levels, LANES), jnp.float32)
            else:
                corner_in[way - 4] = jnp.zeros((levels, LANES), jnp.float32)

    def own_strips(a, state):
        for side in range(2):
            acc = jnp.zeros((GROUP, levels, LANES), jnp.float32)
            for g in range(1, tiles + 1):
                low = width * g + HALO * (1 - side)
                block = field[
                    a, HALO + (g - 1) * GROUP : HALO + g * GROUP, :,
                    (0 if side == 0 else last) : (LANES if side == 0 else cols),
                ]
                moved = rolled(block, low + 2 * HALO * side)
                acc = jnp.where(between(low, low + 2 * HALO, block.shape), moved, acc)
            sfield[a, side, 1 : 1 + GROUP] = acc
        return state

    lax.fori_loop(0, 2, own_strips, 0)

    def wrap(f, side):
        sfield[f, side, 0] = rolled(sfield[f, side, GROUP], width)
        sfield[f, side, GROUP + 1] = rolled(sfield[f, side, 1], -width)

    def level_of(shape):
        return lax.broadcasted_iota(jnp.int32, (1, levels, shape[-1]), 1)

    def faces(c, other):
        return jnp.where(jnp.minimum(c, other) > 0.0, 0.5 * (c + other), 0.0)

    def coefficients(low, n, beside):
        c = field[0, pl.ds(low, n)]
        level = level_of(c.shape)
        at = lax.broadcasted_iota(jnp.int32, (1, 1, cols), 2)
        half = 0.5 * c
        inner = jnp.logical_and(level > 0, level < levels - 1)
        kb = jnp.where(inner, 0.0, half)
        if beside:
            for other in (field[0, pl.ds(low - 1, n)], field[0, pl.ds(low + 1, n)]):
                kb = kb + jnp.where(other > 0.0, 0.0, half)
        ke = jnp.where(at < cols - 1, half + rolled(half, cols - 1), 0.0)
        kw = jnp.where(at > 0, half + rolled(half, 1), 0.0)
        kb = kb + (ke + kw)
        coef[1, pl.ds(low, n)] = ke
        coef[5, pl.ds(low, n)] = kw
        coef[2, pl.ds(low, n)] = jnp.where(
            level < levels - 1, half + pltpu.roll(half, levels - 1, 1), 0.0
        )
        coef[3, pl.ds(low, n)] = kb
        coef[4, pl.ds(low, n)] = kb + shift_1

    def strip_coefficients(side):
        c = sfield[0, side, 1 : 1 + GROUP]
        level = level_of(c.shape)
        half = 0.5 * c
        inner = jnp.logical_and(level > 0, level < levels - 1)
        east, west = rolled(c, LANES - 1), rolled(c, 1)
        kb = jnp.where(inner, 0.0, half)
        for other in (east, west, sfield[0, side, 0:GROUP], sfield[0, side, 2 : 2 + GROUP]):
            kb = kb + jnp.where(other > 0.0, 0.0, half)
        scoef[0, side, 0 : GROUP + 1] = faces(
            sfield[0, side, 0 : GROUP + 1], sfield[0, side, 1 : GROUP + 2]
        )
        ke, kw = faces(c, east), faces(c, west)
        kb = kb + (ke + kw)
        scoef[1, side, 1 : 1 + GROUP] = ke
        scoef[5, side, 1 : 1 + GROUP] = kw
        scoef[2, side, 1 : 1 + GROUP] = jnp.where(
            level < levels - 1, half + pltpu.roll(half, levels - 1, 1), 0.0
        )
        scoef[3, side, 1 : 1 + GROUP] = kb
        scoef[4, side, 1 : 1 + GROUP] = kb + shift_1

    def turned(read, low, n, j):
        v = read(j + 1, low, n)
        down, up = read(j + 1, low - 1, n), read(j + 1, low + 1, n)
        parts = [v[..., at : at + LANES] for at in range(0, v.shape[-1], LANES)]
        ons = [rolled(part, LANES - 1) for part in parts]
        backs = [rolled(part, 1) for part in parts]
        count = len(parts)
        east = [
            jnp.where(between(LANES - 1, LANES, v.shape), ons[i + 1], ons[i]) if i + 1 < count else ons[i]
            for i in range(count)
        ]
        west = [
            jnp.where(between(0, 1, v.shape), backs[i - 1], backs[i]) if i else backs[i]
            for i in range(count)
        ]
        east, west = (
            jnp.concatenate(x, axis=-1) if count > 1 else x[0] for x in (east, west)
        )
        return v, east, west, down, up

    def image(read, k, low, n, j, around):
        third = j % 3 if isinstance(j, int) else lax.rem(j, 3)
        shifted = 4 - (third + 1) // 2
        v, east, west, down, up = around
        axis = v.ndim - 1
        rows_of = jnp.concatenate([down[:1], v, up[n - 1 :]], axis=0)
        across = k(0, low - 1, n + 1) * (rows_of[: n + 1] - rows_of[1:])
        fz = k(2, low, n) * (v - pltpu.roll(v, levels - 1, axis - 1))
        rest = (across[1:] - across[:n]) + ((fz - pltpu.roll(fz, 1, axis - 1)) + k(shifted, low, n) * v)
        if not isinstance(j, int):
            also = jnp.where(third == 1, shift_0, 0.0)
            rest = rest + also * read(jnp.maximum(j, 1), low, n)
        elif third == 1:
            rest = rest + shift_0 * read(j, low, n)
        return rest - (k(1, low, n) * east + k(5, low, n) * west)

    def images(jobs, j):
        ahead = AHEAD
        around = [turned(read, low, n, j) for read, k, low, n, put in jobs[:ahead]]
        for i, (read, k, low, n, put) in enumerate(jobs):
            if i + ahead < len(jobs):
                other = jobs[i + ahead]
                around.append(turned(other[0], other[2], other[3], j))
            put(j + 2, low, n, image(read, k, low, n, j, around[i]))

    def main(f, low, n):
        return field[f, pl.ds(low, n)]

    def main_k(i, low, n):
        return coef[i, pl.ds(low, n)]

    def main_put(f, low, n, v):
        field[f, pl.ds(low, n)] = v

    def summed(read, low, n, state):
        r, p, w, m, q = (read(f, low, n) for f in (1, 3, 4, 6, 7))
        return tuple(
            s + jnp.sum(t, axis=0) for s, t in zip(state, (r * p, w * p, w * m, q * m))
        )

    STEP = 4

    WIDE = 2 * GROUP

    def own_coefficients(i, state):
        low = HALO + i * WIDE
        coefficients(low, WIDE, False)
        coef[0, pl.ds(low, WIDE)] = 0.5 * (
            field[0, pl.ds(low, WIDE)] + field[0, pl.ds(low + 1, WIDE)]
        )
        return state

    lax.fori_loop(0, rows // WIDE, own_coefficients, 0)

    def own_image(j, state):
        images([(main, main_k, HALO + low, STEP, main_put) for low in range(0, rows, STEP)], j)
        return state

    lax.fori_loop(0, 6, own_image, 0)
    zero = jnp.zeros((levels, cols), jnp.float32)
    acc = lax.fori_loop(
        0, (rows - 2 * HALO) // STEP,
        lambda i, state: summed(main, 2 * HALO + i * STEP, STEP, state), (zero,) * 4,
    )


    def arrived(ways, number):
        for way in ways:
            dx, dy = WAYS[way]

            @pl.when(exists(-dx, -dy))
            def _():
                halo_copies(way)[number].wait_recv()

    def strips_halo(corners):
        arrived((4, 5, 6, 7) if corners else (2, 3), 0)
        for a in range(2):
            for side in range(2):
                for i in range(GROUP):
                    out = sfield[a, side, 1 + i]
                    for g in (0, groups - 1) if corners else range(1, groups - 1):
                        if g == 0:
                            if i < GROUP - HALO:
                                continue
                            tile = corner_in[3 - side]
                        elif g == groups - 1:
                            if i >= HALO:
                                continue
                            tile = corner_in[1 - side]
                        else:
                            tile = side_in[1 - side, g - 1]
                        low = width * g + 2 * HALO * side
                        by = low - i * STRIP - (STRIP - HALO) * (1 - side)
                        moved = rolled(tile, by - a * (GROUP * STRIP))
                        out = jnp.where((lane >= low) & (lane < low + HALO), moved, out)
                    sfield[a, side, 1 + i] = out

    def edges(i):
        low = 1 + i * (HALO + rows - 2)
        coefficients(low, HALO, True)
        first = low - 1 + i
        coef[0, pl.ds(first, HALO)] = faces(
            field[0, pl.ds(first, HALO)], field[0, pl.ds(first + 1, HALO)]
        )

    for a in range(2):
        arrived((0, 1), a)
        lower = jnp.transpose(x_in[a, 0], (1, 0, 2))[GROUP - HALO : GROUP]
        upper = jnp.transpose(x_in[a, 1], (1, 0, 2))[0:HALO]
        field[a, 0:HALO] = lower
        field[a, HALO + rows : HALO + rows + HALO] = upper
        for side in range(2):
            edge = (0, LANES) if side == 0 else (last, cols)
            for g, block, slot in ((0, lower, GROUP - HALO), (groups - 1, upper, 0)):
                low = width * g + HALO * (1 - side)
                moved = rolled(block[:, :, edge[0] : edge[1]], low + 2 * HALO * side)
                slots_of = pl.ds(1 + slot, HALO)
                sfield[a, side, slots_of] = jnp.where(
                    between(low, low + 2 * HALO, moved.shape), moved, sfield[a, side, slots_of]
                )
        if a == 0:
            for i in range(2):
                edges(i)
    strips_halo(False)
    strips_halo(True)
    for side in range(2):
        wrap(0, side)
        strip_coefficients(side)
        wrap(1, side)

    PART = 6
    HALF = GROUP // 2

    def strip_job(side, low):
        def read(f, at, n):
            if at == 0:
                first = rolled(sfield[f, side, pl.ds(GROUP, 1)], width)
                return jnp.concatenate([first, sfield[f, side, pl.ds(1, n - 1)]], axis=0)
            if at + n == GROUP + 2:
                last_row = rolled(sfield[f, side, pl.ds(1, 1)], -width)
                return jnp.concatenate([sfield[f, side, pl.ds(at, n - 1)], last_row], axis=0)
            return sfield[f, side, pl.ds(at, n)]

        def k(i, at, n):
            return scoef[i, side, pl.ds(at, n)]

        def put(f, at, n, v):
            sfield[f, side, pl.ds(at, n)] = v

        return read, k, low, HALF, put

    def edge_image(j):
        jobs = []
        for base in (j + 1, rows - 1 - j + HALO):
            jobs += [(main, main_k, low, PART, main_put) for low in (base,)]
        strips = [strip_job(side, low) for side in range(2) for low in (1, 1 + HALF)]
        images(jobs + strips, j)

    for j in range(6):
        edge_image(j)
    for base in (HALO, rows):
        for low in (base,):
            acc = summed(main, low, PART, acc)
    sacc = (jnp.zeros((levels, LANES), jnp.float32),) * 4
    for side in range(2):
        sacc = summed(lambda f, low, n: sfield[f, side, pl.ds(low, n)], 1, GROUP, sacc)

    in_strip = jnp.zeros((levels, LANES), jnp.bool_)
    for g in range(1, tiles + 1):
        low = width * g + HALO
        in_strip = jnp.logical_or(in_strip, (lane >= low) & (lane < low + HALO))
    message = jnp.zeros((levels, LANES), jnp.float32)
    share = LANES // 4
    for i in range(4):
        s = jnp.where(in_strip, sacc[i], 0.0)
        for low in range(0, cols, LANES):
            part = acc[i][:, low : low + LANES]
            if low == 0:
                part = jnp.where(lane >= HALO, part, 0.0)
            if low == last:
                part = jnp.where(lane < LANES - HALO, part, 0.0)
            s = s + part
        s = (s + rolled(s, share)) + (rolled(s, 2 * share) + rolled(s, 3 * share))
        message = jnp.where((lane >= i * share) & (lane < (i + 1) * share), s, message)
    total = jnp.sum(message, axis=0, keepdims=True)

    def finish(t, state):
        low = pl.multiple_of(t * GROUP, GROUP)
        for f, out in ((3, p_out), (4, w_out), (6, m_out), (7, n_out)):
            block = field[f, pl.ds(HALO + low, GROUP)]
            parts = [block[:, :, k : k + LANES] for k in range(0, cols, LANES)]
            for side in range(2):
                strip = sfield[f, side, 1 : 1 + GROUP]
                to = 0 if side == 0 else LANES - HALO
                part = 0 if side == 0 else len(parts) - 1
                by = lax.rem(to - HALO - width + 2 * LANES - width * t, LANES)
                parts[part] = jnp.where(
                    between(to, to + HALO, strip.shape), rolled(strip, by), parts[part]
                )
            for k, part in enumerate(parts):
                out[:, pl.ds(low, GROUP), k * LANES : (k + 1) * LANES] = jnp.transpose(
                    part, (1, 0, 2)
                )
        return state

    if planes:
        relay_wait()
    base = 0
    sent = []
    for index, stage in enumerate(stages):
        count = stage[0] * stage[1]
        mine = base + place_in(stage)[0]
        slots[pl.ds(mine, 1), :] = total

        def send(device):
            pltpu.make_async_remote_copy(
                src_ref=slots.at[pl.ds(mine, 1)], dst_ref=slots.at[pl.ds(mine, 1)],
                send_sem=red_send.at[index], recv_sem=red_recv.at[index],
                device_id=device, device_id_type=LOGICAL,
            ).start()

        each_other(stage, send)
        if index == 0:
            lax.fori_loop(0, tiles, finish, 0)
            r_out[...] = fresh[1]
            for way in range(8):

                @pl.when(exists(*WAYS[way]))
                def _():
                    for copy in halo_copies(way):
                        copy.wait_send()

        if count > 1:
            whole = slots.at[pl.ds(base, count - 1)]
            pltpu.make_async_copy(whole, whole, red_recv.at[index]).wait()
            sent.append((whole, red_send.at[index]))
        total = jnp.sum(slots[base : base + count], axis=0, keepdims=True)
        base += -(-count // 8) * 8
    sums_out[...] = total
    for whole, sem in sent:
        pltpu.make_async_copy(whole, whole, sem).wait()


def combine(p, w, m, n, r, sums, x_hbm, res_hbm, x_vmem, res_vmem, sem):
    levels = p.shape[0]
    total = sums[...]
    lane = lax.broadcasted_iota(jnp.int32, total.shape, 1)
    share = LANES // 4

    def of(i, scale):
        chosen = (lane >= i * share) & (lane < (i + 1) * share)
        return scale * jnp.sum(jnp.where(chosen, total, 0.0), axis=1, keepdims=True)

    rp, wp, wm, nm = (of(i, power_2 ** (i + 1)) for i in range(4))
    gamma_old = rp
    alpha_old = gamma_old / wp
    gamma = (rp - alpha_old * wp) - alpha_old * (wp - alpha_old * wm)
    delta = (wp - alpha_old * wm) - alpha_old * (wm - alpha_old * nm)
    beta = gamma / gamma_old
    alpha = gamma / (delta - beta * gamma / alpha_old)
    near = power_2 * (alpha_old + alpha * (1.0 + beta))
    far = (power_2 * power_2) * (alpha * alpha_old)
    copies = []
    for z in range(levels):
        x_vmem[z] = near * p[z] - far * m[z]
        res_vmem[z] = (r[z] - near * w[z]) + far * n[z]
        for a, (one, two) in enumerate(((x_vmem, x_hbm), (res_vmem, res_hbm))):
            copies.append(pltpu.make_async_copy(one.at[z], two.at[z], sem.at[a]))
            copies[-1].start()
    for a, (one, two) in enumerate(((x_vmem, x_hbm), (res_vmem, res_hbm))):
        pltpu.make_async_copy(one, two, sem.at[a]).wait()


def solution(mesh):
    num_x, num_y = mesh.shape["gx"], mesh.shape["gy"]

    def per_device(right_side, conductivity):
        levels, rows, cols = right_side.shape
        high = rows + 2 * HALO
        tiles = rows // GROUP
        stages = stages_of(num_x, num_y)
        deep = sum(-(-(a * b) // 8) * 8 for a, b in stages)

        def body(*refs):
            kernel(num_x, num_y, *refs)

        block = (levels, rows, cols)
        full = (high, levels, cols)
        slim = (2, GROUP + 2, levels, LANES)
        out = jax.ShapeDtypeStruct(block, jnp.float32)
        sums = jax.ShapeDtypeStruct((1, LANES), jnp.float32)
        vmem = lambda shape: pltpu.VMEM(shape, jnp.float32)
        dma = lambda *n: pltpu.SemaphoreType.DMA(n)
        in_vmem = pl.BlockSpec(memory_space=pltpu.VMEM)
        in_hbm = pl.BlockSpec(memory_space=pltpu.HBM)
        parts = pl.pallas_call(
            body,
            out_shape=(out,) * 5 + (sums,),
            in_specs=[in_hbm] * 2,
            out_specs=(in_vmem,) * 6,
            scratch_shapes=[
                vmem((2,) + block), vmem((2, 2, levels, GROUP, cols)),
                vmem((6,) + full), vmem((6,) + slim), vmem((8,) + full), vmem((8,) + slim),
                vmem((2, tiles, levels, LANES)), vmem((2, tiles, levels, LANES)),
                vmem((4, levels, LANES)), vmem((deep, LANES)),
                dma(2), dma(8, 2), dma(8, 2), dma(len(stages)), dma(len(stages)),
                pltpu.SemaphoreType.REGULAR,
            ],
            compiler_params=pltpu.CompilerParams(
                collective_id=0, has_side_effects=True, vmem_limit_bytes=55000000
            ),
        )(right_side, conductivity)
        return pl.pallas_call(
            combine,
            out_shape=(out, out),
            in_specs=[in_vmem] * 6,
            out_specs=(in_hbm,) * 2,
            scratch_shapes=[vmem(block), vmem(block), dma(2)],
            compiler_params=pltpu.CompilerParams(vmem_limit_bytes=4000000),
        )(*parts)

    return jax.shard_map(
        per_device,
        mesh=mesh,
        in_specs=(P(None, "gx", "gy"), P(None, "gx", "gy")),
        out_specs=(P(None, "gx", "gy"), P(None, "gx", "gy")),
        check_vma=False,
    )
```
